512 devices in a mesh: rows: 64 (over z, y), cols: 8 (over x, core).
Axes of the slice: x: 4, y: 4, z: 16, core: 2. Of those that a mesh axis runs over, the one named last changes fastest.
Arguments:
- sens_base: bfloat16 [524288, 1024], P('rows', 'cols'), may hold values from -0.14157282 to 0.14157282
- design_field: float32 [512, 1024], P('rows'), may hold values from -3 to 3
- gradient: bfloat16 [512, 1024], P('rows'), may hold values from -6 to 6
- tile_index: int32 [1024], P('cols'), may hold values from 0 to 31
- type_codes: int32 [1024], P('cols'), may hold values from 0 to 2
Outputs:
- r_panels: float32 [512, 1024], P(None, 'cols')
- multipliers: float32 [512], replicated
The draws below stay inside these ranges and needn't reach their ends.
Inputs may be any that keep to these rules, and one draw needn't show every extreme that they name: `tile_index`: each constraint names one support tile.
All inputs are finite; a program needn't handle non-finite values.
Results may differ from the reference program's by a relative error of at most 0.0003.
The reference program's roundings to bfloat16 on the way (of `jacobian_t`) count: a program that leaves them out, or rounds other values in their place, can miss the bound.
Values may be sent and summed in bfloat16 or wider, within the bound.
A program may use at most 64 MiB of HBM per device.

```python
import math
import jax
import jax.numpy as jnp
from jax import lax

GX = 1024
TILE = 128
NC = 1024
KF = 512
GY = 512
NV = 524288
NT = 32
N_ROWS = 64
N_COLS = 8


def draw_sens_base(key, part):
    keys = jax.random.split(jax.random.fold_in(key, 7), 6)
    devices_all = N_ROWS * N_COLS
    block_cells = NV // devices_all
    noise = jnp.clip(jax.random.normal(keys[0], (NV, NC), jnp.float32), -4.0, 4.0)
    owner = jax.random.randint(keys[1], (NC,), 0, devices_all)
    cell_ids = jnp.arange(NV, dtype=jnp.int32)
    block_of = cell_ids // block_cells
    boost = jnp.where(block_of[:, None] == owner[None, :], float(devices_all) ** 0.5, 1.0)
    reach = (NC / 8.0) ** 0.5
    freq_rows = jax.random.uniform(keys[2], (NC,), jnp.float32, 0.0, reach)
    freq_cols = jax.random.uniform(keys[3], (NC,), jnp.float32, -reach, reach)
    shift = jax.random.uniform(keys[4], (NC,), jnp.float32, -math.pi, math.pi)
    low_scale = 0.25
    high_scale = 4.0
    cell_scale = jnp.exp(jax.random.uniform(keys[5], (NV,), jnp.float32, math.log(low_scale), math.log(high_scale)))
    mean_square = (high_scale ** 2 - low_scale ** 2) / (2.0 * math.log(high_scale / low_scale))
    amp_norm = (2.0 / (NV * mean_square)) ** 0.5
    rows_at = (cell_ids // GX).astype(jnp.float32)
    cols_at = (cell_ids % GX).astype(jnp.float32)
    column_amp = jnp.ones((NC,), jnp.float32)
    phase = 2.0 * math.pi * (rows_at[:, None] * (freq_rows[None, :] / GY) + cols_at[:, None] * (freq_cols[None, :] / GX)) + shift[None, :]
    wave = (amp_norm * cell_scale)[:, None] * column_amp[None, :] * jnp.cos(phase)
    return (noise * boost / NV ** 0.5 + wave).astype(jnp.bfloat16)


def set_ends(result, key, smallest, largest):
    spot = [jax.random.randint(jax.random.fold_in(key, axis), (), 0, length) for axis, length in enumerate(result.shape)]
    widest = result.shape.index(max(result.shape))
    beside = spot[:widest] + [(spot[widest] + 1) % result.shape[widest]] + spot[widest + 1:]
    return result.at[tuple(spot)].set(smallest).at[tuple(beside)].set(largest)


def level_of(stream_key, extent, cuts, least, high):
    loudness, own = 1.0, jax.random.fold_in(stream_key, 6)
    for position, blocks in cuts:
        heights = jnp.exp(jax.random.uniform(jax.random.fold_in(own, position), (blocks,), jnp.float32, least / len(cuts), high / len(cuts)))
        loudness = loudness * jnp.repeat(heights, extent[position] // blocks).reshape([-1 if axis == position else 1 for axis in range(len(extent))])
    return loudness


def scatter_about(own_key, shape, width, bound, cuts=(), kind=jnp.bfloat16):
    drawn = width * jax.random.normal(own_key, shape, jnp.float32)
    if cuts:
        drawn = drawn * level_of(own_key, shape, cuts, -0.22, 0.18)
    return jnp.clip(drawn, -bound, bound).astype(kind)


def setup_inputs(seed: int = 0) -> dict:
    arg_keys = jax.random.split(jax.random.key(seed), 6)
    return {
        "sens_base": draw_sens_base(jax.random.fold_in(arg_keys[5], 71), 0),
        "design_field": scatter_about(arg_keys[1], (GY, GX), 0.5, 3.0, ((0, 64),), jnp.float32),
        "gradient": scatter_about(arg_keys[2], (GY, GX), 1.0, 6.0, ((0, 64),)),
        "tile_index": set_ends(jax.random.randint(arg_keys[3], (NC,), 0, NT), jax.random.fold_in(arg_keys[3], 1), 0, NT - 1).astype(jnp.int32),
        "type_codes": set_ends(jax.random.randint(arg_keys[4], (NC,), 0, 3), jax.random.fold_in(arg_keys[4], 1), 0, 2).astype(jnp.int32),
    }


def stencil_fields(design_field):
    padded = jnp.pad(design_field, 1)
    north_cells = padded[:-2, 1:-1]
    south_cells = padded[2:, 1:-1]
    west_cells = padded[1:-1, :-2]
    east_cells = padded[1:-1, 2:]
    laplace = 4.0 * design_field - (north_cells + south_cells + west_cells + east_cells)
    slope_x = 0.5 * (east_cells - west_cells)
    slope_y = 0.5 * (south_cells - north_cells)
    return jnp.stack([laplace, slope_x, slope_y]).reshape(3, -1)

def assemble(base_cols, tile_cols, type_cols, stencils, cell_tile):
    kinds_all = jnp.arange(3, dtype=jnp.int32)
    chooser = (type_cols[None, :] == kinds_all[:, None]).astype(jnp.float32)
    picked = lax.dot_general(stencils.astype(jnp.float32), chooser.astype(jnp.float32), (((0,), (0,)), ((), ())), precision=lax.Precision.HIGHEST, preferred_element_type=jnp.float32)
    inside = cell_tile[:, None] == tile_cols[None, :]
    total = base_cols.astype(jnp.float32) + jnp.where(inside, picked / TILE, 0.0)
    return total.astype(jnp.bfloat16)

def reference(sens_base, design_field, gradient, tile_index, type_codes):
    stencils = stencil_fields(design_field)
    row_ids = jnp.arange(GY, dtype=jnp.int32) // TILE
    col_ids = jnp.arange(GX, dtype=jnp.int32) // TILE
    cell_tile = (row_ids[:, None] * (GX // TILE) + col_ids[None, :]).reshape(-1).astype(jnp.int32)
    col_block = min(128, NC)
    pieces = []
    for index_block in range(NC // col_block):
        start = index_block * col_block
        pieces.append(assemble(sens_base[:, start:start + col_block], tile_index[start:start + col_block], type_codes[start:start + col_block], stencils, cell_tile))
    jacobian_t = jnp.concatenate(pieces, axis=1)
    leading = jacobian_t[:, :KF]
    gram_block = lax.dot_general(leading.astype(jnp.float32), jacobian_t.astype(jnp.float32), (((0,), (0,)), ((), ())), preferred_element_type=jnp.float32)
    projected = jnp.dot(gradient.reshape(-1).astype(jnp.float32), leading.astype(jnp.float32), preferred_element_type=jnp.float32)
    lower_chol = jnp.linalg.cholesky(gram_block[:, :KF])
    r_panels = jax.scipy.linalg.solve_triangular(lower_chol, gram_block, lower=True)
    half_solved = jax.scipy.linalg.solve_triangular(lower_chol, projected, lower=True)
    multipliers = jax.scipy.linalg.solve_triangular(lower_chol.T, half_solved, lower=False)
    return (r_panels, multipliers)
```

```python
import functools

import jax
import jax.numpy as jnp
from jax import lax
from jax.experimental import pallas as pl
from jax.experimental.pallas import tpu as pltpu
from jax.sharding import PartitionSpec as P

TILE = 128
BLK = 128
NX = 4
NY = 4
MESH = pl.DeviceIdType.MESH
HIGHEST = lax.Precision.HIGHEST
HEAD = [(a, b) for a in range(4) for b in range(a, 4)]
COUNT = (3, 3, 4, 4)
FIRST = (0, 3, 6, 10)
HALF = 14


def slot_of(core, x, y):
    if x < 2:
        spot = (core * 2 + x) * 3 + y
        if spot < len(HEAD):
            return HEAD[spot]
        return "proj" if spot == len(HEAD) else None
    return (y, x * 2 + core)


def gram_kernel(
    n_rows,
    base_ref, field_ref, grad_ref, tile_ref, type_ref,
    head_ref, own_ref,
    raw, jac, codes_mine, codes, north, south, parts,
    from_core, half, from_x, quarter, from_y, block, from_z, piece,
    line, panel, head_half,
    a2a_send, a2a_recv, code_send, code_recv, halo_send, halo_recv,
    core_sems, x_send, x_recv, y_send, y_recv, z_send, z_recv,
    zg_send, zg_recv, yg_send, yg_recv, xg_send, xg_recv, cg_send, cg_recv,
):
    r = lax.axis_index("rows")
    c = lax.axis_index("cols")
    nz = n_rows // NY
    z, y = r // NY, r % NY
    x, core = c // 2, c % 2
    up, down = (r + n_rows - 1) % n_rows, (r + 1) % n_rows
    cells = raw.shape[1]

    def dev_c(col):
        return (r, col)

    def dev_y(yy):
        return (z * NY + yy, c)

    def dev_z(zz):
        return (zz * NY + y, c)

    def remote(src, dst, send, recv, device):
        return pltpu.make_async_remote_copy(
            src_ref=src, dst_ref=dst, send_sem=send, recv_sem=recv,
            device_id=device, device_id_type=MESH,
        )

    barrier = pltpu.get_barrier_semaphore()

    def greet(device):
        pl.semaphore_signal(barrier, inc=1, device_id=device, device_id_type=MESH)

    for d in range(1, 8):
        greet(dev_c((c + d) % 8))
    for d in range(1, NY):
        greet(dev_y((y + d) % NY))
    for d in range(1, nz):
        greet(dev_z((z + d) % nz))
    greet((up, c))
    greet((down, c))
    codes_mine[...] = jnp.zeros_like(codes_mine)
    codes_mine[0:1, :] = tile_ref[...]
    codes_mine[1:2, :] = type_ref[...]
    pl.semaphore_wait(barrier, 7 + (NY - 1) + (nz - 1) + 2)

    sent = []
    for d in range(1, 8):
        to = (c + d) % 8
        cp = remote(codes_mine, codes.at[c], code_send.at[d], code_recv.at[d], dev_c(to))
        cp.start()
        sent.append(cp)
    cp = remote(field_ref, north, halo_send.at[0], halo_recv.at[0], (down, c))
    cp.start()
    sent.append(cp)
    cp = remote(field_ref, south, halo_send.at[1], halo_recv.at[1], (up, c))
    cp.start()
    sent.append(cp)
    for d in (4, 3, 5, 2, 6, 1, 7):
        to = (c + d) % 8
        cp = remote(
            base_ref.at[pl.ds(to * cells, cells), :], raw.at[c],
            a2a_send.at[d], a2a_recv.at[d], dev_c(to),
        )
        cp.start()
        sent.append(cp)
    mine = pltpu.make_async_copy(
        base_ref.at[pl.ds(c * cells, cells), :], raw.at[c], a2a_recv.at[0]
    )
    mine.start()
    codes[c] = codes_mine[...]

    remote(field_ref, north, halo_send.at[0], halo_recv.at[0], (up, c)).wait_recv()
    remote(field_ref, south, halo_send.at[1], halo_recv.at[1], (down, c)).wait_recv()
    here = field_ref[pl.ds(c, 1), :]
    above = field_ref[pl.ds((c + 7) % 8, 1), :]
    below = field_ref[pl.ds((c + 1) % 8, 1), :]
    above = jnp.where(c == 0, jnp.where(r == 0, 0.0, north[7:8, :]), above)
    below = jnp.where(c == 7, jnp.where(r == n_rows - 1, 0.0, south[0:1, :]), below)
    wide = (8, cells)
    here = jnp.broadcast_to(here, wide)
    above = jnp.broadcast_to(above, wide)
    below = jnp.broadcast_to(below, wide)
    lane = lax.broadcasted_iota(jnp.int32, wide, 1)
    west = jnp.where(lane == 0, 0.0, pltpu.roll(here, 1, 1))
    east = jnp.where(lane == cells - 1, 0.0, pltpu.roll(here, cells - 1, 1))
    laplace = 4.0 * here - (above + below + west + east)
    slope_x = 0.5 * (east - west)
    slope_y = 0.5 * (below - above)
    srow = lax.broadcasted_iota(jnp.int32, wide, 0)
    terms = []
    for fieldval in (laplace, slope_x, slope_y):
        rest = fieldval / TILE
        for _ in range(3):
            term = rest.astype(jnp.bfloat16).astype(jnp.float32)
            terms.append(term)
            rest = rest - term
    low = jnp.zeros(wide, jnp.float32)
    for k in range(8):
        low = jnp.where(srow == k, terms[(k % 3) * 3 + k // 3], low)
    high = jnp.where(srow == 0, terms[2 * 3 + 2], 0.0)
    both = jnp.concatenate([low, high], axis=0)
    tiles = cells // TILE
    spread = jnp.concatenate([both] * tiles, axis=0)
    krow = lax.broadcasted_iota(jnp.int32, spread.shape, 0)
    kcol = lax.broadcasted_iota(jnp.int32, spread.shape, 1)
    spread = jnp.where(krow // 16 == kcol // TILE, spread, 0.0)
    spread_t = spread.T.astype(jnp.bfloat16)

    first_tile = (r * 8 // TILE) * tiles
    rows16 = lax.broadcasted_iota(jnp.int32, (16 * tiles, BLK), 0)
    term_id = rows16 % 16
    kind_of = jnp.where(term_id < 9, term_id % 3, 3)
    tile_of = first_tile + rows16 // 16
    for d in range(1, 8):
        src = (c + 8 - d) % 8
        remote(codes_mine, codes.at[src], code_send.at[d], code_recv.at[d], dev_c(src)).wait_recv()

    for cs in range(8):
        @pl.when(c == cs)
        def _():
            mine.wait()

        @pl.when(c != cs)
        def _():
            d = (c + 8 - cs) % 8
            remote(
                base_ref.at[pl.ds(0, cells), :], raw.at[cs],
                a2a_send.at[d], a2a_recv.at[d], dev_c(cs),
            ).wait_recv()

        chosen = jnp.logical_and(
            kind_of == codes[cs, 1:2, :], tile_of == codes[cs, 0:1, :]
        ).astype(jnp.float32).astype(jnp.bfloat16)
        added = jnp.dot(spread_t, chosen, preferred_element_type=jnp.float32)
        jac[:, cs * BLK:(cs + 1) * BLK] = (raw[cs].astype(jnp.float32) + added).astype(jnp.bfloat16)

    where = {slot_of(k, xx, yy): k * HALF + FIRST[xx] + yy
             for k in range(2) for xx in range(NX) for yy in range(COUNT[xx])}
    contract = (((0,), (0,)), ((), ()))
    for pa in range(2):
        left = jac[:, pa * 256:(pa + 1) * 256]
        for pb in range(pa, 4):
            prod = lax.dot_general(
                left, jac[:, pb * 256:(pb + 1) * 256], contract,
                preferred_element_type=jnp.float32,
            )
            for i in range(2):
                for j in range(2):
                    key = (pa * 2 + i, pb * 2 + j)
                    if key in where:
                        parts[where[key]] = prod[i * BLK:(i + 1) * BLK, j * BLK:(j + 1) * BLK]
    proj = jnp.dot(grad_ref[...], jac[:, 0:512], preferred_element_type=jnp.float32)
    proj = jnp.sum(
        jnp.where(lax.broadcasted_iota(jnp.int32, proj.shape, 0) == c, proj, 0.0),
        axis=0, keepdims=True,
    )
    parts[where["proj"]] = jnp.zeros((BLK, BLK), jnp.float32)
    parts[where[None]] = jnp.zeros((BLK, BLK), jnp.float32)
    for k in range(4):
        parts[where["proj"], k:k + 1, :] = proj[:, k * BLK:(k + 1) * BLK]

    cp = remote(
        parts.at[pl.ds((1 - core) * HALF, HALF)], from_core,
        core_sems.at[0], core_sems.at[1], dev_c(x * 2 + 1 - core),
    )
    cp.start()
    sent.append(cp)
    cp.wait_recv()
    half[...] = parts[pl.ds(core * HALF, HALF)] + from_core[...]

    for xx in range(NX):
        span = COUNT[xx]

        @pl.when(x != xx)
        def _():
            d = (xx + NX - x) % NX
            remote(
                half.at[pl.ds(FIRST[xx], span)], from_x.at[d, pl.ds(0, span)],
                x_send.at[d], x_recv.at[d], dev_c(xx * 2 + core),
            ).start()

    for xx in range(NX):
        span = COUNT[xx]

        @pl.when(x == xx)
        def _():
            total = half[FIRST[xx]:FIRST[xx] + span]
            for d in (1, 3, 2):
                remote(
                    half.at[pl.ds(FIRST[xx], span)], from_x.at[d, pl.ds(0, span)],
                    x_send.at[d], x_recv.at[d], dev_c(((xx + NX - d) % NX) * 2 + core),
                ).wait_recv()
                total = total + from_x[d, 0:span]
            quarter[0:span] = total

    holds = jnp.logical_or(x >= 2, y < 3)

    def y_copy(d, yy, peer):
        return remote(
            quarter.at[yy], from_y.at[d], y_send.at[d], y_recv.at[d], dev_y(peer)
        )

    for d in range(1, NY):
        yy = (y + d) % NY

        @pl.when(jnp.logical_or(x >= 2, yy < 3))
        def _():
            y_copy(d, yy, yy).start()

    def z_copy(d, zz, peer):
        return remote(
            block.at[pl.ds(zz * 8, 8)], from_z.at[d], z_send.at[d], z_recv.at[d], dev_z(peer)
        )

    def zg_copy(d, spot, peer):
        return remote(
            piece, line.at[pl.ds(spot * 8, 8)], zg_send.at[d], zg_recv.at[d], dev_z(peer)
        )

    def yg_copy(d, spot, peer):
        return remote(
            line, panel.at[spot], yg_send.at[d], yg_recv.at[d], dev_y(peer)
        )

    @pl.when(holds)
    def _():
        total = quarter[y]
        for d in range(1, NY):
            y_copy(d, 0, (y + NY - d) % NY).wait_recv()
            total = total + from_y[d]
        block[...] = total
        for d in range(1, nz):
            zz = (z + d) % nz
            z_copy(d, zz, zz).start()
        total = block[pl.ds(pl.multiple_of(z * 8, 8), 8)]
        for d in range(1, nz):
            z_copy(d, 0, (z + nz - d) % nz).wait_recv()
            total = total + from_z[d]
        piece[...] = total
        for d in range(1, nz):
            zg_copy(d, z, (z + d) % nz).start()
        line[pl.ds(pl.multiple_of(z * 8, 8), 8)] = total
        for d in range(1, nz):
            src = (z + nz - d) % nz
            zg_copy(d, src, src).wait_recv()
        for d in range(1, NY):
            yg_copy(d, y, (y + d) % NY).start()
        panel[y] = line[...]

    for d in range(1, NY):
        src = (y + NY - d) % NY

        @pl.when(jnp.logical_or(x >= 2, src < 3))
        def _():
            yg_copy(d, src, src).wait_recv()

    def xg_copy(d, xx, peer):
        return remote(
            panel.at[pl.ds(0, 3)], head_half.at[xx], xg_send.at[d], xg_recv.at[d],
            dev_c(peer * 2 + core),
        )

    def cg_copy(xx):
        return remote(
            head_half.at[xx], head_ref.at[pl.ds((core * 2 + xx) * 3, 3)],
            cg_send.at[xx], cg_recv.at[xx], dev_c(x * 2 + 1 - core),
        )

    @pl.when(x < 2)
    def _():
        for d in range(1, NX):
            xg_copy(d, x, (x + d) % NX).start()
        head_half[x] = panel[0:3]

    for xx in range(2):
        @pl.when(x != xx)
        def _():
            d = (x + NX - xx) % NX
            xg_copy(d, xx, xx).wait_recv()

        cg_copy(xx).start()
        head_ref[pl.ds((core * 2 + xx) * 3, 3)] = head_half[xx]

    @pl.when(x >= 2)
    def _():
        own_ref[...] = panel[...]

    @pl.when(x < 2)
    def _():
        own_ref[...] = jnp.zeros_like(own_ref)

    for xx in range(2):
        remote(
            head_half.at[xx], head_ref.at[pl.ds(((1 - core) * 2 + xx) * 3, 3)],
            cg_send.at[xx], cg_recv.at[xx], dev_c(x * 2 + 1 - core),
        ).wait_recv()

    for cp in sent:
        cp.wait_send()
    for xx in range(NX):
        @pl.when(x != xx)
        def _():
            d = (xx + NX - x) % NX
            remote(
                half.at[pl.ds(FIRST[xx], COUNT[xx])], from_x.at[d, pl.ds(0, COUNT[xx])],
                x_send.at[d], x_recv.at[d], dev_c(xx * 2 + core),
            ).wait_send()
    for d in range(1, NY):
        yy = (y + d) % NY

        @pl.when(jnp.logical_or(x >= 2, yy < 3))
        def _():
            y_copy(d, yy, yy).wait_send()

    @pl.when(holds)
    def _():
        for d in range(1, nz):
            zz = (z + d) % nz
            z_copy(d, zz, zz).wait_send()
            zg_copy(d, z, zz).wait_send()
        for d in range(1, NY):
            yg_copy(d, y, (y + d) % NY).wait_send()

    @pl.when(x < 2)
    def _():
        for d in range(1, NX):
            xg_copy(d, x, (x + d) % NX).wait_send()
    for xx in range(2):
        cg_copy(xx).wait_send()


def gram_everywhere(n_rows, base, field, grad, tile, kind):
    cells = field.shape[1]
    nz = n_rows // NY
    f32 = jnp.float32
    vmem = pl.BlockSpec(memory_space=pltpu.VMEM)
    dma = pltpu.SemaphoreType.DMA
    blocks = lambda *lead: pltpu.VMEM(lead + (BLK, BLK), f32)
    return pl.pallas_call(
        functools.partial(gram_kernel, n_rows),
        out_shape=(
            jax.ShapeDtypeStruct((12, BLK, BLK), f32),
            jax.ShapeDtypeStruct((4, BLK, BLK), f32),
        ),
        in_specs=[pl.BlockSpec(memory_space=pl.ANY), vmem, vmem, vmem, vmem],
        out_specs=(vmem, vmem),
        scratch_shapes=[
            pltpu.VMEM((8, cells, BLK), jnp.bfloat16),
            pltpu.VMEM((cells, 8 * BLK), jnp.bfloat16),
            pltpu.VMEM((8, BLK), jnp.int32),
            pltpu.VMEM((8, 8, BLK), jnp.int32),
            pltpu.VMEM((8, cells), f32),
            pltpu.VMEM((8, cells), f32),
            blocks(2 * HALF), blocks(HALF), blocks(HALF), blocks(NX, 4), blocks(4),
            blocks(NY), blocks(), pltpu.VMEM((nz, 8, BLK), f32), pltpu.VMEM((8, BLK), f32),
            blocks(), blocks(4), blocks(2, 3),
            dma((8,)), dma((8,)), dma((8,)), dma((8,)), dma((2,)), dma((2,)),
            dma((2,)), dma((NX,)), dma((NX,)), dma((NY,)), dma((NY,)), dma((nz,)), dma((nz,)),
            dma((nz,)), dma((nz,)), dma((NY,)), dma((NY,)), dma((NX,)), dma((NX,)),
            dma((2,)), dma((2,)),
        ],
        compiler_params=pltpu.CompilerParams(
            collective_id=0, has_side_effects=True, vmem_limit_bytes=48 << 20
        ),
        name="gram",
    )(base, field, grad, tile, kind)


def dot_f32(left, right, dims=((1,), (0,))):
    return lax.dot_general(
        left, right, (dims, ((), ())), precision=HIGHEST, preferred_element_type=jnp.float32
    )


def across(vec, col):
    return jnp.broadcast_to(vec[:, col:col + 1], (8, BLK))


def along(vec, row):
    return jnp.broadcast_to(vec[row:row + 1, :], (8, BLK))


def eliminate_8(rows8, start):
    cols = [across(rows8, start + t) for t in range(8)]
    entry = [[along(cols[t], s) if t <= s else None for t in range(8)] for s in range(8)]
    inverse = [[None] * 8 for _ in range(8)]
    recip = []
    for t in range(8):
        recip.append(1.0 / entry[t][t])
        for s in range(t + 1, 8):
            factor = entry[s][t] * recip[t]
            for u in range(t + 1, s + 1):
                entry[s][u] = entry[s][u] - factor * entry[u][t]
            for u in range(t):
                inverse[s][u] = inverse[s][u] - factor * inverse[t][u]
            inverse[s][t] = -factor
    return inverse, recip


def factor_block(work, scaled):
    rows = lax.broadcasted_iota(jnp.int32, (8, BLK), 0)
    for q in range(4):
        at = [32 * q + 8 * s for s in range(4)]
        xa = [work[a:a + 8, 0:BLK] for a in at]
        xe = [work[a:a + 8, BLK:2 * BLK] for a in at]
        for s in range(4):
            inverse, recip = eliminate_8(xa[s], at[s])
            new_a, new_e = xa[s], xe[s]
            for t in range(7):
                col = jnp.zeros((8, BLK), jnp.float32)
                for u in range(t + 1, 8):
                    col = jnp.where(rows == u, inverse[u][t], col)
                new_a = new_a + col * along(xa[s], t)
                new_e = new_e + col * along(xe[s], t)
            scale = recip[0]
            for u in range(1, 8):
                scale = jnp.where(rows == u, recip[u], scale)
            scale = jnp.sqrt(scale)
            scaled[at[s]:at[s] + 8, 0:BLK] = new_a * scale
            scaled[at[s]:at[s] + 8, BLK:2 * BLK] = new_e * scale
            row_a = [along(new_a, t) for t in range(8)] if s < 3 else None
            row_e = [along(new_e, t) for t in range(8)] if s < 3 else None
            for later in range(s + 1, 4):
                cols = [across(xa[later], at[s] + u) for u in range(8)]
                for t in range(8):
                    mult = cols[t]
                    for u in range(t):
                        mult = mult + cols[u] * inverse[t][u]
                    mult = mult * recip[t]
                    xa[later] = xa[later] - mult * row_a[t]
                    xe[later] = xe[later] - mult * row_e[t]
        if q < 3:
            low = 32 * (q + 1)
            done = scaled[32 * q:low, :]
            work[low:BLK, :] = work[low:BLK, :] - dot_f32(done[:, low:BLK], done, ((0,), (0,)))


def factor_kernel(head_ref, own_ref, r_ref, m_ref, mat, work, scaled, inv):
    c = lax.axis_index("cols")
    eye = (
        lax.broadcasted_iota(jnp.int32, (BLK, BLK), 0)
        == lax.broadcasted_iota(jnp.int32, (BLK, BLK), 1)
    ).astype(jnp.float32)
    near = jnp.minimum(c, 3)
    for k in range(4):
        for j in range(k, 4):
            mat[k, :, j * BLK:(j + 1) * BLK] = head_ref[HEAD.index((k, j))]
        low, high = jnp.minimum(near, k), jnp.maximum(near, k)
        found = head_ref[low * 4 - low * (low - 1) // 2 + high - low]
        found = jnp.where(k <= near, found, found.T)
        mat[k, :, 512:640] = jnp.where(c >= 4, own_ref[k], found)
        mat[k, :, 640:768] = jnp.broadcast_to(head_ref[len(HEAD), k:k + 1, :], (BLK, BLK)).T
    for k in range(4):
        work[:, 0:BLK] = mat[k, :, k * BLK:(k + 1) * BLK]
        work[:, BLK:2 * BLK] = eye
        factor_block(work, scaled)
        low = (k + 1) * BLK
        inv[k] = scaled[:, BLK:2 * BLK]
        mat[k, :, low:768] = dot_f32(scaled[:, BLK:2 * BLK], mat[k, :, low:768])
        r_ref[k * BLK:(k + 1) * BLK, :] = mat[k, :, 512:640]
        for i in range(k + 1, 4):
            mat[i, :, i * BLK:768] = mat[i, :, i * BLK:768] - dot_f32(
                mat[k, :, i * BLK:(i + 1) * BLK], mat[k, :, i * BLK:768], ((0,), (0,))
            )
    solved = [None] * 4
    for k in (3, 2, 1, 0):
        rest = mat[k, :, 640:768]
        for i in range(k + 1, 4):
            rest = rest - dot_f32(mat[k, :, i * BLK:(i + 1) * BLK], solved[i])
        solved[k] = dot_f32(inv[k], rest, ((0,), (0,)))
        m_ref[k:k + 1, :] = solved[k].T[0:1, :]


def factor_and_solve(head, own):
    f32 = jnp.float32
    vmem = pl.BlockSpec(memory_space=pltpu.VMEM)
    return pl.pallas_call(
        factor_kernel,
        out_shape=(
            jax.ShapeDtypeStruct((512, BLK), f32),
            jax.ShapeDtypeStruct((4, BLK), f32),
        ),
        in_specs=[vmem, vmem],
        out_specs=(vmem, vmem),
        scratch_shapes=[
            pltpu.VMEM((4, BLK, 768), f32),
            pltpu.VMEM((BLK, 2 * BLK), f32),
            pltpu.VMEM((BLK, 2 * BLK), f32),
            pltpu.VMEM((4, BLK, BLK), f32),
        ],
        compiler_params=pltpu.CompilerParams(vmem_limit_bytes=48 << 20),
        name="factor",
    )(head, own)


def shards(n_rows, sens_base, design_field, gradient, tile_index, type_codes):
    head, own = gram_everywhere(
        n_rows, sens_base, design_field, gradient,
        tile_index.reshape(1, BLK), type_codes.reshape(1, BLK),
    )
    r_panels, multipliers = factor_and_solve(head, own)
    return r_panels, multipliers.reshape(-1)


def solution(mesh):
    placed = (P("rows", "cols"), P("rows", None), P("rows", None), P("cols"), P("cols"))
    return jax.shard_map(
        functools.partial(shards, mesh.shape["rows"]),
        mesh=mesh, in_specs=placed, out_specs=(P(None, "cols"), P()), check_vma=False,
    )
```

```python
import functools

import jax
import jax.numpy as jnp
from jax import lax
from jax.experimental import pallas as pl
from jax.experimental.pallas import tpu as pltpu
from jax.sharding import PartitionSpec as P

TILE = 128
BLK = 128
NX = 4
NY = 4
MESH = pl.DeviceIdType.MESH
HIGHEST = lax.Precision.HIGHEST
HEAD = [(a, b) for a in range(4) for b in range(a, 4)]
COUNT_X = (3, 3, 4, 4)
FIRST_X = (0, 3, 6, 10)
COUNT_Y = (4, 4, 4, 2)
FIRST_Y = (0, 4, 8, 12)
HALF = 14
ROWS = BLK // 2


def slot_of(core, x, y):
    if x < 2:
        spot = (core * 2 + x) * 3 + y
        if spot < len(HEAD):
            return HEAD[spot]
        return "proj" if spot == len(HEAD) else None
    return (y, x * 2 + core)


def gram_kernel(
    n_rows,
    base_ref, field_hbm, grad_hbm, tile_hbm, type_hbm,
    out_a, out_b, own_ref,
    raw, jac, field_ref, grad_ref, tile_ref, type_ref, codes_mine, codes, north, south,
    parts, from_core, half, from_x, from_y, sum_a, sum_b, from_x2, from_y2,
    block, from_zl, from_zh, line,
    load_sems, a2a_send, a2a_recv, code_send, code_recv, halo_send, halo_recv, core_sems,
    xa_send, xa_recv, yb_send, yb_recv, ya_send, ya_recv, xb_send, xb_recv,
    zl_send, zl_recv, zh_send, zh_recv, zg_send, zg_recv,
    gy_send, gy_recv, gx_send, gx_recv, hx_send, hx_recv, hy_send, hy_recv,
    cg_send, cg_recv,
):
    r = lax.axis_index("rows")
    c = lax.axis_index("cols")
    z, y = r // NY, r % NY
    zh, zl = z // 4, z % 4
    hops = n_rows // NY // 4
    x, core = c // 2, c % 2
    up, down = (r + n_rows - 1) % n_rows, (r + 1) % n_rows
    cells = raw.shape[1]

    def dev_c(col):
        return (r, col)

    def dev_x(xx):
        return (r, xx * 2 + core)

    def dev_y(yy):
        return (z * NY + yy, c)

    def dev_z(hi, lo):
        return ((hi * 4 + lo) * NY + y, c)

    def remote(src, dst, send, recv, device):
        return pltpu.make_async_remote_copy(
            src_ref=src, dst_ref=dst, send_sem=send, recv_sem=recv,
            device_id=device, device_id_type=MESH,
        )

    barrier = pltpu.get_barrier_semaphore()

    def greet(device):
        pl.semaphore_signal(barrier, inc=1, device_id=device, device_id_type=MESH)

    for d in range(1, 8):
        greet(dev_c((c + d) % 8))
    for d in range(1, NY):
        greet(dev_y((y + d) % NY))
    for d in range(1, 4):
        greet(dev_z(zh, (zl + d) % 4))
    for d in range(1, hops):
        greet(dev_z((zh + d) % hops, zl))
    greet((up, c))
    greet((down, c))
    loads = []
    for i, (src, dst) in enumerate((
        (field_hbm, field_ref), (tile_hbm, tile_ref), (type_hbm, type_ref), (grad_hbm, grad_ref),
    )):
        loads.append(pltpu.make_async_copy(src, dst, load_sems.at[i]))
        loads[-1].start()
    codes_mine[...] = jnp.zeros_like(codes_mine)
    loads[1].wait()
    loads[2].wait()
    codes_mine[0:1, :] = tile_ref[...]
    codes_mine[1:2, :] = type_ref[...]
    loads[0].wait()
    pl.semaphore_wait(barrier, 7 + (NY - 1) + 3 + (hops - 1) + 2)

    sent = []
    for d in range(1, 8):
        to = (c + d) % 8
        cp = remote(codes_mine, codes.at[c], code_send.at[d], code_recv.at[d], dev_c(to))
        cp.start()
        sent.append(cp)
    cp = remote(field_ref, north, halo_send.at[0], halo_recv.at[0], (down, c))
    cp.start()
    sent.append(cp)
    cp = remote(field_ref, south, halo_send.at[1], halo_recv.at[1], (up, c))
    cp.start()
    sent.append(cp)
    for d in (4, 3, 5, 2, 6, 1, 7):
        to = (c + d) % 8
        cp = remote(
            base_ref.at[pl.ds(to * cells, cells), :], raw.at[c],
            a2a_send.at[d], a2a_recv.at[d], dev_c(to),
        )
        cp.start()
        sent.append(cp)
    mine = pltpu.make_async_copy(
        base_ref.at[pl.ds(c * cells, cells), :], raw.at[c], a2a_recv.at[0]
    )
    mine.start()
    codes[c] = codes_mine[...]

    remote(field_ref, north, halo_send.at[0], halo_recv.at[0], (up, c)).wait_recv()
    remote(field_ref, south, halo_send.at[1], halo_recv.at[1], (down, c)).wait_recv()
    here = field_ref[pl.ds(c, 1), :]
    above = field_ref[pl.ds((c + 7) % 8, 1), :]
    below = field_ref[pl.ds((c + 1) % 8, 1), :]
    above = jnp.where(c == 0, jnp.where(r == 0, 0.0, north[7:8, :]), above)
    below = jnp.where(c == 7, jnp.where(r == n_rows - 1, 0.0, south[0:1, :]), below)
    wide = (8, cells)
    here = jnp.broadcast_to(here, wide)
    above = jnp.broadcast_to(above, wide)
    below = jnp.broadcast_to(below, wide)
    lane = lax.broadcasted_iota(jnp.int32, wide, 1)
    west = jnp.where(lane == 0, 0.0, pltpu.roll(here, 1, 1))
    east = jnp.where(lane == cells - 1, 0.0, pltpu.roll(here, cells - 1, 1))
    laplace = 4.0 * here - (above + below + west + east)
    slope_x = 0.5 * (east - west)
    slope_y = 0.5 * (below - above)
    srow = lax.broadcasted_iota(jnp.int32, wide, 0)
    terms = []
    for fieldval in (laplace, slope_x, slope_y):
        rest = fieldval / TILE
        for _ in range(3):
            term = rest.astype(jnp.bfloat16).astype(jnp.float32)
            terms.append(term)
            rest = rest - term
    low = jnp.zeros(wide, jnp.float32)
    for k in range(8):
        low = jnp.where(srow == k, terms[(k % 3) * 3 + k // 3], low)
    high = jnp.where(srow == 0, terms[2 * 3 + 2], 0.0)
    both = jnp.concatenate([low, high], axis=0)
    tiles = cells // TILE
    spread = jnp.concatenate([both] * tiles, axis=0)
    krow = lax.broadcasted_iota(jnp.int32, spread.shape, 0)
    kcol = lax.broadcasted_iota(jnp.int32, spread.shape, 1)
    spread = jnp.where(krow // 16 == kcol // TILE, spread, 0.0)
    spread_t = spread.T.astype(jnp.bfloat16)

    first_tile = (r * 8 // TILE) * tiles
    rows16 = lax.broadcasted_iota(jnp.int32, (16 * tiles, BLK), 0)
    term_id = rows16 % 16
    kind_of = jnp.where(term_id < 9, term_id % 3, 3)
    tile_of = first_tile + rows16 // 16
    for d in range(1, 8):
        src = (c + 8 - d) % 8
        remote(codes_mine, codes.at[src], code_send.at[d], code_recv.at[d], dev_c(src)).wait_recv()

    for cs in range(8):
        @pl.when(c == cs)
        def _():
            mine.wait()

        @pl.when(c != cs)
        def _():
            d = (c + 8 - cs) % 8
            remote(
                base_ref.at[pl.ds(0, cells), :], raw.at[cs],
                a2a_send.at[d], a2a_recv.at[d], dev_c(cs),
            ).wait_recv()

        chosen = jnp.logical_and(
            kind_of == codes[cs, 1:2, :], tile_of == codes[cs, 0:1, :]
        ).astype(jnp.float32).astype(jnp.bfloat16)
        added = jnp.dot(spread_t, chosen, preferred_element_type=jnp.float32)
        jac[:, cs * BLK:(cs + 1) * BLK] = (raw[cs].astype(jnp.float32) + added).astype(jnp.bfloat16)

    where = {}
    for k in range(2):
        for xx in range(NX):
            for yy in range(COUNT_X[xx]):
                low = FIRST_Y[yy] + (xx if yy < 3 else xx - 2)
                where[slot_of(k, xx, yy)] = (k, FIRST_X[xx] + yy, HALF + low)

    def put(key, value):
        k, upper, lower = where[key]
        parts[k, upper] = value[0:ROWS]
        parts[k, lower] = value[ROWS:BLK]

    contract = (((0,), (0,)), ((), ()))
    for pa in range(2):
        left = jac[:, pa * 256:(pa + 1) * 256]
        for pb in range(pa, 4):
            prod = lax.dot_general(
                left, jac[:, pb * 256:(pb + 1) * 256], contract,
                preferred_element_type=jnp.float32,
            )
            for i in range(2):
                for j in range(2):
                    key = (pa * 2 + i, pb * 2 + j)
                    if key in where:
                        put(key, prod[i * BLK:(i + 1) * BLK, j * BLK:(j + 1) * BLK])
    loads[3].wait()
    proj = jnp.dot(grad_ref[...], jac[:, 0:512], preferred_element_type=jnp.float32)
    proj = jnp.sum(
        jnp.where(lax.broadcasted_iota(jnp.int32, proj.shape, 0) == c, proj, 0.0),
        axis=0, keepdims=True,
    )
    put("proj", jnp.zeros((BLK, BLK), jnp.float32))
    put(None, jnp.zeros((BLK, BLK), jnp.float32))
    k, upper, _ = where["proj"]
    for i in range(4):
        parts[k, upper, i:i + 1, :] = proj[:, i * BLK:(i + 1) * BLK]

    cp = remote(
        parts.at[1 - core], from_core, core_sems.at[0], core_sems.at[1], dev_c(x * 2 + 1 - core)
    )
    cp.start()
    sent.append(cp)
    cp.wait_recv()
    half[...] = parts[core] + from_core[...]

    def xa_copy(xx, d, peer):
        span = COUNT_X[xx]
        return remote(
            half.at[pl.ds(FIRST_X[xx], span)], from_x.at[d, pl.ds(0, span)],
            xa_send.at[d], xa_recv.at[d], dev_x(peer),
        )

    def yb_copy(yy, d, peer):
        span = COUNT_Y[yy]
        return remote(
            half.at[pl.ds(HALF + FIRST_Y[yy], span)], from_y.at[d, pl.ds(0, span)],
            yb_send.at[d], yb_recv.at[d], dev_y(peer),
        )

    for q in range(4):
        @pl.when(x != q)
        def _():
            xa_copy(q, (q + NX - x) % NX, q).start()

        @pl.when(y != q)
        def _():
            yb_copy(q, (q + NY - y) % NY, q).start()

    for q in range(4):
        @pl.when(x == q)
        def _():
            span = COUNT_X[q]
            total = half[FIRST_X[q]:FIRST_X[q] + span]
            for d in (1, 3, 2):
                xa_copy(q, d, (q + NX - d) % NX).wait_recv()
                total = total + from_x[d, 0:span]
            sum_a[0:span] = total

    for q in range(4):
        @pl.when(y == q)
        def _():
            span = COUNT_Y[q]
            total = half[HALF + FIRST_Y[q]:HALF + FIRST_Y[q] + span]
            for d in (1, 3, 2):
                yb_copy(q, d, (q + NY - d) % NY).wait_recv()
                total = total + from_y[d, 0:span]
            sum_b[0:span] = total

    skip = jnp.where(y == 3, 2, 0)
    holds = jnp.logical_or(x >= 2, y < 3)

    def ya_copy(d, yy, peer):
        return remote(sum_a.at[yy], from_y2.at[d], ya_send.at[d], ya_recv.at[d], dev_y(peer))

    def xb_copy(d, spot, peer):
        return remote(sum_b.at[spot], from_x2.at[d], xb_send.at[d], xb_recv.at[d], dev_x(peer))

    for d in range(1, 4):
        yy = (y + d) % NY
        xx = (x + d) % NX

        @pl.when(jnp.logical_or(x >= 2, yy < 3))
        def _():
            ya_copy(d, yy, yy).start()

        @pl.when(jnp.logical_or(xx >= 2, y < 3))
        def _():
            xb_copy(d, xx - skip, xx).start()

    def zl_copy(d, spot, peer):
        return remote(
            block.at[pl.ds(spot * 32, 32)], from_zl.at[d],
            zl_send.at[d], zl_recv.at[d], dev_z(zh, peer),
        )

    def zh_copy(d, spot, peer):
        return remote(
            from_zh.at[spot], from_zh.at[spot], zh_send.at[d], zh_recv.at[d], dev_z(peer, zl)
        )

    def zg_copy(d, spot, peer):
        return remote(
            line.at[pl.ds(spot * 32, 32)], line.at[pl.ds(spot * 32, 32)],
            zg_send.at[d], zg_recv.at[d], dev_z(zh, peer),
        )

    def gy_own(d, spot, peer):
        return remote(line, own_ref.at[spot], gy_send.at[d], gy_recv.at[d], dev_y(peer))

    def gy_head(d, spot, peer):
        return remote(
            line.at[pl.ds(0, ROWS)], out_a.at[core, x, spot],
            gy_send.at[d], gy_recv.at[d], dev_y(peer),
        )

    def gx_head(d, spot, peer):
        return remote(
            line.at[pl.ds(ROWS, ROWS)], out_b.at[core, y, spot],
            gx_send.at[d], gx_recv.at[d], dev_x(peer),
        )

    @pl.when(holds)
    def _():
        upper = sum_a[y]
        lower = sum_b[x - skip]
        for d in (1, 3, 2):
            ya_copy(d, 0, (y + NY - d) % NY).wait_recv()
            upper = upper + from_y2[d]
        for d in (1, 3, 2):
            xb_copy(d, 0, (x + NX - d) % NX).wait_recv()
            lower = lower + from_x2[d]
        block[0:ROWS] = upper
        block[ROWS:BLK] = lower
        for d in range(1, 4):
            lo = (zl + d) % 4
            zl_copy(d, lo, lo).start()
        total = block[pl.ds(pl.multiple_of(zl * 32, 32), 32)]
        for d in range(1, 4):
            zl_copy(d, 0, (zl + 4 - d) % 4).wait_recv()
            total = total + from_zl[d]
        from_zh[zh] = total
        for d in range(1, hops):
            zh_copy(d, zh, (zh + d) % hops).start()
        for d in range(1, hops):
            src = (zh + hops - d) % hops
            zh_copy(d, src, src).wait_recv()
        total = from_zh[0]
        for i in range(1, hops):
            total = total + from_zh[i]
        line[pl.ds(pl.multiple_of(zl * 32, 32), 32)] = total
        for d in range(1, 4):
            zg_copy(d, zl, (zl + d) % 4).start()
        for d in range(1, 4):
            src = (zl + 4 - d) % 4
            zg_copy(d, src, src).wait_recv()

        @pl.when(x >= 2)
        def _():
            for d in range(1, 4):
                gy_own(d, y, (y + d) % NY).start()
            own_ref[y] = line[...]

        @pl.when(x < 2)
        def _():
            for d in range(1, 4):
                gy_head(d, y, (y + d) % NY).start()
                gx_head(d, x, (x + d) % NX).start()
            out_a[core, x, y] = line[0:ROWS]
            out_b[core, y, x] = line[ROWS:BLK]

    def hx_copy(d, xx, peer):
        return remote(
            out_a.at[core, xx], out_a.at[core, xx], hx_send.at[d], hx_recv.at[d], dev_x(peer)
        )

    def hy_copy(d, yy, peer):
        return remote(
            out_b.at[core, yy], out_b.at[core, yy], hy_send.at[d], hy_recv.at[d], dev_y(peer)
        )

    @pl.when(x < 2)
    def _():
        for d in range(1, 4):
            src = (y + NY - d) % NY

            @pl.when(src < 3)
            def _():
                gy_head(d, src, src).wait_recv()

        for d in range(1, 4):
            hx_copy(d, x, (x + d) % NX).start()
        own_ref[...] = jnp.zeros_like(own_ref)

    @pl.when(y < 3)
    def _():
        for d in range(1, 4):
            src = (x + NX - d) % NX

            @pl.when(src < 2)
            def _():
                gx_head(d, src, src).wait_recv()

        for d in range(1, 4):
            hy_copy(d, y, (y + d) % NY).start()

    def swap_a(half_core):
        return remote(
            out_a.at[half_core], out_a.at[half_core], cg_send.at[0], cg_recv.at[0],
            dev_c(x * 2 + 1 - core),
        )

    def swap_b(half_core):
        return remote(
            out_b.at[half_core], out_b.at[half_core], cg_send.at[1], cg_recv.at[1],
            dev_c(x * 2 + 1 - core),
        )

    for d in range(1, 4):
        src = (y + NY - d) % NY

        @pl.when(src < 3)
        def _():
            hy_copy(d, src, src).wait_recv()

    swap_b(core).start()
    for d in range(1, 4):
        src = (x + NX - d) % NX

        @pl.when(src < 2)
        def _():
            hx_copy(d, src, src).wait_recv()

    swap_a(core).start()

    @pl.when(x >= 2)
    def _():
        for d in range(1, 4):
            src = (y + NY - d) % NY
            gy_own(d, src, src).wait_recv()

    swap_b(1 - core).wait_recv()
    swap_a(1 - core).wait_recv()

    for cp in sent:
        cp.wait_send()
    for q in range(4):
        @pl.when(x != q)
        def _():
            xa_copy(q, (q + NX - x) % NX, q).wait_send()

        @pl.when(y != q)
        def _():
            yb_copy(q, (q + NY - y) % NY, q).wait_send()

    for d in range(1, 4):
        yy = (y + d) % NY
        xx = (x + d) % NX

        @pl.when(jnp.logical_or(x >= 2, yy < 3))
        def _():
            ya_copy(d, yy, yy).wait_send()

        @pl.when(jnp.logical_or(xx >= 2, y < 3))
        def _():
            xb_copy(d, xx - skip, xx).wait_send()

    @pl.when(holds)
    def _():
        for d in range(1, 4):
            lo = (zl + d) % 4
            zl_copy(d, lo, lo).wait_send()
            zg_copy(d, zl, lo).wait_send()
        for d in range(1, hops):
            zh_copy(d, zh, (zh + d) % hops).wait_send()

        @pl.when(x >= 2)
        def _():
            for d in range(1, 4):
                gy_own(d, y, (y + d) % NY).wait_send()

        @pl.when(x < 2)
        def _():
            for d in range(1, 4):
                gy_head(d, y, (y + d) % NY).wait_send()
                gx_head(d, x, (x + d) % NX).wait_send()

    @pl.when(x < 2)
    def _():
        for d in range(1, 4):
            hx_copy(d, x, (x + d) % NX).wait_send()

    @pl.when(y < 3)
    def _():
        for d in range(1, 4):
            hy_copy(d, y, (y + d) % NY).wait_send()

    swap_b(core).wait_send()
    swap_a(core).wait_send()


def gram_everywhere(n_rows, base, field, grad, tile, kind):
    cells = field.shape[1]
    hops = n_rows // NY // 4
    f32 = jnp.float32
    vmem = pl.BlockSpec(memory_space=pltpu.VMEM)
    hbm = pl.BlockSpec(memory_space=pltpu.HBM)
    pairs = [pltpu.SemaphoreType.DMA((4,))] * 2
    halves = lambda *lead: pltpu.VMEM(lead + (ROWS, BLK), f32)
    strip = lambda dtype: pltpu.VMEM((8, cells), dtype)
    return pl.pallas_call(
        functools.partial(gram_kernel, n_rows),
        out_shape=(
            jax.ShapeDtypeStruct((2, 2, 3, ROWS, BLK), f32),
            jax.ShapeDtypeStruct((2, 3, 2, ROWS, BLK), f32),
            jax.ShapeDtypeStruct((4, BLK, BLK), f32),
        ),
        in_specs=[hbm] * 5,
        out_specs=(vmem, vmem, vmem),
        scratch_shapes=[
            pltpu.VMEM((8, cells, BLK), jnp.bfloat16),
            pltpu.VMEM((cells, 8 * BLK), jnp.bfloat16),
            strip(f32), strip(jnp.bfloat16),
            pltpu.VMEM((1, BLK), jnp.int32), pltpu.VMEM((1, BLK), jnp.int32),
            pltpu.VMEM((8, BLK), jnp.int32), pltpu.VMEM((8, 8, BLK), jnp.int32),
            strip(f32), strip(f32),
            halves(2, 2 * HALF), halves(2 * HALF), halves(2 * HALF),
            halves(4, 4), halves(4, 4), halves(4), halves(4), halves(4), halves(4),
            pltpu.VMEM((BLK, BLK), f32), pltpu.VMEM((4, 32, BLK), f32),
            pltpu.VMEM((hops, 32, BLK), f32), pltpu.VMEM((BLK, BLK), f32),
            pltpu.SemaphoreType.DMA((4,)),
            *[pltpu.SemaphoreType.DMA((8,))] * 4,
            pltpu.SemaphoreType.DMA((2,)), pltpu.SemaphoreType.DMA((2,)),
            pltpu.SemaphoreType.DMA((2,)),
            *pairs * 4, *pairs, *pairs, *pairs, *pairs * 4,
            pltpu.SemaphoreType.DMA((2,)), pltpu.SemaphoreType.DMA((2,)),
        ],
        compiler_params=pltpu.CompilerParams(
            collective_id=0, has_side_effects=True, vmem_limit_bytes=48 << 20
        ),
        name="gram",
    )(*[pltpu.with_memory_space_constraint(v, pltpu.HBM) for v in (base, field, grad, tile, kind)])


def dot_f32(left, right, dims=((1,), (0,))):
    return lax.dot_general(
        left, right, (dims, ((), ())), precision=HIGHEST, preferred_element_type=jnp.float32
    )


def across(vec, col):
    return jnp.broadcast_to(vec[:, col:col + 1], (8, BLK))


def along(vec, row):
    return jnp.broadcast_to(vec[row:row + 1, :], (8, BLK))


def eliminate_8(rows8, start):
    cols = [across(rows8, start + t) for t in range(8)]
    entry = [[along(cols[t], s) if t <= s else None for t in range(8)] for s in range(8)]
    inverse = [[None] * 8 for _ in range(8)]
    recip = []
    for t in range(8):
        recip.append(1.0 / entry[t][t])
        for s in range(t + 1, 8):
            factor = entry[s][t] * recip[t]
            for u in range(t + 1, s + 1):
                entry[s][u] = entry[s][u] - factor * entry[u][t]
            for u in range(t):
                inverse[s][u] = inverse[s][u] - factor * inverse[t][u]
            inverse[s][t] = -factor
    return inverse, recip


def factor_block(work, scaled):
    rows = lax.broadcasted_iota(jnp.int32, (8, BLK), 0)
    for q in range(4):
        at = [32 * q + 8 * s for s in range(4)]
        xa = [work[a:a + 8, 0:BLK] for a in at]
        xe = [work[a:a + 8, BLK:2 * BLK] for a in at]
        for s in range(4):
            inverse, recip = eliminate_8(xa[s], at[s])
            new_a, new_e = xa[s], xe[s]
            for t in range(7):
                col = jnp.zeros((8, BLK), jnp.float32)
                for u in range(t + 1, 8):
                    col = jnp.where(rows == u, inverse[u][t], col)
                new_a = new_a + col * along(xa[s], t)
                new_e = new_e + col * along(xe[s], t)
            scale = recip[0]
            for u in range(1, 8):
                scale = jnp.where(rows == u, recip[u], scale)
            scale = jnp.sqrt(scale)
            scaled[at[s]:at[s] + 8, 0:BLK] = new_a * scale
            scaled[at[s]:at[s] + 8, BLK:2 * BLK] = new_e * scale
            row_a = [along(new_a, t) for t in range(8)] if s < 3 else None
            row_e = [along(new_e, t) for t in range(8)] if s < 3 else None
            for later in range(s + 1, 4):
                cols = [across(xa[later], at[s] + u) for u in range(8)]
                for t in range(8):
                    mult = cols[t]
                    for u in range(t):
                        mult = mult + cols[u] * inverse[t][u]
                    mult = mult * recip[t]
                    xa[later] = xa[later] - mult * row_a[t]
                    xe[later] = xe[later] - mult * row_e[t]
        if q < 3:
            low = 32 * (q + 1)
            done = scaled[32 * q:low, :]
            work[low:BLK, :] = work[low:BLK, :] - dot_f32(done[:, low:BLK], done, ((0,), (0,)))


def factor_kernel(head_a, head_b, own_ref, r_ref, m_ref, mat, head_ref, work, scaled, inv):
    c = lax.axis_index("cols")
    eye = (
        lax.broadcasted_iota(jnp.int32, (BLK, BLK), 0)
        == lax.broadcasted_iota(jnp.int32, (BLK, BLK), 1)
    ).astype(jnp.float32)
    for spot in range(12):
        k, at_x, at_y = spot // 6, spot // 3 % 2, spot % 3
        head_ref[spot, 0:ROWS] = head_a[k, at_x, at_y]
        head_ref[spot, ROWS:BLK] = head_b[k, at_y, at_x]
    near = jnp.minimum(c, 3)
    for k in range(4):
        for j in range(k, 4):
            mat[k, :, j * BLK:(j + 1) * BLK] = head_ref[HEAD.index((k, j))]
        low, high = jnp.minimum(near, k), jnp.maximum(near, k)
        found = head_ref[low * 4 - low * (low - 1) // 2 + high - low]
        found = jnp.where(k <= near, found, found.T)
        mat[k, :, 512:640] = jnp.where(c >= 4, own_ref[k], found)
        mat[k, :, 640:768] = jnp.broadcast_to(head_ref[len(HEAD), k:k + 1, :], (BLK, BLK)).T
    for k in range(4):
        work[:, 0:BLK] = mat[k, :, k * BLK:(k + 1) * BLK]
        work[:, BLK:2 * BLK] = eye
        factor_block(work, scaled)
        low = (k + 1) * BLK
        inv[k] = scaled[:, BLK:2 * BLK]
        mat[k, :, low:768] = dot_f32(scaled[:, BLK:2 * BLK], mat[k, :, low:768])
        r_ref[k * BLK:(k + 1) * BLK, :] = mat[k, :, 512:640]
        for i in range(k + 1, 4):
            mat[i, :, i * BLK:768] = mat[i, :, i * BLK:768] - dot_f32(
                mat[k, :, i * BLK:(i + 1) * BLK], mat[k, :, i * BLK:768], ((0,), (0,))
            )
    solved = [None] * 4
    for k in (3, 2, 1, 0):
        rest = mat[k, :, 640:768]
        for i in range(k + 1, 4):
            rest = rest - dot_f32(mat[k, :, i * BLK:(i + 1) * BLK], solved[i])
        solved[k] = dot_f32(inv[k], rest, ((0,), (0,)))
        m_ref[k:k + 1, :] = solved[k].T[0:1, :]


def factor_and_solve(head_a, head_b, own):
    f32 = jnp.float32
    vmem = pl.BlockSpec(memory_space=pltpu.VMEM)
    return pl.pallas_call(
        factor_kernel,
        out_shape=(
            jax.ShapeDtypeStruct((512, BLK), f32),
            jax.ShapeDtypeStruct((4, BLK), f32),
        ),
        in_specs=[vmem, vmem, vmem],
        out_specs=(vmem, vmem),
        scratch_shapes=[
            pltpu.VMEM((4, BLK, 768), f32),
            pltpu.VMEM((12, BLK, BLK), f32),
            pltpu.VMEM((BLK, 2 * BLK), f32),
            pltpu.VMEM((BLK, 2 * BLK), f32),
            pltpu.VMEM((4, BLK, BLK), f32),
        ],
        compiler_params=pltpu.CompilerParams(vmem_limit_bytes=48 << 20),
        name="factor",
    )(head_a, head_b, own)


def shards(n_rows, sens_base, design_field, gradient, tile_index, type_codes):
    head_a, head_b, own = gram_everywhere(
        n_rows, sens_base, design_field, gradient,
        tile_index.reshape(1, BLK), type_codes.reshape(1, BLK),
    )
    r_panels, multipliers = factor_and_solve(head_a, head_b, own)
    return r_panels, multipliers.reshape(-1)


def solution(mesh):
    placed = (P("rows", "cols"), P("rows", None), P("rows", None), P("cols"), P("cols"))
    return jax.shard_map(
        functools.partial(shards, mesh.shape["rows"]),
        mesh=mesh, in_specs=placed, out_specs=(P(None, "cols"), P()), check_vma=False,
    )
```

```python
import functools

import jax
import jax.numpy as jnp
from jax import lax
from jax.experimental import pallas as pl
from jax.experimental.pallas import tpu as pltpu
from jax.sharding import PartitionSpec as P

TILE = 128
BLK = 128
NX = 4
NY = 4
MESH = pl.DeviceIdType.MESH
HIGHEST = lax.Precision.HIGHEST
HEAD = [(a, b) for a in range(4) for b in range(a, 4)]
COUNT_X = (3, 3, 4, 4)
FIRST_X = (0, 3, 6, 10)
COUNT_Y = (4, 4, 4, 2)
FIRST_Y = (0, 4, 8, 12)
HALF = 14
ROWS = BLK // 2


def slot_of(core, x, y):
    if x < 2:
        spot = (core * 2 + x) * 3 + y
        if spot < len(HEAD):
            return HEAD[spot]
        return "proj" if spot == len(HEAD) else None
    return (y, x * 2 + core)


def gram_kernel(
    n_rows,
    base_ref, field_hbm, grad_hbm, tile_hbm, type_hbm,
    out_a, out_b, own_ref,
    raw, jac, field_ref, grad_ref, tile_ref, type_ref, codes_mine, codes, north, south,
    parts, from_core, half, from_x, from_y, sum_a, sum_b, from_x2, from_y2,
    block, from_zl, from_zh, line,
    load_sems, a2a_send, a2a_recv, code_send, code_recv, halo_send, halo_recv, core_sems,
    xa_send, xa_recv, yb_send, yb_recv, ya_send, ya_recv, xb_send, xb_recv,
    zl_send, zl_recv, zh_send, zh_recv, zg_send, zg_recv,
    gy_send, gy_recv, gx_send, gx_recv, hx_send, hx_recv, hy_send, hy_recv,
    cg_send, cg_recv,
):
    r = lax.axis_index("rows")
    c = lax.axis_index("cols")
    z, y = r // NY, r % NY
    zh, zl = z // 4, z % 4
    hops = n_rows // NY // 4
    x, core = c // 2, c % 2
    up, down = (r + n_rows - 1) % n_rows, (r + 1) % n_rows
    cells = raw.shape[1]

    def dev_c(col):
        return (r, col)

    def dev_x(xx):
        return (r, xx * 2 + core)

    def dev_y(yy):
        return (z * NY + yy, c)

    def dev_z(hi, lo):
        return ((hi * 4 + lo) * NY + y, c)

    def remote(src, dst, send, recv, device):
        return pltpu.make_async_remote_copy(
            src_ref=src, dst_ref=dst, send_sem=send, recv_sem=recv,
            device_id=device, device_id_type=MESH,
        )

    barrier = pltpu.get_barrier_semaphore()

    def greet(device):
        pl.semaphore_signal(barrier, inc=1, device_id=device, device_id_type=MESH)

    for d in range(1, 8):
        greet(dev_c((c + d) % 8))
    for d in range(1, NY):
        greet(dev_y((y + d) % NY))
    for d in range(1, 4):
        greet(dev_z(zh, (zl + d) % 4))
    for d in range(1, hops):
        greet(dev_z((zh + d) % hops, zl))
    greet((up, c))
    greet((down, c))
    loads = []
    for i, (src, dst) in enumerate((
        (field_hbm, field_ref), (tile_hbm, tile_ref), (type_hbm, type_ref), (grad_hbm, grad_ref),
    )):
        loads.append(pltpu.make_async_copy(src, dst, load_sems.at[i]))
        loads[-1].start()
    codes_mine[...] = jnp.zeros_like(codes_mine)
    loads[1].wait()
    loads[2].wait()
    codes_mine[0:1, :] = tile_ref[...]
    codes_mine[1:2, :] = type_ref[...]
    loads[0].wait()
    pl.semaphore_wait(barrier, 7 + (NY - 1) + 3 + (hops - 1) + 2)

    sent = []
    for d in range(1, 8):
        to = (c + d) % 8
        cp = remote(codes_mine, codes.at[c], code_send.at[d], code_recv.at[d], dev_c(to))
        cp.start()
        sent.append(cp)
    cp = remote(field_ref, north, halo_send.at[0], halo_recv.at[0], (down, c))
    cp.start()
    sent.append(cp)
    cp = remote(field_ref, south, halo_send.at[1], halo_recv.at[1], (up, c))
    cp.start()
    sent.append(cp)
    for d in (4, 3, 5, 2, 6, 1, 7):
        to = (c + d) % 8
        cp = remote(
            base_ref.at[pl.ds(to * cells, cells), :], raw.at[c],
            a2a_send.at[d], a2a_recv.at[d], dev_c(to),
        )
        cp.start()
        sent.append(cp)
    mine = pltpu.make_async_copy(
        base_ref.at[pl.ds(c * cells, cells), :], raw.at[c], a2a_recv.at[0]
    )
    mine.start()
    codes[c] = codes_mine[...]

    remote(field_ref, north, halo_send.at[0], halo_recv.at[0], (up, c)).wait_recv()
    remote(field_ref, south, halo_send.at[1], halo_recv.at[1], (down, c)).wait_recv()
    here = field_ref[pl.ds(c, 1), :]
    above = field_ref[pl.ds((c + 7) % 8, 1), :]
    below = field_ref[pl.ds((c + 1) % 8, 1), :]
    above = jnp.where(c == 0, jnp.where(r == 0, 0.0, north[7:8, :]), above)
    below = jnp.where(c == 7, jnp.where(r == n_rows - 1, 0.0, south[0:1, :]), below)
    wide = (8, cells)
    here = jnp.broadcast_to(here, wide)
    above = jnp.broadcast_to(above, wide)
    below = jnp.broadcast_to(below, wide)
    lane = lax.broadcasted_iota(jnp.int32, wide, 1)
    west = jnp.where(lane == 0, 0.0, pltpu.roll(here, 1, 1))
    east = jnp.where(lane == cells - 1, 0.0, pltpu.roll(here, cells - 1, 1))
    laplace = 4.0 * here - (above + below + west + east)
    slope_x = 0.5 * (east - west)
    slope_y = 0.5 * (below - above)
    srow = lax.broadcasted_iota(jnp.int32, wide, 0)
    terms = []
    for fieldval in (laplace, slope_x, slope_y):
        rest = fieldval / TILE
        for _ in range(3):
            term = rest.astype(jnp.bfloat16).astype(jnp.float32)
            terms.append(term)
            rest = rest - term
    low = jnp.zeros(wide, jnp.float32)
    for k in range(8):
        low = jnp.where(srow == k, terms[(k % 3) * 3 + k // 3], low)
    high = jnp.where(srow == 0, terms[2 * 3 + 2], 0.0)
    both = jnp.concatenate([low, high], axis=0)
    tiles = cells // TILE
    spread = jnp.concatenate([both] * tiles, axis=0)
    krow = lax.broadcasted_iota(jnp.int32, spread.shape, 0)
    kcol = lax.broadcasted_iota(jnp.int32, spread.shape, 1)
    spread = jnp.where(krow // 16 == kcol // TILE, spread, 0.0)
    spread_t = spread.T.astype(jnp.bfloat16)

    first_tile = (r * 8 // TILE) * tiles
    rows16 = lax.broadcasted_iota(jnp.int32, (16 * tiles, BLK), 0)
    term_id = rows16 % 16
    kind_of = jnp.where(term_id < 9, term_id % 3, 3)
    tile_of = first_tile + rows16 // 16
    for d in range(1, 8):
        src = (c + 8 - d) % 8
        remote(codes_mine, codes.at[src], code_send.at[d], code_recv.at[d], dev_c(src)).wait_recv()

    for cs in range(8):
        @pl.when(c == cs)
        def _():
            mine.wait()

        @pl.when(c != cs)
        def _():
            d = (c + 8 - cs) % 8
            remote(
                base_ref.at[pl.ds(0, cells), :], raw.at[cs],
                a2a_send.at[d], a2a_recv.at[d], dev_c(cs),
            ).wait_recv()

        chosen = jnp.logical_and(
            kind_of == codes[cs, 1:2, :], tile_of == codes[cs, 0:1, :]
        ).astype(jnp.float32).astype(jnp.bfloat16)
        added = jnp.dot(spread_t, chosen, preferred_element_type=jnp.float32)
        jac[:, cs * BLK:(cs + 1) * BLK] = (raw[cs].astype(jnp.float32) + added).astype(jnp.bfloat16)

    where = {}
    for k in range(2):
        for xx in range(NX):
            for yy in range(COUNT_X[xx]):
                low = FIRST_Y[yy] + (xx if yy < 3 else xx - 2)
                where[slot_of(k, xx, yy)] = (k, FIRST_X[xx] + yy, HALF + low)

    def put(key, value):
        k, upper, lower = where[key]
        parts[k, upper] = value[0:ROWS]
        parts[k, lower] = value[ROWS:BLK]

    contract = (((0,), (0,)), ((), ()))
    for pa in range(2):
        left = jac[:, pa * 256:(pa + 1) * 256]
        for pb in range(pa, 4):
            prod = lax.dot_general(
                left, jac[:, pb * 256:(pb + 1) * 256], contract,
                preferred_element_type=jnp.float32,
            )
            for i in range(2):
                for j in range(2):
                    key = (pa * 2 + i, pb * 2 + j)
                    if key in where:
                        put(key, prod[i * BLK:(i + 1) * BLK, j * BLK:(j + 1) * BLK])
    loads[3].wait()
    proj = jnp.dot(grad_ref[...], jac[:, 0:512], preferred_element_type=jnp.float32)
    proj = jnp.sum(
        jnp.where(lax.broadcasted_iota(jnp.int32, proj.shape, 0) == c, proj, 0.0),
        axis=0, keepdims=True,
    )
    put("proj", jnp.zeros((BLK, BLK), jnp.float32))
    put(None, jnp.zeros((BLK, BLK), jnp.float32))
    k, upper, _ = where["proj"]
    for i in range(4):
        parts[k, upper, i:i + 1, :] = proj[:, i * BLK:(i + 1) * BLK]

    cp = remote(
        parts.at[1 - core], from_core, core_sems.at[0], core_sems.at[1], dev_c(x * 2 + 1 - core)
    )
    cp.start()
    sent.append(cp)
    cp.wait_recv()
    half[...] = parts[core] + from_core[...]

    def xa_copy(xx, d, peer):
        span = COUNT_X[xx]
        return remote(
            half.at[pl.ds(FIRST_X[xx], span)], from_x.at[d, pl.ds(0, span)],
            xa_send.at[d], xa_recv.at[d], dev_x(peer),
        )

    def yb_copy(yy, d, peer):
        span = COUNT_Y[yy]
        return remote(
            half.at[pl.ds(HALF + FIRST_Y[yy], span)], from_y.at[d, pl.ds(0, span)],
            yb_send.at[d], yb_recv.at[d], dev_y(peer),
        )

    for q in range(4):
        @pl.when(x != q)
        def _():
            xa_copy(q, (q + NX - x) % NX, q).start()

        @pl.when(y != q)
        def _():
            yb_copy(q, (q + NY - y) % NY, q).start()

    for q in range(4):
        @pl.when(x == q)
        def _():
            span = COUNT_X[q]
            total = half[FIRST_X[q]:FIRST_X[q] + span]
            for d in (1, 3, 2):
                xa_copy(q, d, (q + NX - d) % NX).wait_recv()
                total = total + from_x[d, 0:span]
            sum_a[0:span] = total

    for q in range(4):
        @pl.when(y == q)
        def _():
            span = COUNT_Y[q]
            total = half[HALF + FIRST_Y[q]:HALF + FIRST_Y[q] + span]
            for d in (1, 3, 2):
                yb_copy(q, d, (q + NY - d) % NY).wait_recv()
                total = total + from_y[d, 0:span]
            sum_b[0:span] = total

    skip = jnp.where(y == 3, 2, 0)
    holds = jnp.logical_or(x >= 2, y < 3)

    def ya_copy(d, yy, peer):
        return remote(sum_a.at[yy], from_y2.at[d], ya_send.at[d], ya_recv.at[d], dev_y(peer))

    def xb_copy(d, spot, peer):
        return remote(sum_b.at[spot], from_x2.at[d], xb_send.at[d], xb_recv.at[d], dev_x(peer))

    for d in range(1, 4):
        yy = (y + d) % NY
        xx = (x + d) % NX

        @pl.when(jnp.logical_or(x >= 2, yy < 3))
        def _():
            ya_copy(d, yy, yy).start()

        @pl.when(jnp.logical_or(xx >= 2, y < 3))
        def _():
            xb_copy(d, xx - skip, xx).start()

    def zl_copy(d, spot, peer):
        return remote(
            block.at[pl.ds(spot * 32, 32)], from_zl.at[d],
            zl_send.at[d], zl_recv.at[d], dev_z(zh, peer),
        )

    def zh_copy(d, spot, peer):
        return remote(
            from_zh.at[spot], from_zh.at[spot], zh_send.at[d], zh_recv.at[d], dev_z(peer, zl)
        )

    def zg_copy(d, spot, peer):
        return remote(
            line.at[pl.ds(spot * 32, 32)], line.at[pl.ds(spot * 32, 32)],
            zg_send.at[d], zg_recv.at[d], dev_z(zh, peer),
        )

    def gy_own(d, spot, peer):
        return remote(line, own_ref.at[spot], gy_send.at[d], gy_recv.at[d], dev_y(peer))

    def gy_head(d, spot, peer):
        return remote(
            line.at[pl.ds(0, ROWS)], out_a.at[core, x, spot],
            gy_send.at[d], gy_recv.at[d], dev_y(peer),
        )

    def gx_head(d, spot, peer):
        return remote(
            line.at[pl.ds(ROWS, ROWS)], out_b.at[core, y, spot],
            gx_send.at[d], gx_recv.at[d], dev_x(peer),
        )

    @pl.when(holds)
    def _():
        upper = sum_a[y]
        lower = sum_b[x - skip]
        for d in (1, 3, 2):
            ya_copy(d, 0, (y + NY - d) % NY).wait_recv()
            upper = upper + from_y2[d]
        for d in (1, 3, 2):
            xb_copy(d, 0, (x + NX - d) % NX).wait_recv()
            lower = lower + from_x2[d]
        block[0:ROWS] = upper
        block[ROWS:BLK] = lower
        for d in range(1, 4):
            lo = (zl + d) % 4
            zl_copy(d, lo, lo).start()
        total = block[pl.ds(pl.multiple_of(zl * 32, 32), 32)]
        for d in range(1, 4):
            zl_copy(d, 0, (zl + 4 - d) % 4).wait_recv()
            total = total + from_zl[d]
        from_zh[zh] = total
        for d in range(1, hops):
            zh_copy(d, zh, (zh + d) % hops).start()
        for d in range(1, hops):
            src = (zh + hops - d) % hops
            zh_copy(d, src, src).wait_recv()
        total = from_zh[0]
        for i in range(1, hops):
            total = total + from_zh[i]
        line[pl.ds(pl.multiple_of(zl * 32, 32), 32)] = total
        for d in range(1, 4):
            zg_copy(d, zl, (zl + d) % 4).start()
        for d in range(1, 4):
            src = (zl + 4 - d) % 4
            zg_copy(d, src, src).wait_recv()

        @pl.when(x >= 2)
        def _():
            for d in range(1, 4):
                gy_own(d, y, (y + d) % NY).start()
            own_ref[y] = line[...]

        @pl.when(x < 2)
        def _():
            for d in range(1, 4):
                gy_head(d, y, (y + d) % NY).start()
                gx_head(d, x, (x + d) % NX).start()
            out_a[core, x, y] = line[0:ROWS]
            out_b[core, y, x] = line[ROWS:BLK]

    def hx_copy(d, xx, peer):
        return remote(
            out_a.at[core, xx], out_a.at[core, xx], hx_send.at[d], hx_recv.at[d], dev_x(peer)
        )

    def hy_copy(d, yy, peer):
        return remote(
            out_b.at[core, yy], out_b.at[core, yy], hy_send.at[d], hy_recv.at[d], dev_y(peer)
        )

    @pl.when(x < 2)
    def _():
        for d in range(1, 4):
            src = (y + NY - d) % NY

            @pl.when(src < 3)
            def _():
                gy_head(d, src, src).wait_recv()

        for d in range(1, 4):
            hx_copy(d, x, (x + d) % NX).start()
        own_ref[...] = jnp.zeros_like(own_ref)

    @pl.when(y < 3)
    def _():
        for d in range(1, 4):
            src = (x + NX - d) % NX

            @pl.when(src < 2)
            def _():
                gx_head(d, src, src).wait_recv()

        for d in range(1, 4):
            hy_copy(d, y, (y + d) % NY).start()

    def swap_a(half_core):
        return remote(
            out_a.at[half_core], out_a.at[half_core], cg_send.at[0], cg_recv.at[0],
            dev_c(x * 2 + 1 - core),
        )

    def swap_b(half_core):
        return remote(
            out_b.at[half_core], out_b.at[half_core], cg_send.at[1], cg_recv.at[1],
            dev_c(x * 2 + 1 - core),
        )

    for d in range(1, 4):
        src = (y + NY - d) % NY

        @pl.when(src < 3)
        def _():
            hy_copy(d, src, src).wait_recv()

    swap_b(core).start()
    for d in range(1, 4):
        src = (x + NX - d) % NX

        @pl.when(src < 2)
        def _():
            hx_copy(d, src, src).wait_recv()

    swap_a(core).start()

    @pl.when(x >= 2)
    def _():
        for d in range(1, 4):
            src = (y + NY - d) % NY
            gy_own(d, src, src).wait_recv()

    swap_b(1 - core).wait_recv()
    swap_a(1 - core).wait_recv()

    for cp in sent:
        cp.wait_send()
    for q in range(4):
        @pl.when(x != q)
        def _():
            xa_copy(q, (q + NX - x) % NX, q).wait_send()

        @pl.when(y != q)
        def _():
            yb_copy(q, (q + NY - y) % NY, q).wait_send()

    for d in range(1, 4):
        yy = (y + d) % NY
        xx = (x + d) % NX

        @pl.when(jnp.logical_or(x >= 2, yy < 3))
        def _():
            ya_copy(d, yy, yy).wait_send()

        @pl.when(jnp.logical_or(xx >= 2, y < 3))
        def _():
            xb_copy(d, xx - skip, xx).wait_send()

    @pl.when(holds)
    def _():
        for d in range(1, 4):
            lo = (zl + d) % 4
            zl_copy(d, lo, lo).wait_send()
            zg_copy(d, zl, lo).wait_send()
        for d in range(1, hops):
            zh_copy(d, zh, (zh + d) % hops).wait_send()

        @pl.when(x >= 2)
        def _():
            for d in range(1, 4):
                gy_own(d, y, (y + d) % NY).wait_send()

        @pl.when(x < 2)
        def _():
            for d in range(1, 4):
                gy_head(d, y, (y + d) % NY).wait_send()
                gx_head(d, x, (x + d) % NX).wait_send()

    @pl.when(x < 2)
    def _():
        for d in range(1, 4):
            hx_copy(d, x, (x + d) % NX).wait_send()

    @pl.when(y < 3)
    def _():
        for d in range(1, 4):
            hy_copy(d, y, (y + d) % NY).wait_send()

    swap_b(core).wait_send()
    swap_a(core).wait_send()


def gram_everywhere(n_rows, base, field, grad, tile, kind):
    cells = field.shape[1]
    hops = n_rows // NY // 4
    f32 = jnp.float32
    vmem = pl.BlockSpec(memory_space=pltpu.VMEM)
    hbm = pl.BlockSpec(memory_space=pltpu.HBM)
    pairs = [pltpu.SemaphoreType.DMA((4,))] * 2
    halves = lambda *lead: pltpu.VMEM(lead + (ROWS, BLK), f32)
    strip = lambda dtype: pltpu.VMEM((8, cells), dtype)
    return pl.pallas_call(
        functools.partial(gram_kernel, n_rows),
        out_shape=(
            jax.ShapeDtypeStruct((2, 2, 3, ROWS, BLK), f32),
            jax.ShapeDtypeStruct((2, 3, 2, ROWS, BLK), f32),
            jax.ShapeDtypeStruct((4, BLK, BLK), f32),
        ),
        in_specs=[hbm] * 5,
        out_specs=(vmem, vmem, vmem),
        scratch_shapes=[
            pltpu.VMEM((8, cells, BLK), jnp.bfloat16),
            pltpu.VMEM((cells, 8 * BLK), jnp.bfloat16),
            strip(f32), strip(jnp.bfloat16),
            pltpu.VMEM((1, BLK), jnp.int32), pltpu.VMEM((1, BLK), jnp.int32),
            pltpu.VMEM((8, BLK), jnp.int32), pltpu.VMEM((8, 8, BLK), jnp.int32),
            strip(f32), strip(f32),
            halves(2, 2 * HALF), halves(2 * HALF), halves(2 * HALF),
            halves(4, 4), halves(4, 4), halves(4), halves(4), halves(4), halves(4),
            pltpu.VMEM((BLK, BLK), f32), pltpu.VMEM((4, 32, BLK), f32),
            pltpu.VMEM((hops, 32, BLK), f32), pltpu.VMEM((BLK, BLK), f32),
            pltpu.SemaphoreType.DMA((4,)),
            *[pltpu.SemaphoreType.DMA((8,))] * 4,
            pltpu.SemaphoreType.DMA((2,)), pltpu.SemaphoreType.DMA((2,)),
            pltpu.SemaphoreType.DMA((2,)),
            *pairs * 4, *pairs, *pairs, *pairs, *pairs * 4,
            pltpu.SemaphoreType.DMA((2,)), pltpu.SemaphoreType.DMA((2,)),
        ],
        compiler_params=pltpu.CompilerParams(
            collective_id=0, has_side_effects=True, vmem_limit_bytes=48 << 20
        ),
        name="gram",
    )(*[pltpu.with_memory_space_constraint(v, pltpu.HBM) for v in (base, field, grad, tile, kind)])


def dot_f32(left, right, dims=((1,), (0,))):
    return lax.dot_general(
        left, right, (dims, ((), ())), precision=HIGHEST, preferred_element_type=jnp.float32
    )


def across(vec, col):
    return jnp.broadcast_to(vec[:, col:col + 1], (8, BLK))


def along(vec, row):
    return jnp.broadcast_to(vec[row:row + 1, :], (8, BLK))


def split_3(x):
    high = x.astype(jnp.bfloat16)
    rest = x - high.astype(jnp.float32)
    mid = rest.astype(jnp.bfloat16)
    return high, mid, (rest - mid.astype(jnp.float32)).astype(jnp.bfloat16)


def outer(left, right):
    lh, lm, ll = split_3(left)
    rh, rm, rl = split_3(right)
    return lax.dot_general(
        jnp.concatenate([lh, lh, lm, lm, lh, ll], axis=0),
        jnp.concatenate([rh, rm, rh, rm, rl, rh], axis=0),
        (((0,), (0,)), ((), ())), preferred_element_type=jnp.float32,
    )


def factor_block(work, scaled):
    rows = lax.broadcasted_iota(jnp.int32, (8, BLK), 0)
    tall = 64
    for q in range(BLK // tall):
        at = [tall * q + 8 * s for s in range(tall // 8)]
        xa = [work[a:a + 8, 0:BLK] for a in at]
        xe = [work[a:a + 8, BLK:2 * BLK] for a in at]
        for s in range(len(at)):
            cols = [across(xa[s], at[s] + t) for t in range(8)]
            below = {n: [across(xa[n], at[s] + t) for t in range(8)]
                     for n in range(s + 1, len(at))}
            pivots = None
            for t in range(8):
                entry = {u: along(cols[t], u) for u in range(t, 8)}
                pivots = entry[t] if pivots is None else jnp.where(rows >= t, entry[t], pivots)
                recip = 1.0 / entry[t]
                row_a, row_e = along(xa[s], t), along(xe[s], t)
                if t < 7:
                    mult = cols[t] * recip
                    for u in range(t + 1, 8):
                        cols[u] = cols[u] - mult * entry[u]
                    mult = jnp.where(rows > t, mult, 0.0)
                    xa[s] = xa[s] - mult * row_a
                    xe[s] = xe[s] - mult * row_e
                for n in below:
                    mult = below[n][t] * recip
                    for u in range(t + 1, 8):
                        below[n][u] = below[n][u] - mult * entry[u]
                    xa[n] = xa[n] - mult * row_a
                    xe[n] = xe[n] - mult * row_e
            scale = 1.0 / jnp.sqrt(pivots)
            scaled[at[s]:at[s] + 8, 0:BLK] = xa[s] * scale
            scaled[at[s]:at[s] + 8, BLK:2 * BLK] = xe[s] * scale
        low = tall * (q + 1)
        if low < BLK:
            done = scaled[tall * q:low, :]
            work[low:BLK, :] = work[low:BLK, :] - outer(done[:, low:BLK], done)


def factor_kernel(head_a, head_b, own_ref, r_ref, m_ref, mat, head_ref, work, scaled, inv):
    c = lax.axis_index("cols")
    eye = (
        lax.broadcasted_iota(jnp.int32, (BLK, BLK), 0)
        == lax.broadcasted_iota(jnp.int32, (BLK, BLK), 1)
    ).astype(jnp.float32)
    for spot in range(12):
        k, at_x, at_y = spot // 6, spot // 3 % 2, spot % 3
        head_ref[spot, 0:ROWS] = head_a[k, at_x, at_y]
        head_ref[spot, ROWS:BLK] = head_b[k, at_y, at_x]
    near = jnp.minimum(c, 3)
    for k in range(4):
        for j in range(k, 4):
            mat[k, :, j * BLK:(j + 1) * BLK] = head_ref[HEAD.index((k, j))]
        low, high = jnp.minimum(near, k), jnp.maximum(near, k)
        found = head_ref[low * 4 - low * (low - 1) // 2 + high - low]
        found = jnp.where(k <= near, found, found.T)
        mat[k, :, 512:640] = jnp.where(c >= 4, own_ref[k], found)
        mat[k, :, 640:768] = jnp.broadcast_to(head_ref[len(HEAD), k:k + 1, :], (BLK, BLK)).T
    for k in range(4):
        work[:, 0:BLK] = mat[k, :, k * BLK:(k + 1) * BLK]
        work[:, BLK:2 * BLK] = eye
        factor_block(work, scaled)
        low = (k + 1) * BLK
        inverse = scaled[:, BLK:2 * BLK]
        inv[k] = inverse
        if k == 3:
            mat[k, :, low:768] = dot_f32(inverse, mat[k, :, low:768])
            r_ref[k * BLK:(k + 1) * BLK, :] = mat[k, :, 512:640]
            continue
        near_cols = dot_f32(inverse, mat[k, :, low:low + BLK])
        mat[k, :, low:low + BLK] = near_cols
        mat[k + 1, :, low:low + BLK] = mat[k + 1, :, low:low + BLK] - dot_f32(
            near_cols, near_cols, ((0,), (0,))
        )
        far = low + BLK
        mat[k, :, far:768] = dot_f32(inverse, mat[k, :, far:768])
        r_ref[k * BLK:(k + 1) * BLK, :] = mat[k, :, 512:640]
        mat[k + 1, :, far:768] = mat[k + 1, :, far:768] - dot_f32(
            near_cols, mat[k, :, far:768], ((0,), (0,))
        )
        for i in range(k + 2, 4):
            mat[i, :, i * BLK:768] = mat[i, :, i * BLK:768] - dot_f32(
                mat[k, :, i * BLK:(i + 1) * BLK], mat[k, :, i * BLK:768], ((0,), (0,))
            )
    rest = [mat[k, :, 640:768] for k in range(4)]
    for k in (3, 2, 1, 0):
        solved = dot_f32(inv[k], rest[k], ((0,), (0,)))
        for i in range(k):
            rest[i] = rest[i] - dot_f32(mat[i, :, k * BLK:(k + 1) * BLK], solved)
        m_ref[k:k + 1, :] = solved.T[0:1, :]


def factor_and_solve(head_a, head_b, own):
    f32 = jnp.float32
    vmem = pl.BlockSpec(memory_space=pltpu.VMEM)
    return pl.pallas_call(
        factor_kernel,
        out_shape=(
            jax.ShapeDtypeStruct((512, BLK), f32),
            jax.ShapeDtypeStruct((4, BLK), f32),
        ),
        in_specs=[vmem, vmem, vmem],
        out_specs=(vmem, vmem),
        scratch_shapes=[
            pltpu.VMEM((4, BLK, 768), f32),
            pltpu.VMEM((12, BLK, BLK), f32),
            pltpu.VMEM((BLK, 2 * BLK), f32),
            pltpu.VMEM((BLK, 2 * BLK), f32),
            pltpu.VMEM((4, BLK, BLK), f32),
        ],
        compiler_params=pltpu.CompilerParams(vmem_limit_bytes=48 << 20),
        name="factor",
    )(head_a, head_b, own)


def shards(n_rows, sens_base, design_field, gradient, tile_index, type_codes):
    head_a, head_b, own = gram_everywhere(
        n_rows, sens_base, design_field, gradient,
        tile_index.reshape(1, BLK), type_codes.reshape(1, BLK),
    )
    r_panels, multipliers = factor_and_solve(head_a, head_b, own)
    return r_panels, multipliers.reshape(-1)


def solution(mesh):
    placed = (P("rows", "cols"), P("rows", None), P("rows", None), P("cols"), P("cols"))
    return jax.shard_map(
        functools.partial(shards, mesh.shape["rows"]),
        mesh=mesh, in_specs=placed, out_specs=(P(None, "cols"), P()), check_vma=False,
    )
```

```python
import functools

import jax
import jax.numpy as jnp
from jax import lax
from jax.experimental import pallas as pl
from jax.experimental.pallas import tpu as pltpu
from jax.sharding import PartitionSpec as P

TILE = 128
BLK = 128
NX = 4
NY = 4
MESH = pl.DeviceIdType.MESH
HIGHEST = lax.Precision.HIGHEST
HEAD = [(a, b) for a in range(4) for b in range(a, 4)]
COUNT_X = (3, 3, 4, 4)
FIRST_X = (0, 3, 6, 10)
COUNT_Y = (4, 4, 4, 2)
FIRST_Y = (0, 4, 8, 12)
HALF = 14
ROWS = BLK // 2


def slot_of(core, x, y):
    if x < 2:
        spot = (core * 2 + x) * 3 + y
        if spot < len(HEAD):
            return HEAD[spot]
        return "proj" if spot == len(HEAD) else None
    return (y, x * 2 + core)


def gram_kernel(
    n_rows,
    base_ref, field_hbm, grad_hbm, tile_hbm, type_hbm,
    out_a, out_b, own_ref,
    raw, jac, field_ref, grad_ref, tile_ref, type_ref, codes_mine, codes, north, south,
    parts, from_core, half, from_x, from_y, sum_a, sum_b, from_x2, from_y2,
    block, from_zl, from_zh, line,
    load_sems, a2a_send, a2a_recv, code_send, code_recv, halo_send, halo_recv, core_sems,
    xa_send, xa_recv, yb_send, yb_recv, ya_send, ya_recv, xb_send, xb_recv,
    zl_send, zl_recv, zh_send, zh_recv, zg_send, zg_recv,
    gy_send, gy_recv, gx_send, gx_recv, hx_send, hx_recv, hy_send, hy_recv,
    cg_send, cg_recv,
):
    r = lax.axis_index("rows")
    c = lax.axis_index("cols")
    z, y = r // NY, r % NY
    zh, zl = z // 4, z % 4
    hops = n_rows // NY // 4
    x, core = c // 2, c % 2
    up, down = (r + n_rows - 1) % n_rows, (r + 1) % n_rows
    cells = raw.shape[1]

    def dev_c(col):
        return (r, col)

    def dev_x(xx):
        return (r, xx * 2 + core)

    def dev_y(yy):
        return (z * NY + yy, c)

    def dev_z(hi, lo):
        return ((hi * 4 + lo) * NY + y, c)

    def remote(src, dst, send, recv, device):
        return pltpu.make_async_remote_copy(
            src_ref=src, dst_ref=dst, send_sem=send, recv_sem=recv,
            device_id=device, device_id_type=MESH,
        )

    barrier = pltpu.get_barrier_semaphore()

    def greet(device):
        pl.semaphore_signal(barrier, inc=1, device_id=device, device_id_type=MESH)

    for d in range(1, hops):
        greet(dev_z((zh + d) % hops, zl))
    for d in range(1, 8):
        greet(dev_c((c + d) % 8))
    for d in range(1, NY):
        greet(dev_y((y + d) % NY))
    for d in range(1, 4):
        greet(dev_z(zh, (zl + d) % 4))
    greet((up, c))
    greet((down, c))
    loads = []
    for i, (src, dst) in enumerate((
        (field_hbm, field_ref), (tile_hbm, tile_ref), (type_hbm, type_ref), (grad_hbm, grad_ref),
    )):
        loads.append(pltpu.make_async_copy(src, dst, load_sems.at[i]))
        loads[-1].start()
    codes_mine[...] = jnp.zeros_like(codes_mine)
    loads[1].wait()
    loads[2].wait()
    codes_mine[0:1, :] = tile_ref[...]
    codes_mine[1:2, :] = type_ref[...]
    loads[0].wait()
    pl.semaphore_wait(barrier, 7 + (NY - 1) + 3 + (hops - 1) + 2)

    sent = []
    for d in range(1, 8):
        to = (c + d) % 8
        cp = remote(codes_mine, codes.at[c], code_send.at[d], code_recv.at[d], dev_c(to))
        cp.start()
        sent.append(cp)
    cp = remote(field_ref, north, halo_send.at[0], halo_recv.at[0], (down, c))
    cp.start()
    sent.append(cp)
    cp = remote(field_ref, south, halo_send.at[1], halo_recv.at[1], (up, c))
    cp.start()
    sent.append(cp)
    for d in (4, 3, 5, 2, 6, 1, 7):
        to = (c + d) % 8
        cp = remote(
            base_ref.at[pl.ds(to * cells, cells), :], raw.at[c],
            a2a_send.at[d], a2a_recv.at[d], dev_c(to),
        )
        cp.start()
        sent.append(cp)
    mine = pltpu.make_async_copy(
        base_ref.at[pl.ds(c * cells, cells), :], raw.at[c], a2a_recv.at[0]
    )
    mine.start()
    codes[c] = codes_mine[...]

    remote(field_ref, north, halo_send.at[0], halo_recv.at[0], (up, c)).wait_recv()
    remote(field_ref, south, halo_send.at[1], halo_recv.at[1], (down, c)).wait_recv()
    here = field_ref[pl.ds(c, 1), :]
    above = field_ref[pl.ds((c + 7) % 8, 1), :]
    below = field_ref[pl.ds((c + 1) % 8, 1), :]
    above = jnp.where(c == 0, jnp.where(r == 0, 0.0, north[7:8, :]), above)
    below = jnp.where(c == 7, jnp.where(r == n_rows - 1, 0.0, south[0:1, :]), below)
    wide = (8, cells)
    here = jnp.broadcast_to(here, wide)
    above = jnp.broadcast_to(above, wide)
    below = jnp.broadcast_to(below, wide)
    lane = lax.broadcasted_iota(jnp.int32, wide, 1)
    west = jnp.where(lane == 0, 0.0, pltpu.roll(here, 1, 1))
    east = jnp.where(lane == cells - 1, 0.0, pltpu.roll(here, cells - 1, 1))
    laplace = 4.0 * here - (above + below + west + east)
    slope_x = 0.5 * (east - west)
    slope_y = 0.5 * (below - above)
    srow = lax.broadcasted_iota(jnp.int32, wide, 0)
    terms = []
    for fieldval in (laplace, slope_x, slope_y):
        rest = fieldval / TILE
        for _ in range(3):
            term = rest.astype(jnp.bfloat16).astype(jnp.float32)
            terms.append(term)
            rest = rest - term
    low = jnp.zeros(wide, jnp.float32)
    for k in range(8):
        low = jnp.where(srow == k, terms[(k % 3) * 3 + k // 3], low)
    high = jnp.where(srow == 0, terms[2 * 3 + 2], 0.0)
    both = jnp.concatenate([low, high], axis=0)
    tiles = cells // TILE
    spread = jnp.concatenate([both] * tiles, axis=0)
    krow = lax.broadcasted_iota(jnp.int32, spread.shape, 0)
    kcol = lax.broadcasted_iota(jnp.int32, spread.shape, 1)
    spread = jnp.where(krow // 16 == kcol // TILE, spread, 0.0)
    spread_t = spread.T.astype(jnp.bfloat16)

    first_tile = (r * 8 // TILE) * tiles
    rows16 = lax.broadcasted_iota(jnp.int32, (16 * tiles, BLK), 0)
    term_id = rows16 % 16
    kind_of = jnp.where(term_id < 9, term_id % 3, 3)
    tile_of = first_tile + rows16 // 16
    for d in range(1, 8):
        src = (c + 8 - d) % 8
        remote(codes_mine, codes.at[src], code_send.at[d], code_recv.at[d], dev_c(src)).wait_recv()

    for cs in range(8):
        @pl.when(c == cs)
        def _():
            mine.wait()

        @pl.when(c != cs)
        def _():
            d = (c + 8 - cs) % 8
            remote(
                base_ref.at[pl.ds(0, cells), :], raw.at[cs],
                a2a_send.at[d], a2a_recv.at[d], dev_c(cs),
            ).wait_recv()

        chosen = jnp.logical_and(
            kind_of == codes[cs, 1:2, :], tile_of == codes[cs, 0:1, :]
        ).astype(jnp.float32).astype(jnp.bfloat16)
        added = jnp.dot(spread_t, chosen, preferred_element_type=jnp.float32)
        jac[:, cs * BLK:(cs + 1) * BLK] = (raw[cs].astype(jnp.float32) + added).astype(jnp.bfloat16)

    where = {}
    for k in range(2):
        for xx in range(NX):
            for yy in range(COUNT_X[xx]):
                low = FIRST_Y[yy] + (xx if yy < 3 else xx - 2)
                where[slot_of(k, xx, yy)] = (k, FIRST_X[xx] + yy, HALF + low)

    def put(key, value):
        k, upper, lower = where[key]
        parts[k, upper] = value[0:ROWS]
        parts[k, lower] = value[ROWS:BLK]

    contract = (((0,), (0,)), ((), ()))
    for pa in range(2):
        left = jac[:, pa * 256:(pa + 1) * 256]
        for pb in range(pa, 4):
            prod = lax.dot_general(
                left, jac[:, pb * 256:(pb + 1) * 256], contract,
                preferred_element_type=jnp.float32,
            )
            for i in range(2):
                for j in range(2):
                    key = (pa * 2 + i, pb * 2 + j)
                    if key in where:
                        put(key, prod[i * BLK:(i + 1) * BLK, j * BLK:(j + 1) * BLK])
    loads[3].wait()
    proj = jnp.dot(grad_ref[...], jac[:, 0:512], preferred_element_type=jnp.float32)
    proj = jnp.sum(
        jnp.where(lax.broadcasted_iota(jnp.int32, proj.shape, 0) == c, proj, 0.0),
        axis=0, keepdims=True,
    )
    put("proj", jnp.zeros((BLK, BLK), jnp.float32))
    put(None, jnp.zeros((BLK, BLK), jnp.float32))
    k, upper, _ = where["proj"]
    for i in range(4):
        parts[k, upper, i:i + 1, :] = proj[:, i * BLK:(i + 1) * BLK]

    cp = remote(
        parts.at[1 - core], from_core, core_sems.at[0], core_sems.at[1], dev_c(x * 2 + 1 - core)
    )
    cp.start()
    sent.append(cp)
    cp.wait_recv()
    half[...] = parts[core] + from_core[...]

    def xa_copy(xx, d, peer):
        span = COUNT_X[xx]
        return remote(
            half.at[pl.ds(FIRST_X[xx], span)], from_x.at[d, pl.ds(0, span)],
            xa_send.at[d], xa_recv.at[d], dev_x(peer),
        )

    def yb_copy(yy, d, peer):
        span = COUNT_Y[yy]
        return remote(
            half.at[pl.ds(HALF + FIRST_Y[yy], span)], from_y.at[d, pl.ds(0, span)],
            yb_send.at[d], yb_recv.at[d], dev_y(peer),
        )

    for q in range(4):
        @pl.when(x != q)
        def _():
            xa_copy(q, (q + NX - x) % NX, q).start()

        @pl.when(y != q)
        def _():
            yb_copy(q, (q + NY - y) % NY, q).start()

    for q in range(4):
        @pl.when(x == q)
        def _():
            span = COUNT_X[q]
            total = half[FIRST_X[q]:FIRST_X[q] + span]
            for d in (1, 3, 2):
                xa_copy(q, d, (q + NX - d) % NX).wait_recv()
                total = total + from_x[d, 0:span]
            sum_a[0:span] = total

    for q in range(4):
        @pl.when(y == q)
        def _():
            span = COUNT_Y[q]
            total = half[HALF + FIRST_Y[q]:HALF + FIRST_Y[q] + span]
            for d in (1, 3, 2):
                yb_copy(q, d, (q + NY - d) % NY).wait_recv()
                total = total + from_y[d, 0:span]
            sum_b[0:span] = total

    skip = jnp.where(y == 3, 2, 0)
    holds = jnp.logical_or(x >= 2, y < 3)

    def ya_copy(d, yy, peer):
        return remote(sum_a.at[yy], from_y2.at[d], ya_send.at[d], ya_recv.at[d], dev_y(peer))

    def xb_copy(d, spot, peer):
        return remote(sum_b.at[spot], from_x2.at[d], xb_send.at[d], xb_recv.at[d], dev_x(peer))

    for d in range(1, 4):
        yy = (y + d) % NY
        xx = (x + d) % NX

        @pl.when(jnp.logical_or(x >= 2, yy < 3))
        def _():
            ya_copy(d, yy, yy).start()

        @pl.when(jnp.logical_or(xx >= 2, y < 3))
        def _():
            xb_copy(d, xx - skip, xx).start()

    def zl_copy(d, spot, peer):
        return remote(
            block.at[pl.ds(spot * 32, 32)], from_zl.at[d],
            zl_send.at[d], zl_recv.at[d], dev_z(zh, peer),
        )

    def zh_copy(d, spot, peer):
        return remote(
            from_zh.at[spot], from_zh.at[spot], zh_send.at[d], zh_recv.at[d], dev_z(peer, zl)
        )

    def zg_copy(d, spot, peer):
        return remote(
            line.at[pl.ds(spot * 32, 32)], line.at[pl.ds(spot * 32, 32)],
            zg_send.at[d], zg_recv.at[d], dev_z(zh, peer),
        )

    def gy_own(d, spot, peer):
        return remote(line, own_ref.at[spot], gy_send.at[d], gy_recv.at[d], dev_y(peer))

    def gy_head(d, spot, peer):
        return remote(
            line.at[pl.ds(0, ROWS)], out_a.at[core, x, spot],
            gy_send.at[d], gy_recv.at[d], dev_y(peer),
        )

    def gx_head(d, spot, peer):
        return remote(
            line.at[pl.ds(ROWS, ROWS)], out_b.at[core, y, spot],
            gx_send.at[d], gx_recv.at[d], dev_x(peer),
        )

    @pl.when(holds)
    def _():
        upper = sum_a[y]
        lower = sum_b[x - skip]
        for d in (1, 3, 2):
            ya_copy(d, 0, (y + NY - d) % NY).wait_recv()
            upper = upper + from_y2[d]
        for d in (1, 3, 2):
            xb_copy(d, 0, (x + NX - d) % NX).wait_recv()
            lower = lower + from_x2[d]
        block[0:ROWS] = upper
        block[ROWS:BLK] = lower
        for d in range(1, 4):
            lo = (zl + d) % 4
            zl_copy(d, lo, lo).start()
        total = block[pl.ds(pl.multiple_of(zl * 32, 32), 32)]
        for d in range(1, 4):
            zl_copy(d, 0, (zl + 4 - d) % 4).wait_recv()
            total = total + from_zl[d]
        from_zh[zh] = total
        for d in range(1, hops):
            zh_copy(d, zh, (zh + d) % hops).start()
        for d in range(1, hops):
            src = (zh + hops - d) % hops
            zh_copy(d, src, src).wait_recv()
        total = from_zh[0]
        for i in range(1, hops):
            total = total + from_zh[i]
        line[pl.ds(pl.multiple_of(zl * 32, 32), 32)] = total
        for d in range(1, 4):
            zg_copy(d, zl, (zl + d) % 4).start()
        for d in range(1, 4):
            src = (zl + 4 - d) % 4
            zg_copy(d, src, src).wait_recv()

        @pl.when(x >= 2)
        def _():
            for d in range(1, 4):
                gy_own(d, y, (y + d) % NY).start()
            own_ref[y] = line[...]

        @pl.when(x < 2)
        def _():
            for d in range(1, 4):
                gy_head(d, y, (y + d) % NY).start()
                gx_head(d, x, (x + d) % NX).start()
            out_a[core, x, y] = line[0:ROWS]
            out_b[core, y, x] = line[ROWS:BLK]

    def hx_copy(d, xx, peer):
        return remote(
            out_a.at[core, xx], out_a.at[core, xx], hx_send.at[d], hx_recv.at[d], dev_x(peer)
        )

    def hy_copy(d, yy, peer):
        return remote(
            out_b.at[core, yy], out_b.at[core, yy], hy_send.at[d], hy_recv.at[d], dev_y(peer)
        )

    @pl.when(x < 2)
    def _():
        for d in range(1, 4):
            src = (y + NY - d) % NY

            @pl.when(src < 3)
            def _():
                gy_head(d, src, src).wait_recv()

        for d in range(1, 4):
            hx_copy(d, x, (x + d) % NX).start()
        own_ref[...] = jnp.zeros_like(own_ref)

    @pl.when(y < 3)
    def _():
        for d in range(1, 4):
            src = (x + NX - d) % NX

            @pl.when(src < 2)
            def _():
                gx_head(d, src, src).wait_recv()

        for d in range(1, 4):
            hy_copy(d, y, (y + d) % NY).start()

    def swap_a(half_core):
        return remote(
            out_a.at[half_core], out_a.at[half_core], cg_send.at[0], cg_recv.at[0],
            dev_c(x * 2 + 1 - core),
        )

    def swap_b(half_core):
        return remote(
            out_b.at[half_core], out_b.at[half_core], cg_send.at[1], cg_recv.at[1],
            dev_c(x * 2 + 1 - core),
        )

    for d in range(1, 4):
        src = (y + NY - d) % NY

        @pl.when(src < 3)
        def _():
            hy_copy(d, src, src).wait_recv()

    swap_b(core).start()
    for d in range(1, 4):
        src = (x + NX - d) % NX

        @pl.when(src < 2)
        def _():
            hx_copy(d, src, src).wait_recv()

    swap_a(core).start()

    @pl.when(x >= 2)
    def _():
        for d in range(1, 4):
            src = (y + NY - d) % NY
            gy_own(d, src, src).wait_recv()

    swap_b(1 - core).wait_recv()
    swap_a(1 - core).wait_recv()

    for cp in sent:
        cp.wait_send()
    for q in range(4):
        @pl.when(x != q)
        def _():
            xa_copy(q, (q + NX - x) % NX, q).wait_send()

        @pl.when(y != q)
        def _():
            yb_copy(q, (q + NY - y) % NY, q).wait_send()

    for d in range(1, 4):
        yy = (y + d) % NY
        xx = (x + d) % NX

        @pl.when(jnp.logical_or(x >= 2, yy < 3))
        def _():
            ya_copy(d, yy, yy).wait_send()

        @pl.when(jnp.logical_or(xx >= 2, y < 3))
        def _():
            xb_copy(d, xx - skip, xx).wait_send()

    @pl.when(holds)
    def _():
        for d in range(1, 4):
            lo = (zl + d) % 4
            zl_copy(d, lo, lo).wait_send()
            zg_copy(d, zl, lo).wait_send()
        for d in range(1, hops):
            zh_copy(d, zh, (zh + d) % hops).wait_send()

        @pl.when(x >= 2)
        def _():
            for d in range(1, 4):
                gy_own(d, y, (y + d) % NY).wait_send()

        @pl.when(x < 2)
        def _():
            for d in range(1, 4):
                gy_head(d, y, (y + d) % NY).wait_send()
                gx_head(d, x, (x + d) % NX).wait_send()

    @pl.when(x < 2)
    def _():
        for d in range(1, 4):
            hx_copy(d, x, (x + d) % NX).wait_send()

    @pl.when(y < 3)
    def _():
        for d in range(1, 4):
            hy_copy(d, y, (y + d) % NY).wait_send()

    swap_b(core).wait_send()
    swap_a(core).wait_send()


def gram_everywhere(n_rows, base, field, grad, tile, kind):
    cells = field.shape[1]
    hops = n_rows // NY // 4
    f32 = jnp.float32
    vmem = pl.BlockSpec(memory_space=pltpu.VMEM)
    hbm = pl.BlockSpec(memory_space=pltpu.HBM)
    pairs = [pltpu.SemaphoreType.DMA((4,))] * 2
    halves = lambda *lead: pltpu.VMEM(lead + (ROWS, BLK), f32)
    strip = lambda dtype: pltpu.VMEM((8, cells), dtype)
    return pl.pallas_call(
        functools.partial(gram_kernel, n_rows),
        out_shape=(
            jax.ShapeDtypeStruct((2, 2, 3, ROWS, BLK), f32),
            jax.ShapeDtypeStruct((2, 3, 2, ROWS, BLK), f32),
            jax.ShapeDtypeStruct((4, BLK, BLK), f32),
        ),
        in_specs=[hbm] * 5,
        out_specs=(vmem, vmem, vmem),
        scratch_shapes=[
            pltpu.VMEM((8, cells, BLK), jnp.bfloat16),
            pltpu.VMEM((cells, 8 * BLK), jnp.bfloat16),
            strip(f32), strip(jnp.bfloat16),
            pltpu.VMEM((1, BLK), jnp.int32), pltpu.VMEM((1, BLK), jnp.int32),
            pltpu.VMEM((8, BLK), jnp.int32), pltpu.VMEM((8, 8, BLK), jnp.int32),
            strip(f32), strip(f32),
            halves(2, 2 * HALF), halves(2 * HALF), halves(2 * HALF),
            halves(4, 4), halves(4, 4), halves(4), halves(4), halves(4), halves(4),
            pltpu.VMEM((BLK, BLK), f32), pltpu.VMEM((4, 32, BLK), f32),
            pltpu.VMEM((hops, 32, BLK), f32), pltpu.VMEM((BLK, BLK), f32),
            pltpu.SemaphoreType.DMA((4,)),
            *[pltpu.SemaphoreType.DMA((8,))] * 4,
            pltpu.SemaphoreType.DMA((2,)), pltpu.SemaphoreType.DMA((2,)),
            pltpu.SemaphoreType.DMA((2,)),
            *pairs * 4, *pairs, *pairs, *pairs, *pairs * 4,
            pltpu.SemaphoreType.DMA((2,)), pltpu.SemaphoreType.DMA((2,)),
        ],
        compiler_params=pltpu.CompilerParams(
            collective_id=0, has_side_effects=True, vmem_limit_bytes=48 << 20
        ),
        name="gram",
    )(*[pltpu.with_memory_space_constraint(v, pltpu.HBM) for v in (base, field, grad, tile, kind)])


def dot_f32(left, right, dims=((1,), (0,))):
    return lax.dot_general(
        left, right, (dims, ((), ())), precision=HIGHEST, preferred_element_type=jnp.float32
    )


def across(vec, col):
    return jnp.broadcast_to(vec[:, col:col + 1], (8, BLK))


def along(vec, row):
    return jnp.broadcast_to(vec[row:row + 1, :], (8, BLK))


def split_3(x):
    high = x.astype(jnp.bfloat16)
    rest = x - high.astype(jnp.float32)
    mid = rest.astype(jnp.bfloat16)
    return high, mid, (rest - mid.astype(jnp.float32)).astype(jnp.bfloat16)


def outer(left, right):
    lh, lm, ll = split_3(left)
    rh, rm, rl = split_3(right)
    return lax.dot_general(
        jnp.concatenate([lh, lh, lm, lm, lh, ll], axis=0),
        jnp.concatenate([rh, rm, rh, rm, rl, rh], axis=0),
        (((0,), (0,)), ((), ())), preferred_element_type=jnp.float32,
    )


def factor_block(work, inv):
    rows = lax.broadcasted_iota(jnp.int32, (8, BLK), 0)
    lane = lax.broadcasted_iota(jnp.int32, (8, BLK), 1)
    tall = 64
    for q in range(BLK // tall):
        at = [tall * q + 8 * s for s in range(tall // 8)]
        xs = [work[a:a + 8, :] for a in at]
        ahead = None
        for s in range(len(at)):
            start = at[s]
            cols = ahead or [across(xs[s], start + t) for t in range(8)]
            later = range(s + 1, len(at))
            below = {n: [across(xs[n], start + t) for t in range(8)] for n in later}
            ahead = [across(xs[s + 1], at[s + 1] + t) for t in range(8)] if later else None
            here = jnp.logical_and(lane >= start, lane < start + 8)
            xs[s] = jnp.where(here, jnp.where(lane - start == rows, 1.0, 0.0), xs[s])
            for n in later:
                xs[n] = jnp.where(here, 0.0, xs[n])
            pivot = along(cols[0], 0)
            pivots = pivot
            for t in range(8):
                entry = {u: along(cols[t], u) for u in range(t + 1, 8)}
                recip = 1.0 / pivot
                row = along(xs[s], t)
                if t < 7:
                    pivot = along(cols[t + 1], t + 1) - (entry[t + 1] * recip) * entry[t + 1]
                    pivots = jnp.where(rows >= t + 1, pivot, pivots)
                    mult = cols[t] * recip
                    for u in range(t + 1, 8):
                        cols[u] = cols[u] - mult * entry[u]
                    xs[s] = xs[s] - jnp.where(rows > t, mult, 0.0) * row
                for n in later:
                    mult = below[n][t] * recip
                    if n == s + 1:
                        for u in range(8):
                            ahead[u] = ahead[u] - mult * along(below[n][t], u)
                    for u in range(t + 1, 8):
                        below[n][u] = below[n][u] - mult * entry[u]
                    xs[n] = xs[n] - mult * row
            inv[start:start + 8, :] = xs[s] * (1.0 / jnp.sqrt(pivots))
        low = tall * (q + 1)
        if low < BLK:
            done = inv[tall * q:low, :]
            row_at = lax.broadcasted_iota(jnp.int32, done.shape, 0) + tall * q
            col_at = lax.broadcasted_iota(jnp.int32, done.shape, 1)
            past = jnp.where(jnp.logical_and(col_at < low, col_at > row_at), 0.0, done)
            rest = work[low:BLK, :]
            col_at = lax.broadcasted_iota(jnp.int32, rest.shape, 1)
            rest = jnp.where(jnp.logical_and(col_at >= tall * q, col_at < low), 0.0, rest)
            work[low:BLK, :] = rest - outer(done[:, low:BLK], past)
    lower = (
        lax.broadcasted_iota(jnp.int32, (BLK, BLK), 0)
        >= lax.broadcasted_iota(jnp.int32, (BLK, BLK), 1)
    )
    inv[...] = jnp.where(lower, inv[...], 0.0)


def factor_kernel(head_a, head_b, own_ref, r_ref, m_ref, mat, head_ref, work, inv):
    c = lax.axis_index("cols")
    for spot in range(12):
        k, at_x, at_y = spot // 6, spot // 3 % 2, spot % 3
        head_ref[spot, 0:ROWS] = head_a[k, at_x, at_y]
        head_ref[spot, ROWS:BLK] = head_b[k, at_y, at_x]
    near = jnp.minimum(c, 3)
    for k in range(4):
        for j in range(k, 4):
            mat[k, :, j * BLK:(j + 1) * BLK] = head_ref[HEAD.index((k, j))]
        low, high = jnp.minimum(near, k), jnp.maximum(near, k)
        found = head_ref[low * 4 - low * (low - 1) // 2 + high - low]
        found = jnp.where(k <= near, found, found.T)
        mat[k, :, 512:640] = jnp.where(c >= 4, own_ref[k], found)
        mat[k, :, 640:768] = jnp.broadcast_to(head_ref[len(HEAD), k:k + 1, :], (BLK, BLK)).T
    for k in range(4):
        work[...] = mat[k, :, k * BLK:(k + 1) * BLK]
        factor_block(work, inv.at[k])
        low = (k + 1) * BLK
        inverse = inv[k]
        if k == 3:
            mat[k, :, low:768] = dot_f32(inverse, mat[k, :, low:768])
            r_ref[k * BLK:(k + 1) * BLK, :] = mat[k, :, 512:640]
            continue
        near_cols = dot_f32(inverse, mat[k, :, low:low + BLK])
        mat[k, :, low:low + BLK] = near_cols
        mat[k + 1, :, low:low + BLK] = mat[k + 1, :, low:low + BLK] - dot_f32(
            near_cols, near_cols, ((0,), (0,))
        )
        far = low + BLK
        mat[k, :, far:768] = dot_f32(inverse, mat[k, :, far:768])
        r_ref[k * BLK:(k + 1) * BLK, :] = mat[k, :, 512:640]
        mat[k + 1, :, far:768] = mat[k + 1, :, far:768] - dot_f32(
            near_cols, mat[k, :, far:768], ((0,), (0,))
        )
        for i in range(k + 2, 4):
            mat[i, :, i * BLK:768] = mat[i, :, i * BLK:768] - dot_f32(
                mat[k, :, i * BLK:(i + 1) * BLK], mat[k, :, i * BLK:768], ((0,), (0,))
            )
    rest = [mat[k, :, 640:768] for k in range(4)]
    for k in (3, 2, 1, 0):
        solved = dot_f32(inv[k], rest[k], ((0,), (0,)))
        for i in range(k):
            rest[i] = rest[i] - dot_f32(mat[i, :, k * BLK:(k + 1) * BLK], solved)
        m_ref[k:k + 1, :] = solved.T[0:1, :]


def factor_and_solve(head_a, head_b, own):
    f32 = jnp.float32
    vmem = pl.BlockSpec(memory_space=pltpu.VMEM)
    return pl.pallas_call(
        factor_kernel,
        out_shape=(
            jax.ShapeDtypeStruct((512, BLK), f32),
            jax.ShapeDtypeStruct((4, BLK), f32),
        ),
        in_specs=[vmem, vmem, vmem],
        out_specs=(vmem, vmem),
        scratch_shapes=[
            pltpu.VMEM((4, BLK, 768), f32),
            pltpu.VMEM((12, BLK, BLK), f32),
            pltpu.VMEM((BLK, BLK), f32),
            pltpu.VMEM((4, BLK, BLK), f32),
        ],
        compiler_params=pltpu.CompilerParams(vmem_limit_bytes=48 << 20),
        name="factor",
    )(head_a, head_b, own)


def shards(n_rows, sens_base, design_field, gradient, tile_index, type_codes):
    head_a, head_b, own = gram_everywhere(
        n_rows, sens_base, design_field, gradient,
        tile_index.reshape(1, BLK), type_codes.reshape(1, BLK),
    )
    r_panels, multipliers = factor_and_solve(head_a, head_b, own)
    return r_panels, multipliers.reshape(-1)


def solution(mesh):
    placed = (P("rows", "cols"), P("rows", None), P("rows", None), P("cols"), P("cols"))
    return jax.shard_map(
        functools.partial(shards, mesh.shape["rows"]),
        mesh=mesh, in_specs=placed, out_specs=(P(None, "cols"), P()), check_vma=False,
    )
```

```python
import functools

import jax
import jax.numpy as jnp
from jax import lax
from jax.experimental import pallas as pl
from jax.experimental.pallas import tpu as pltpu
from jax.sharding import PartitionSpec as P

TILE = 128
BLK = 128
NX = 4
NY = 4
MESH = pl.DeviceIdType.MESH
HEAD = [(a, b) for a in range(4) for b in range(a, 4)]
COUNT_X = (3, 3, 4, 4)
FIRST_X = (0, 3, 6, 10)
COUNT_Y = (4, 4, 4, 2)
FIRST_Y = (0, 4, 8, 12)
HALF = 14
ROWS = BLK // 2
PARTS = 2


def slot_of(core, x, y):
    if x < 2:
        spot = (core * 2 + x) * 3 + y
        if spot < len(HEAD):
            return HEAD[spot]
        return "proj" if spot == len(HEAD) else None
    return (y, x * 2 + core)


def gram_kernel(
    n_rows,
    base_ref, field_hbm, grad_hbm, tile_hbm, type_hbm,
    out_a, out_b, own_ref,
    raw, jac, field_ref, grad_ref, tile_ref, type_ref, codes_mine, codes, north, south,
    parts, from_core, half, from_x, from_y, sum_a, sum_b, from_x2, from_y2,
    block, from_zl, from_zh, line,
    load_sems, a2a_send, a2a_recv, code_send, code_recv, halo_send, halo_recv, core_sems,
    xa_send, xa_recv, yb_send, yb_recv, ya_send, ya_recv, xb_send, xb_recv,
    zl_send, zl_recv, zh_send, zh_recv, zg_send, zg_recv,
    gy_send, gy_recv, gx_send, gx_recv, hx_send, hx_recv, hy_send, hy_recv,
    cg_send, cg_recv,
):
    r = lax.axis_index("rows")
    c = lax.axis_index("cols")
    z, y = r // NY, r % NY
    zh, zl = z // 4, z % 4
    hops = n_rows // NY // 4
    x, core = c // 2, c % 2
    up, down = (r + n_rows - 1) % n_rows, (r + 1) % n_rows
    cells = raw.shape[1]

    def dev_c(col):
        return (r, col)

    def dev_x(xx):
        return (r, xx * 2 + core)

    def dev_y(yy):
        return (z * NY + yy, c)

    def dev_z(hi, lo):
        return ((hi * 4 + lo) * NY + y, c)

    def remote(src, dst, send, recv, device):
        return pltpu.make_async_remote_copy(
            src_ref=src, dst_ref=dst, send_sem=send, recv_sem=recv,
            device_id=device, device_id_type=MESH,
        )

    barrier = pltpu.get_barrier_semaphore()

    def greet(device):
        pl.semaphore_signal(barrier, inc=1, device_id=device, device_id_type=MESH)

    for d in range(1, hops):
        greet(dev_z((zh + d) % hops, zl))
    for d in range(1, 8):
        greet(dev_c((c + d) % 8))
    for d in range(1, NY):
        greet(dev_y((y + d) % NY))
    for d in range(1, 4):
        greet(dev_z(zh, (zl + d) % 4))
    greet((up, c))
    greet((down, c))
    loads = []
    for i, (src, dst) in enumerate((
        (field_hbm, field_ref), (tile_hbm, tile_ref), (type_hbm, type_ref), (grad_hbm, grad_ref),
    )):
        loads.append(pltpu.make_async_copy(src, dst, load_sems.at[i]))
        loads[-1].start()
    codes_mine[...] = jnp.zeros_like(codes_mine)
    loads[1].wait()
    loads[2].wait()
    codes_mine[0:1, :] = tile_ref[...]
    codes_mine[1:2, :] = type_ref[...]
    loads[0].wait()
    pl.semaphore_wait(barrier, 7 + (NY - 1) + 3 + (hops - 1) + 2)

    sent = []
    for d in range(1, 8):
        to = (c + d) % 8
        cp = remote(codes_mine, codes.at[c], code_send.at[d], code_recv.at[d], dev_c(to))
        cp.start()
        sent.append(cp)
    cp = remote(field_ref, north, halo_send.at[0], halo_recv.at[0], (down, c))
    cp.start()
    sent.append(cp)
    cp = remote(field_ref, south, halo_send.at[1], halo_recv.at[1], (up, c))
    cp.start()
    sent.append(cp)
    part = cells // PARTS

    def a2a_copy(h, d, spot, peer):
        return remote(
            base_ref.at[pl.ds(peer * cells + h * part, part), :],
            raw.at[spot, pl.ds(h * part, part)],
            a2a_send.at[h * 8 + d], a2a_recv.at[h * 8 + d], dev_c(peer),
        )

    for h in range(PARTS):
        for d in (4, 3, 5, 2, 6, 1, 7):
            cp = a2a_copy(h, d, c, (c + d) % 8)
            cp.start()
            sent.append(cp)
    mine = pltpu.make_async_copy(
        base_ref.at[pl.ds(c * cells, cells), :], raw.at[c], a2a_recv.at[0]
    )
    mine.start()
    codes[c] = codes_mine[...]

    remote(field_ref, north, halo_send.at[0], halo_recv.at[0], (up, c)).wait_recv()
    remote(field_ref, south, halo_send.at[1], halo_recv.at[1], (down, c)).wait_recv()
    here = field_ref[pl.ds(c, 1), :]
    above = field_ref[pl.ds((c + 7) % 8, 1), :]
    below = field_ref[pl.ds((c + 1) % 8, 1), :]
    above = jnp.where(c == 0, jnp.where(r == 0, 0.0, north[7:8, :]), above)
    below = jnp.where(c == 7, jnp.where(r == n_rows - 1, 0.0, south[0:1, :]), below)
    wide = (8, cells)
    here = jnp.broadcast_to(here, wide)
    above = jnp.broadcast_to(above, wide)
    below = jnp.broadcast_to(below, wide)
    lane = lax.broadcasted_iota(jnp.int32, wide, 1)
    west = jnp.where(lane == 0, 0.0, pltpu.roll(here, 1, 1))
    east = jnp.where(lane == cells - 1, 0.0, pltpu.roll(here, cells - 1, 1))
    laplace = 4.0 * here - (above + below + west + east)
    slope_x = 0.5 * (east - west)
    slope_y = 0.5 * (below - above)
    srow = lax.broadcasted_iota(jnp.int32, wide, 0)
    terms = []
    for fieldval in (laplace, slope_x, slope_y):
        rest = fieldval / TILE
        for _ in range(3):
            term = rest.astype(jnp.bfloat16).astype(jnp.float32)
            terms.append(term)
            rest = rest - term
    low = jnp.zeros(wide, jnp.float32)
    for k in range(8):
        low = jnp.where(srow == k, terms[(k % 3) * 3 + k // 3], low)
    high = jnp.where(srow == 0, terms[2 * 3 + 2], 0.0)
    both = jnp.concatenate([low, high], axis=0)
    tiles = cells // TILE
    spread = jnp.concatenate([both] * tiles, axis=0)
    krow = lax.broadcasted_iota(jnp.int32, spread.shape, 0)
    kcol = lax.broadcasted_iota(jnp.int32, spread.shape, 1)
    spread = jnp.where(krow // 16 == kcol // TILE, spread, 0.0)
    spread_t = spread.T.astype(jnp.bfloat16)

    first_tile = (r * 8 // TILE) * tiles
    rows16 = lax.broadcasted_iota(jnp.int32, (16 * tiles, BLK), 0)
    term_id = rows16 % 16
    kind_of = jnp.where(term_id < 9, term_id % 3, 3)
    tile_of = first_tile + rows16 // 16
    for d in range(1, 8):
        src = (c + 8 - d) % 8
        remote(codes_mine, codes.at[src], code_send.at[d], code_recv.at[d], dev_c(src)).wait_recv()

    where = {}
    for k in range(2):
        for xx in range(NX):
            for yy in range(COUNT_X[xx]):
                low = FIRST_Y[yy] + (xx if yy < 3 else xx - 2)
                where[slot_of(k, xx, yy)] = (k, FIRST_X[xx] + yy, HALF + low)

    def put(key, value, add=False):
        k, upper, lower = where[key]
        parts[k, upper] = value[0:ROWS] + (parts[k, upper] if add else 0.0)
        parts[k, lower] = value[ROWS:BLK] + (parts[k, lower] if add else 0.0)

    contract = (((0,), (0,)), ((), ()))
    for h in range(PARTS):
        for cs in range(8):
            if h == 0:
                @pl.when(c == cs)
                def _():
                    mine.wait()

            @pl.when(c != cs)
            def _():
                a2a_copy(h, (c + 8 - cs) % 8, cs, cs).wait_recv()

            chosen = jnp.logical_and(
                kind_of == codes[cs, 1:2, :], tile_of == codes[cs, 0:1, :]
            ).astype(jnp.float32).astype(jnp.bfloat16)
            span = slice(h * part, (h + 1) * part)
            added = jnp.dot(spread_t[span], chosen, preferred_element_type=jnp.float32)
            jac[span, cs * BLK:(cs + 1) * BLK] = (
                raw[cs, span].astype(jnp.float32) + added
            ).astype(jnp.bfloat16)

        for pa in range(2):
            left = jac[span, pa * 256:(pa + 1) * 256]
            for pb in range(pa, 4):
                prod = lax.dot_general(
                    left, jac[span, pb * 256:(pb + 1) * 256], contract,
                    preferred_element_type=jnp.float32,
                )
                for i in range(2):
                    for j in range(2):
                        key = (pa * 2 + i, pb * 2 + j)
                        if key in where:
                            put(key, prod[i * BLK:(i + 1) * BLK, j * BLK:(j + 1) * BLK], h > 0)
    loads[3].wait()
    proj = jnp.dot(grad_ref[...], jac[:, 0:512], preferred_element_type=jnp.float32)
    proj = jnp.sum(
        jnp.where(lax.broadcasted_iota(jnp.int32, proj.shape, 0) == c, proj, 0.0),
        axis=0, keepdims=True,
    )
    put("proj", jnp.zeros((BLK, BLK), jnp.float32))
    put(None, jnp.zeros((BLK, BLK), jnp.float32))
    k, upper, _ = where["proj"]
    for i in range(4):
        parts[k, upper, i:i + 1, :] = proj[:, i * BLK:(i + 1) * BLK]

    cp = remote(
        parts.at[1 - core], from_core, core_sems.at[0], core_sems.at[1], dev_c(x * 2 + 1 - core)
    )
    cp.start()
    sent.append(cp)
    cp.wait_recv()
    half[...] = parts[core] + from_core[...]

    def xa_copy(xx, d, peer):
        span = COUNT_X[xx]
        return remote(
            half.at[pl.ds(FIRST_X[xx], span)], from_x.at[d, pl.ds(0, span)],
            xa_send.at[d], xa_recv.at[d], dev_x(peer),
        )

    def yb_copy(yy, d, peer):
        span = COUNT_Y[yy]
        return remote(
            half.at[pl.ds(HALF + FIRST_Y[yy], span)], from_y.at[d, pl.ds(0, span)],
            yb_send.at[d], yb_recv.at[d], dev_y(peer),
        )

    for q in range(4):
        @pl.when(x != q)
        def _():
            xa_copy(q, (q + NX - x) % NX, q).start()

        @pl.when(y != q)
        def _():
            yb_copy(q, (q + NY - y) % NY, q).start()

    for q in range(4):
        @pl.when(x == q)
        def _():
            span = COUNT_X[q]
            total = half[FIRST_X[q]:FIRST_X[q] + span]
            for d in (1, 3, 2):
                xa_copy(q, d, (q + NX - d) % NX).wait_recv()
                total = total + from_x[d, 0:span]
            sum_a[0:span] = total

    for q in range(4):
        @pl.when(y == q)
        def _():
            span = COUNT_Y[q]
            total = half[HALF + FIRST_Y[q]:HALF + FIRST_Y[q] + span]
            for d in (1, 3, 2):
                yb_copy(q, d, (q + NY - d) % NY).wait_recv()
                total = total + from_y[d, 0:span]
            sum_b[0:span] = total

    skip = jnp.where(y == 3, 2, 0)
    holds = jnp.logical_or(x >= 2, y < 3)

    def ya_copy(d, yy, peer):
        return remote(sum_a.at[yy], from_y2.at[d], ya_send.at[d], ya_recv.at[d], dev_y(peer))

    def xb_copy(d, spot, peer):
        return remote(sum_b.at[spot], from_x2.at[d], xb_send.at[d], xb_recv.at[d], dev_x(peer))

    for d in range(1, 4):
        yy = (y + d) % NY
        xx = (x + d) % NX

        @pl.when(jnp.logical_or(x >= 2, yy < 3))
        def _():
            ya_copy(d, yy, yy).start()

        @pl.when(jnp.logical_or(xx >= 2, y < 3))
        def _():
            xb_copy(d, xx - skip, xx).start()

    def zl_copy(d, spot, peer):
        return remote(
            block.at[pl.ds(spot * 32, 32)], from_zl.at[d],
            zl_send.at[d], zl_recv.at[d], dev_z(zh, peer),
        )

    def zh_copy(d, spot, peer):
        return remote(
            from_zh.at[spot], from_zh.at[spot], zh_send.at[d], zh_recv.at[d], dev_z(peer, zl)
        )

    def zg_copy(d, spot, peer):
        return remote(
            line.at[pl.ds(spot * 32, 32)], line.at[pl.ds(spot * 32, 32)],
            zg_send.at[d], zg_recv.at[d], dev_z(zh, peer),
        )

    def gy_own(d, spot, peer):
        return remote(line, own_ref.at[spot], gy_send.at[d], gy_recv.at[d], dev_y(peer))

    def gy_head(d, spot, peer):
        return remote(
            line.at[pl.ds(0, ROWS)], out_a.at[core, x, spot],
            gy_send.at[d], gy_recv.at[d], dev_y(peer),
        )

    def gx_head(d, spot, peer):
        return remote(
            line.at[pl.ds(ROWS, ROWS)], out_b.at[core, y, spot],
            gx_send.at[d], gx_recv.at[d], dev_x(peer),
        )

    @pl.when(holds)
    def _():
        upper = sum_a[y]
        lower = sum_b[x - skip]
        for d in (1, 3, 2):
            ya_copy(d, 0, (y + NY - d) % NY).wait_recv()
            upper = upper + from_y2[d]
        for d in (1, 3, 2):
            xb_copy(d, 0, (x + NX - d) % NX).wait_recv()
            lower = lower + from_x2[d]
        block[0:ROWS] = upper
        block[ROWS:BLK] = lower
        for d in range(1, 4):
            lo = (zl + d) % 4
            zl_copy(d, lo, lo).start()
        total = block[pl.ds(pl.multiple_of(zl * 32, 32), 32)]
        for d in range(1, 4):
            zl_copy(d, 0, (zl + 4 - d) % 4).wait_recv()
            total = total + from_zl[d]
        from_zh[zh] = total
        for d in range(1, hops):
            zh_copy(d, zh, (zh + d) % hops).start()
        for d in range(1, hops):
            src = (zh + hops - d) % hops
            zh_copy(d, src, src).wait_recv()
        total = from_zh[0]
        for i in range(1, hops):
            total = total + from_zh[i]
        line[pl.ds(pl.multiple_of(zl * 32, 32), 32)] = total
        for d in range(1, 4):
            zg_copy(d, zl, (zl + d) % 4).start()
        for d in range(1, 4):
            src = (zl + 4 - d) % 4
            zg_copy(d, src, src).wait_recv()

        @pl.when(x >= 2)
        def _():
            for d in range(1, 4):
                gy_own(d, y, (y + d) % NY).start()
            own_ref[y] = line[...]

        @pl.when(x < 2)
        def _():
            for d in range(1, 4):
                gy_head(d, y, (y + d) % NY).start()
                gx_head(d, x, (x + d) % NX).start()
            out_a[core, x, y] = line[0:ROWS]
            out_b[core, y, x] = line[ROWS:BLK]

    def hx_copy(d, xx, peer):
        return remote(
            out_a.at[core, xx], out_a.at[core, xx], hx_send.at[d], hx_recv.at[d], dev_x(peer)
        )

    def hy_copy(d, yy, peer):
        return remote(
            out_b.at[core, yy], out_b.at[core, yy], hy_send.at[d], hy_recv.at[d], dev_y(peer)
        )

    @pl.when(x < 2)
    def _():
        for d in range(1, 4):
            src = (y + NY - d) % NY

            @pl.when(src < 3)
            def _():
                gy_head(d, src, src).wait_recv()

        for d in range(1, 4):
            hx_copy(d, x, (x + d) % NX).start()
        own_ref[...] = jnp.zeros_like(own_ref)

    @pl.when(y < 3)
    def _():
        for d in range(1, 4):
            src = (x + NX - d) % NX

            @pl.when(src < 2)
            def _():
                gx_head(d, src, src).wait_recv()

        for d in range(1, 4):
            hy_copy(d, y, (y + d) % NY).start()

    def swap_a(half_core):
        return remote(
            out_a.at[half_core], out_a.at[half_core], cg_send.at[0], cg_recv.at[0],
            dev_c(x * 2 + 1 - core),
        )

    def swap_b(half_core):
        return remote(
            out_b.at[half_core], out_b.at[half_core], cg_send.at[1], cg_recv.at[1],
            dev_c(x * 2 + 1 - core),
        )

    for d in range(1, 4):
        src = (y + NY - d) % NY

        @pl.when(src < 3)
        def _():
            hy_copy(d, src, src).wait_recv()

    swap_b(core).start()
    for d in range(1, 4):
        src = (x + NX - d) % NX

        @pl.when(src < 2)
        def _():
            hx_copy(d, src, src).wait_recv()

    swap_a(core).start()

    @pl.when(x >= 2)
    def _():
        for d in range(1, 4):
            src = (y + NY - d) % NY
            gy_own(d, src, src).wait_recv()

    swap_b(1 - core).wait_recv()
    swap_a(1 - core).wait_recv()

    for cp in sent:
        cp.wait_send()
    for q in range(4):
        @pl.when(x != q)
        def _():
            xa_copy(q, (q + NX - x) % NX, q).wait_send()

        @pl.when(y != q)
        def _():
            yb_copy(q, (q + NY - y) % NY, q).wait_send()

    for d in range(1, 4):
        yy = (y + d) % NY
        xx = (x + d) % NX

        @pl.when(jnp.logical_or(x >= 2, yy < 3))
        def _():
            ya_copy(d, yy, yy).wait_send()

        @pl.when(jnp.logical_or(xx >= 2, y < 3))
        def _():
            xb_copy(d, xx - skip, xx).wait_send()

    @pl.when(holds)
    def _():
        for d in range(1, 4):
            lo = (zl + d) % 4
            zl_copy(d, lo, lo).wait_send()
            zg_copy(d, zl, lo).wait_send()
        for d in range(1, hops):
            zh_copy(d, zh, (zh + d) % hops).wait_send()

        @pl.when(x >= 2)
        def _():
            for d in range(1, 4):
                gy_own(d, y, (y + d) % NY).wait_send()

        @pl.when(x < 2)
        def _():
            for d in range(1, 4):
                gy_head(d, y, (y + d) % NY).wait_send()
                gx_head(d, x, (x + d) % NX).wait_send()

    @pl.when(x < 2)
    def _():
        for d in range(1, 4):
            hx_copy(d, x, (x + d) % NX).wait_send()

    @pl.when(y < 3)
    def _():
        for d in range(1, 4):
            hy_copy(d, y, (y + d) % NY).wait_send()

    swap_b(core).wait_send()
    swap_a(core).wait_send()


def gram_everywhere(n_rows, base, field, grad, tile, kind):
    cells = field.shape[1]
    hops = n_rows // NY // 4
    f32 = jnp.float32
    vmem = pl.BlockSpec(memory_space=pltpu.VMEM)
    hbm = pl.BlockSpec(memory_space=pltpu.HBM)
    pairs = [pltpu.SemaphoreType.DMA((4,))] * 2
    halves = lambda *lead: pltpu.VMEM(lead + (ROWS, BLK), f32)
    strip = lambda dtype: pltpu.VMEM((8, cells), dtype)
    return pl.pallas_call(
        functools.partial(gram_kernel, n_rows),
        out_shape=(
            jax.ShapeDtypeStruct((2, 2, 3, ROWS, BLK), f32),
            jax.ShapeDtypeStruct((2, 3, 2, ROWS, BLK), f32),
            jax.ShapeDtypeStruct((4, BLK, BLK), f32),
        ),
        in_specs=[hbm] * 5,
        out_specs=(vmem, vmem, vmem),
        scratch_shapes=[
            pltpu.VMEM((8, cells, BLK), jnp.bfloat16),
            pltpu.VMEM((cells, 8 * BLK), jnp.bfloat16),
            strip(f32), strip(jnp.bfloat16),
            pltpu.VMEM((1, BLK), jnp.int32), pltpu.VMEM((1, BLK), jnp.int32),
            pltpu.VMEM((8, BLK), jnp.int32), pltpu.VMEM((8, 8, BLK), jnp.int32),
            strip(f32), strip(f32),
            halves(2, 2 * HALF), halves(2 * HALF), halves(2 * HALF),
            halves(4, 4), halves(4, 4), halves(4), halves(4), halves(4), halves(4),
            pltpu.VMEM((BLK, BLK), f32), pltpu.VMEM((4, 32, BLK), f32),
            pltpu.VMEM((hops, 32, BLK), f32), pltpu.VMEM((BLK, BLK), f32),
            pltpu.SemaphoreType.DMA((4,)),
            *[pltpu.SemaphoreType.DMA((8 * PARTS,))] * 2, *[pltpu.SemaphoreType.DMA((8,))] * 2,
            pltpu.SemaphoreType.DMA((2,)), pltpu.SemaphoreType.DMA((2,)),
            pltpu.SemaphoreType.DMA((2,)),
            *pairs * 4, *pairs, *pairs, *pairs, *pairs * 4,
            pltpu.SemaphoreType.DMA((2,)), pltpu.SemaphoreType.DMA((2,)),
        ],
        compiler_params=pltpu.CompilerParams(
            collective_id=0, has_side_effects=True, vmem_limit_bytes=48 << 20
        ),
        name="gram",
    )(*[pltpu.with_memory_space_constraint(v, pltpu.HBM) for v in (base, field, grad, tile, kind)])


def across(vec, col):
    return jnp.broadcast_to(vec[:, col:col + 1], (8, BLK))


def along(vec, row):
    return jnp.broadcast_to(vec[row:row + 1, :], (8, BLK))


def split_3(x):
    high = x.astype(jnp.bfloat16)
    rest = x - high.astype(jnp.float32)
    mid = rest.astype(jnp.bfloat16)
    return high, mid, (rest - mid.astype(jnp.float32)).astype(jnp.bfloat16)


def dot_f32(left, right, dims=((1,), (0,))):
    lh, lm, ll = split_3(left)
    rh, rm, rl = split_3(right)
    return lax.dot_general(
        jnp.concatenate([lh, lh, lm, lm, lh, ll], axis=dims[0][0]),
        jnp.concatenate([rh, rm, rh, rm, rl, rh], axis=dims[1][0]),
        (dims, ((), ())), preferred_element_type=jnp.float32,
    )


def factor_block(work, inv):
    rows = lax.broadcasted_iota(jnp.int32, (8, BLK), 0)
    lane = lax.broadcasted_iota(jnp.int32, (8, BLK), 1)
    tall = 64
    for q in range(BLK // tall):
        at = [tall * q + 8 * s for s in range(tall // 8)]
        xs = [work[a:a + 8, :] for a in at]
        ahead = None
        for s in range(len(at)):
            start = at[s]
            cols = ahead or [across(xs[s], start + t) for t in range(8)]
            later = range(s + 1, len(at))
            below = {n: [across(xs[n], start + t) for t in range(8)] for n in later}
            ahead = [across(xs[s + 1], at[s + 1] + t) for t in range(8)] if later else None
            here = jnp.logical_and(lane >= start, lane < start + 8)
            xs[s] = jnp.where(here, jnp.where(lane - start == rows, 1.0, 0.0), xs[s])
            for n in later:
                xs[n] = jnp.where(here, 0.0, xs[n])
            pivot = along(cols[0], 0)
            pivots = pivot
            for t in range(8):
                entry = {u: along(cols[t], u) for u in range(t + 1, 8)}
                recip = 1.0 / pivot
                row = along(xs[s], t)
                if t < 7:
                    pivot = along(cols[t + 1], t + 1) - (entry[t + 1] * recip) * entry[t + 1]
                    pivots = jnp.where(rows >= t + 1, pivot, pivots)
                    mult = cols[t] * recip
                    for u in range(t + 1, 8):
                        cols[u] = cols[u] - mult * entry[u]
                    xs[s] = xs[s] - jnp.where(rows > t, mult, 0.0) * row
                for n in later:
                    mult = below[n][t] * recip
                    if n == s + 1:
                        for u in range(8):
                            ahead[u] = ahead[u] - mult * along(below[n][t], u)
                    for u in range(t + 1, 8):
                        below[n][u] = below[n][u] - mult * entry[u]
                    xs[n] = xs[n] - mult * row
            inv[start:start + 8, :] = xs[s] * (1.0 / jnp.sqrt(pivots))
        low = tall * (q + 1)
        if low < BLK:
            done = inv[tall * q:low, :]
            row_at = lax.broadcasted_iota(jnp.int32, done.shape, 0) + tall * q
            col_at = lax.broadcasted_iota(jnp.int32, done.shape, 1)
            past = jnp.where(jnp.logical_and(col_at < low, col_at > row_at), 0.0, done)
            rest = work[low:BLK, :]
            col_at = lax.broadcasted_iota(jnp.int32, rest.shape, 1)
            rest = jnp.where(jnp.logical_and(col_at >= tall * q, col_at < low), 0.0, rest)
            work[low:BLK, :] = rest - dot_f32(done[:, low:BLK], past, ((0,), (0,)))
    lower = (
        lax.broadcasted_iota(jnp.int32, (BLK, BLK), 0)
        >= lax.broadcasted_iota(jnp.int32, (BLK, BLK), 1)
    )
    inv[...] = jnp.where(lower, inv[...], 0.0)


def factor_kernel(head_a, head_b, own_ref, r_ref, m_ref, mat, head_ref, work, inv):
    c = lax.axis_index("cols")
    for spot in range(12):
        k, at_x, at_y = spot // 6, spot // 3 % 2, spot % 3
        head_ref[spot, 0:ROWS] = head_a[k, at_x, at_y]
        head_ref[spot, ROWS:BLK] = head_b[k, at_y, at_x]
    near = jnp.minimum(c, 3)
    for k in range(4):
        for j in range(k, 4):
            mat[k, :, j * BLK:(j + 1) * BLK] = head_ref[HEAD.index((k, j))]
        low, high = jnp.minimum(near, k), jnp.maximum(near, k)
        found = head_ref[low * 4 - low * (low - 1) // 2 + high - low]
        found = jnp.where(k <= near, found, found.T)
        mat[k, :, 512:640] = jnp.where(c >= 4, own_ref[k], found)
        mat[k, :, 640:768] = jnp.broadcast_to(head_ref[len(HEAD), k:k + 1, :], (BLK, BLK)).T
    for k in range(4):
        work[...] = mat[k, :, k * BLK:(k + 1) * BLK]
        factor_block(work, inv.at[k])
        low = (k + 1) * BLK
        inverse = inv[k]
        if k == 3:
            mat[k, :, low:768] = dot_f32(inverse, mat[k, :, low:768])
            r_ref[k * BLK:(k + 1) * BLK, :] = mat[k, :, 512:640]
            continue
        near_cols = dot_f32(inverse, mat[k, :, low:low + BLK])
        mat[k, :, low:low + BLK] = near_cols
        mat[k + 1, :, low:low + BLK] = mat[k + 1, :, low:low + BLK] - dot_f32(
            near_cols, near_cols, ((0,), (0,))
        )
        far = low + BLK
        mat[k, :, far:768] = dot_f32(inverse, mat[k, :, far:768])
        r_ref[k * BLK:(k + 1) * BLK, :] = mat[k, :, 512:640]
        mat[k + 1, :, far:768] = mat[k + 1, :, far:768] - dot_f32(
            near_cols, mat[k, :, far:768], ((0,), (0,))
        )
        for i in range(k + 2, 4):
            mat[i, :, i * BLK:768] = mat[i, :, i * BLK:768] - dot_f32(
                mat[k, :, i * BLK:(i + 1) * BLK], mat[k, :, i * BLK:768], ((0,), (0,))
            )
    rest = [mat[k, :, 640:768] for k in range(4)]
    for k in (3, 2, 1, 0):
        solved = dot_f32(inv[k], rest[k], ((0,), (0,)))
        for i in range(k):
            rest[i] = rest[i] - dot_f32(mat[i, :, k * BLK:(k + 1) * BLK], solved)
        m_ref[k:k + 1, :] = solved.T[0:1, :]


def factor_and_solve(head_a, head_b, own):
    f32 = jnp.float32
    vmem = pl.BlockSpec(memory_space=pltpu.VMEM)
    return pl.pallas_call(
        factor_kernel,
        out_shape=(
            jax.ShapeDtypeStruct((512, BLK), f32),
            jax.ShapeDtypeStruct((4, BLK), f32),
        ),
        in_specs=[vmem, vmem, vmem],
        out_specs=(vmem, vmem),
        scratch_shapes=[
            pltpu.VMEM((4, BLK, 768), f32),
            pltpu.VMEM((12, BLK, BLK), f32),
            pltpu.VMEM((BLK, BLK), f32),
            pltpu.VMEM((4, BLK, BLK), f32),
        ],
        compiler_params=pltpu.CompilerParams(vmem_limit_bytes=48 << 20),
        name="factor",
    )(head_a, head_b, own)


def shards(n_rows, sens_base, design_field, gradient, tile_index, type_codes):
    head_a, head_b, own = gram_everywhere(
        n_rows, sens_base, design_field, gradient,
        tile_index.reshape(1, BLK), type_codes.reshape(1, BLK),
    )
    r_panels, multipliers = factor_and_solve(head_a, head_b, own)
    return r_panels, multipliers.reshape(-1)


def solution(mesh):
    placed = (P("rows", "cols"), P("rows", None), P("rows", None), P("cols"), P("cols"))
    return jax.shard_map(
        functools.partial(shards, mesh.shape["rows"]),
        mesh=mesh, in_specs=placed, out_specs=(P(None, "cols"), P()), check_vma=False,
    )
```

```python
import functools

import jax
import jax.numpy as jnp
from jax import lax
from jax.experimental import pallas as pl
from jax.experimental.pallas import tpu as pltpu
from jax.sharding import PartitionSpec as P

TILE = 128
BLK = 128
NX = 4
NY = 4
MESH = pl.DeviceIdType.MESH
HEAD = [(a, b) for a in range(4) for b in range(a, 4)]
COUNT_X = (3, 3, 4, 4)
FIRST_X = (0, 3, 6, 10)
COUNT_Y = (4, 4, 4, 2)
FIRST_Y = (0, 4, 8, 12)
HALF = 14
ROWS = BLK // 2
LEAD = 48
PARTS = 2


def slot_of(core, x, y):
    if x < 2:
        spot = (core * 2 + x) * 3 + y
        if spot < len(HEAD):
            return HEAD[spot]
        return "proj" if spot == len(HEAD) else None
    return (y, x * 2 + core)


def gram_kernel(
    n_rows,
    base_ref, field_hbm, grad_hbm, tile_hbm, type_hbm,
    out_a, out_b, own_ref,
    raw, jac, field_ref, grad_ref, tile_ref, type_ref, codes_mine, codes, north, south,
    parts, from_core, half, from_x, from_y, sum_a, sum_b, from_x2, from_y2,
    block, from_zl, from_zh, line,
    load_sems, a2a_send, a2a_recv, code_send, code_recv, halo_send, halo_recv, core_sems,
    xa_send, xa_recv, yb_send, yb_recv, ya_send, ya_recv, xb_send, xb_recv,
    zl_send, zl_recv, zh_send, zh_recv, zg_send, zg_recv,
    gy_send, gy_recv, gx_send, gx_recv, hx_send, hx_recv, hy_send, hy_recv,
    cg_send, cg_recv,
):
    r = lax.axis_index("rows")
    c = lax.axis_index("cols")
    z, y = r // NY, r % NY
    zh, zl = z // 4, z % 4
    hops = n_rows // NY // 4
    x, core = c // 2, c % 2
    up, down = (r + n_rows - 1) % n_rows, (r + 1) % n_rows
    cells = raw.shape[1]

    def dev_c(col):
        return (r, col)

    def dev_x(xx):
        return (r, xx * 2 + core)

    def dev_y(yy):
        return (z * NY + yy, c)

    def dev_z(hi, lo):
        return ((hi * 4 + lo) * NY + y, c)

    def remote(src, dst, send, recv, device):
        return pltpu.make_async_remote_copy(
            src_ref=src, dst_ref=dst, send_sem=send, recv_sem=recv,
            device_id=device, device_id_type=MESH,
        )

    barrier = pltpu.get_barrier_semaphore()

    def greet(device):
        pl.semaphore_signal(barrier, inc=1, device_id=device, device_id_type=MESH)

    for d in range(1, hops):
        greet(dev_z((zh + d) % hops, zl))
    for d in range(1, 8):
        greet(dev_c((c + d) % 8))
    for d in range(1, NY):
        greet(dev_y((y + d) % NY))
    for d in range(1, 4):
        greet(dev_z(zh, (zl + d) % 4))
    greet((up, c))
    greet((down, c))
    loads = []
    for i, (src, dst) in enumerate((
        (field_hbm, field_ref), (tile_hbm, tile_ref), (type_hbm, type_ref), (grad_hbm, grad_ref),
    )):
        loads.append(pltpu.make_async_copy(src, dst, load_sems.at[i]))
        loads[-1].start()
    codes_mine[...] = jnp.zeros_like(codes_mine)
    loads[1].wait()
    loads[2].wait()
    codes_mine[0:1, :] = tile_ref[...]
    codes_mine[1:2, :] = type_ref[...]
    loads[0].wait()
    pl.semaphore_wait(barrier, 7 + (NY - 1) + 3 + (hops - 1) + 2)

    sent = []
    for d in range(1, 8):
        to = (c + d) % 8
        cp = remote(codes_mine, codes.at[c], code_send.at[d], code_recv.at[d], dev_c(to))
        cp.start()
        sent.append(cp)
    cp = remote(field_ref, north, halo_send.at[0], halo_recv.at[0], (down, c))
    cp.start()
    sent.append(cp)
    cp = remote(field_ref, south, halo_send.at[1], halo_recv.at[1], (up, c))
    cp.start()
    sent.append(cp)
    part = cells // PARTS

    def a2a_copy(h, d, spot, peer):
        return remote(
            base_ref.at[pl.ds(peer * cells + h * part, part), :],
            raw.at[spot, pl.ds(h * part, part)],
            a2a_send.at[h * 8 + d], a2a_recv.at[h * 8 + d], dev_c(peer),
        )

    for h in range(PARTS):
        for d in (4, 3, 5, 2, 6, 1, 7):
            cp = a2a_copy(h, d, c, (c + d) % 8)
            cp.start()
            sent.append(cp)
    mine = pltpu.make_async_copy(
        base_ref.at[pl.ds(c * cells, cells), :], raw.at[c], a2a_recv.at[0]
    )
    mine.start()
    codes[c] = codes_mine[...]

    remote(field_ref, north, halo_send.at[0], halo_recv.at[0], (up, c)).wait_recv()
    remote(field_ref, south, halo_send.at[1], halo_recv.at[1], (down, c)).wait_recv()
    here = field_ref[pl.ds(c, 1), :]
    above = field_ref[pl.ds((c + 7) % 8, 1), :]
    below = field_ref[pl.ds((c + 1) % 8, 1), :]
    above = jnp.where(c == 0, jnp.where(r == 0, 0.0, north[7:8, :]), above)
    below = jnp.where(c == 7, jnp.where(r == n_rows - 1, 0.0, south[0:1, :]), below)
    wide = (8, cells)
    here = jnp.broadcast_to(here, wide)
    above = jnp.broadcast_to(above, wide)
    below = jnp.broadcast_to(below, wide)
    lane = lax.broadcasted_iota(jnp.int32, wide, 1)
    west = jnp.where(lane == 0, 0.0, pltpu.roll(here, 1, 1))
    east = jnp.where(lane == cells - 1, 0.0, pltpu.roll(here, cells - 1, 1))
    laplace = 4.0 * here - (above + below + west + east)
    slope_x = 0.5 * (east - west)
    slope_y = 0.5 * (below - above)
    srow = lax.broadcasted_iota(jnp.int32, wide, 0)
    terms = []
    for fieldval in (laplace, slope_x, slope_y):
        rest = fieldval / TILE
        for _ in range(3):
            term = rest.astype(jnp.bfloat16).astype(jnp.float32)
            terms.append(term)
            rest = rest - term
    low = jnp.zeros(wide, jnp.float32)
    for k in range(8):
        low = jnp.where(srow == k, terms[(k % 3) * 3 + k // 3], low)
    high = jnp.where(srow == 0, terms[2 * 3 + 2], 0.0)
    both = jnp.concatenate([low, high], axis=0)
    tiles = cells // TILE
    spread = jnp.concatenate([both] * tiles, axis=0)
    krow = lax.broadcasted_iota(jnp.int32, spread.shape, 0)
    kcol = lax.broadcasted_iota(jnp.int32, spread.shape, 1)
    spread = jnp.where(krow // 16 == kcol // TILE, spread, 0.0)
    spread_t = spread.T.astype(jnp.bfloat16)

    first_tile = (r * 8 // TILE) * tiles
    rows16 = lax.broadcasted_iota(jnp.int32, (16 * tiles, BLK), 0)
    term_id = rows16 % 16
    kind_of = jnp.where(term_id < 9, term_id % 3, 3)
    tile_of = first_tile + rows16 // 16
    for d in range(1, 8):
        src = (c + 8 - d) % 8
        remote(codes_mine, codes.at[src], code_send.at[d], code_recv.at[d], dev_c(src)).wait_recv()

    where = {}
    for k in range(2):
        for xx in range(NX):
            for yy in range(COUNT_X[xx]):
                low = FIRST_Y[yy] + (xx if yy < 3 else xx - 2)
                where[slot_of(k, xx, yy)] = (k, FIRST_X[xx] + yy, HALF + low)

    def put(key, value, add=False):
        k, upper, lower = where[key]
        parts[k, upper] = value[0:ROWS] + (parts[k, upper] if add else 0.0)
        parts[k, lower] = value[ROWS:BLK] + (parts[k, lower] if add else 0.0)

    contract = (((0,), (0,)), ((), ()))
    for h in range(PARTS):
        for cs in range(8):
            if h == 0:
                @pl.when(c == cs)
                def _():
                    mine.wait()

            @pl.when(c != cs)
            def _():
                a2a_copy(h, (c + 8 - cs) % 8, cs, cs).wait_recv()

            chosen = jnp.logical_and(
                kind_of == codes[cs, 1:2, :], tile_of == codes[cs, 0:1, :]
            ).astype(jnp.float32).astype(jnp.bfloat16)
            span = slice(h * part, (h + 1) * part)
            added = jnp.dot(spread_t[span], chosen, preferred_element_type=jnp.float32)
            jac[span, cs * BLK:(cs + 1) * BLK] = (
                raw[cs, span].astype(jnp.float32) + added
            ).astype(jnp.bfloat16)

        for pa in range(2):
            left = jac[span, pa * 256:(pa + 1) * 256]
            for pb in range(pa, 4):
                prod = lax.dot_general(
                    left, jac[span, pb * 256:(pb + 1) * 256], contract,
                    preferred_element_type=jnp.float32,
                )
                for i in range(2):
                    for j in range(2):
                        key = (pa * 2 + i, pb * 2 + j)
                        if key in where:
                            put(key, prod[i * BLK:(i + 1) * BLK, j * BLK:(j + 1) * BLK], h > 0)
    loads[3].wait()
    proj = jnp.dot(grad_ref[...], jac[:, 0:512], preferred_element_type=jnp.float32)
    proj = jnp.sum(
        jnp.where(lax.broadcasted_iota(jnp.int32, proj.shape, 0) == c, proj, 0.0),
        axis=0, keepdims=True,
    )
    put("proj", jnp.zeros((BLK, BLK), jnp.float32))
    put(None, jnp.zeros((BLK, BLK), jnp.float32))
    k, upper, _ = where["proj"]
    for i in range(4):
        parts[k, upper, i:i + 1, :] = proj[:, i * BLK:(i + 1) * BLK]

    cp = remote(
        parts.at[1 - core], from_core, core_sems.at[0], core_sems.at[1], dev_c(x * 2 + 1 - core)
    )
    cp.start()
    sent.append(cp)
    cp.wait_recv()

    def xa_copy(xx, d, peer):
        span = COUNT_X[xx]
        return remote(
            half.at[pl.ds(FIRST_X[xx], span)], from_x.at[d, pl.ds(0, span)],
            xa_send.at[d], xa_recv.at[d], dev_x(peer),
        )

    def yb_copy(yy, d, peer):
        span = COUNT_Y[yy]
        return remote(
            half.at[pl.ds(HALF + FIRST_Y[yy], span)], from_y.at[d, pl.ds(0, span)],
            yb_send.at[d], yb_recv.at[d], dev_y(peer),
        )

    half[0:HALF] = parts[core, 0:HALF] + from_core[0:HALF]
    for q in range(4):
        @pl.when(x != q)
        def _():
            xa_copy(q, (q + NX - x) % NX, q).start()

    half[HALF:2 * HALF] = parts[core, HALF:2 * HALF] + from_core[HALF:2 * HALF]
    for q in range(4):
        @pl.when(y != q)
        def _():
            yb_copy(q, (q + NY - y) % NY, q).start()

    for q in range(4):
        @pl.when(x == q)
        def _():
            span = COUNT_X[q]
            total = half[FIRST_X[q]:FIRST_X[q] + span]
            for d in (1, 3, 2):
                xa_copy(q, d, (q + NX - d) % NX).wait_recv()
                total = total + from_x[d, 0:span]
            sum_a[0:span] = total

    skip = jnp.where(y == 3, 2, 0)
    holds = jnp.logical_or(x >= 2, y < 3)

    def ya_copy(d, yy, peer):
        return remote(sum_a.at[yy], from_y2.at[d], ya_send.at[d], ya_recv.at[d], dev_y(peer))

    def xb_copy(d, spot, peer):
        return remote(sum_b.at[spot], from_x2.at[d], xb_send.at[d], xb_recv.at[d], dev_x(peer))

    for d in range(1, 4):
        yy = (y + d) % NY

        @pl.when(jnp.logical_or(x >= 2, yy < 3))
        def _():
            ya_copy(d, yy, yy).start()

    for q in range(4):
        @pl.when(y == q)
        def _():
            span = COUNT_Y[q]
            total = half[HALF + FIRST_Y[q]:HALF + FIRST_Y[q] + span]
            for d in (1, 3, 2):
                yb_copy(q, d, (q + NY - d) % NY).wait_recv()
                total = total + from_y[d, 0:span]
            sum_b[0:span] = total

    for d in range(1, 4):
        xx = (x + d) % NX

        @pl.when(jnp.logical_or(xx >= 2, y < 3))
        def _():
            xb_copy(d, xx - skip, xx).start()

    def zl_copy(d, spot, peer):
        return remote(
            block.at[pl.ds(spot * 32, 32)], from_zl.at[d],
            zl_send.at[d], zl_recv.at[d], dev_z(zh, peer),
        )

    def zh_copy(d, spot, peer):
        return remote(
            from_zh.at[spot], from_zh.at[spot], zh_send.at[d], zh_recv.at[d], dev_z(peer, zl)
        )

    def zg_copy(d, spot, peer):
        return remote(
            line.at[pl.ds(spot * 32, 32)], line.at[pl.ds(spot * 32, 32)],
            zg_send.at[d], zg_recv.at[d], dev_z(zh, peer),
        )

    def gy_own(d, spot, peer):
        return remote(line, own_ref.at[spot], gy_send.at[d], gy_recv.at[d], dev_y(peer))

    def gy_head(d, spot, peer):
        return remote(
            line.at[pl.ds(0, LEAD)], out_a.at[core, x, spot],
            gy_send.at[d], gy_recv.at[d], dev_y(peer),
        )

    def gx_head(d, spot, peer):
        return remote(
            line.at[pl.ds(LEAD, BLK - LEAD)], out_b.at[core, y, spot],
            gx_send.at[d], gx_recv.at[d], dev_x(peer),
        )

    @pl.when(holds)
    def _():
        upper = sum_a[y]
        lower = sum_b[x - skip]
        for d in (1, 3, 2):
            ya_copy(d, 0, (y + NY - d) % NY).wait_recv()
            upper = upper + from_y2[d]
        for d in (1, 3, 2):
            xb_copy(d, 0, (x + NX - d) % NX).wait_recv()
            lower = lower + from_x2[d]
        block[0:ROWS] = upper
        block[ROWS:BLK] = lower
        for d in range(1, 4):
            lo = (zl + d) % 4
            zl_copy(d, lo, lo).start()
        total = block[pl.ds(pl.multiple_of(zl * 32, 32), 32)]
        for d in range(1, 4):
            zl_copy(d, 0, (zl + 4 - d) % 4).wait_recv()
            total = total + from_zl[d]
        from_zh[zh] = total
        for d in range(1, hops):
            zh_copy(d, zh, (zh + d) % hops).start()
        for d in range(1, hops):
            src = (zh + hops - d) % hops
            zh_copy(d, src, src).wait_recv()
        total = from_zh[0]
        for i in range(1, hops):
            total = total + from_zh[i]
        line[pl.ds(pl.multiple_of(zl * 32, 32), 32)] = total
        for d in range(1, 4):
            zg_copy(d, zl, (zl + d) % 4).start()
        for d in range(1, 4):
            src = (zl + 4 - d) % 4
            zg_copy(d, src, src).wait_recv()

        @pl.when(x >= 2)
        def _():
            for d in range(1, 4):
                gy_own(d, y, (y + d) % NY).start()
            own_ref[y] = line[...]

        @pl.when(x < 2)
        def _():
            for d in range(1, 4):
                gy_head(d, y, (y + d) % NY).start()
                gx_head(d, x, (x + d) % NX).start()
            out_a[core, x, y] = line[0:LEAD]
            out_b[core, y, x] = line[LEAD:BLK]

    def hx_copy(d, xx, peer):
        return remote(
            out_a.at[core, xx], out_a.at[core, xx], hx_send.at[d], hx_recv.at[d], dev_x(peer)
        )

    def hy_copy(d, yy, peer):
        return remote(
            out_b.at[core, yy], out_b.at[core, yy], hy_send.at[d], hy_recv.at[d], dev_y(peer)
        )

    @pl.when(x < 2)
    def _():
        for d in range(1, 4):
            src = (y + NY - d) % NY

            @pl.when(src < 3)
            def _():
                gy_head(d, src, src).wait_recv()

        for d in range(1, 4):
            hx_copy(d, x, (x + d) % NX).start()
        own_ref[...] = jnp.zeros_like(own_ref)

    @pl.when(y < 3)
    def _():
        for d in range(1, 4):
            src = (x + NX - d) % NX

            @pl.when(src < 2)
            def _():
                gx_head(d, src, src).wait_recv()

        for d in range(1, 4):
            hy_copy(d, y, (y + d) % NY).start()

    def swap_a(half_core):
        return remote(
            out_a.at[half_core], out_a.at[half_core], cg_send.at[0], cg_recv.at[0],
            dev_c(x * 2 + 1 - core),
        )

    def swap_b(half_core):
        return remote(
            out_b.at[half_core], out_b.at[half_core], cg_send.at[1], cg_recv.at[1],
            dev_c(x * 2 + 1 - core),
        )

    for d in range(1, 4):
        src = (y + NY - d) % NY

        @pl.when(src < 3)
        def _():
            hy_copy(d, src, src).wait_recv()

    swap_b(core).start()
    for d in range(1, 4):
        src = (x + NX - d) % NX

        @pl.when(src < 2)
        def _():
            hx_copy(d, src, src).wait_recv()

    swap_a(core).start()

    @pl.when(x >= 2)
    def _():
        for d in range(1, 4):
            src = (y + NY - d) % NY
            gy_own(d, src, src).wait_recv()

    swap_b(1 - core).wait_recv()
    swap_a(1 - core).wait_recv()

    for cp in sent:
        cp.wait_send()
    for q in range(4):
        @pl.when(x != q)
        def _():
            xa_copy(q, (q + NX - x) % NX, q).wait_send()

        @pl.when(y != q)
        def _():
            yb_copy(q, (q + NY - y) % NY, q).wait_send()

    for d in range(1, 4):
        yy = (y + d) % NY
        xx = (x + d) % NX

        @pl.when(jnp.logical_or(x >= 2, yy < 3))
        def _():
            ya_copy(d, yy, yy).wait_send()

        @pl.when(jnp.logical_or(xx >= 2, y < 3))
        def _():
            xb_copy(d, xx - skip, xx).wait_send()

    @pl.when(holds)
    def _():
        for d in range(1, 4):
            lo = (zl + d) % 4
            zl_copy(d, lo, lo).wait_send()
            zg_copy(d, zl, lo).wait_send()
        for d in range(1, hops):
            zh_copy(d, zh, (zh + d) % hops).wait_send()

        @pl.when(x >= 2)
        def _():
            for d in range(1, 4):
                gy_own(d, y, (y + d) % NY).wait_send()

        @pl.when(x < 2)
        def _():
            for d in range(1, 4):
                gy_head(d, y, (y + d) % NY).wait_send()
                gx_head(d, x, (x + d) % NX).wait_send()

    @pl.when(x < 2)
    def _():
        for d in range(1, 4):
            hx_copy(d, x, (x + d) % NX).wait_send()

    @pl.when(y < 3)
    def _():
        for d in range(1, 4):
            hy_copy(d, y, (y + d) % NY).wait_send()

    swap_b(core).wait_send()
    swap_a(core).wait_send()


def gram_everywhere(n_rows, base, field, grad, tile, kind):
    cells = field.shape[1]
    hops = n_rows // NY // 4
    f32 = jnp.float32
    vmem = pl.BlockSpec(memory_space=pltpu.VMEM)
    hbm = pl.BlockSpec(memory_space=pltpu.HBM)
    pairs = [pltpu.SemaphoreType.DMA((4,))] * 2
    halves = lambda *lead: pltpu.VMEM(lead + (ROWS, BLK), f32)
    strip = lambda dtype: pltpu.VMEM((8, cells), dtype)
    return pl.pallas_call(
        functools.partial(gram_kernel, n_rows),
        out_shape=(
            jax.ShapeDtypeStruct((2, 2, 3, LEAD, BLK), f32),
            jax.ShapeDtypeStruct((2, 3, 2, BLK - LEAD, BLK), f32),
            jax.ShapeDtypeStruct((4, BLK, BLK), f32),
        ),
        in_specs=[hbm] * 5,
        out_specs=(vmem, vmem, vmem),
        scratch_shapes=[
            pltpu.VMEM((8, cells, BLK), jnp.bfloat16),
            pltpu.VMEM((cells, 8 * BLK), jnp.bfloat16),
            strip(f32), strip(jnp.bfloat16),
            pltpu.VMEM((1, BLK), jnp.int32), pltpu.VMEM((1, BLK), jnp.int32),
            pltpu.VMEM((8, BLK), jnp.int32), pltpu.VMEM((8, 8, BLK), jnp.int32),
            strip(f32), strip(f32),
            halves(2, 2 * HALF), halves(2 * HALF), halves(2 * HALF),
            halves(4, 4), halves(4, 4), halves(4), halves(4), halves(4), halves(4),
            pltpu.VMEM((BLK, BLK), f32), pltpu.VMEM((4, 32, BLK), f32),
            pltpu.VMEM((hops, 32, BLK), f32), pltpu.VMEM((BLK, BLK), f32),
            pltpu.SemaphoreType.DMA((4,)),
            *[pltpu.SemaphoreType.DMA((8 * PARTS,))] * 2, *[pltpu.SemaphoreType.DMA((8,))] * 2,
            pltpu.SemaphoreType.DMA((2,)), pltpu.SemaphoreType.DMA((2,)),
            pltpu.SemaphoreType.DMA((2,)),
            *pairs * 4, *pairs, *pairs, *pairs, *pairs * 4,
            pltpu.SemaphoreType.DMA((2,)), pltpu.SemaphoreType.DMA((2,)),
        ],
        compiler_params=pltpu.CompilerParams(
            collective_id=0, has_side_effects=True, vmem_limit_bytes=48 << 20
        ),
        name="gram",
    )(*[pltpu.with_memory_space_constraint(v, pltpu.HBM) for v in (base, field, grad, tile, kind)])


def across(vec, col):
    return jnp.broadcast_to(vec[:, col:col + 1], (8, BLK))


def along(vec, row):
    return jnp.broadcast_to(vec[row:row + 1, :], (8, BLK))


def split_3(x):
    high = x.astype(jnp.bfloat16)
    rest = x - high.astype(jnp.float32)
    mid = rest.astype(jnp.bfloat16)
    return high, mid, (rest - mid.astype(jnp.float32)).astype(jnp.bfloat16)


def dot_f32(left, right, dims=((1,), (0,))):
    lh, lm, ll = split_3(left)
    rh, rm, rl = split_3(right)
    return lax.dot_general(
        jnp.concatenate([lh, lh, lm, lm, lh, ll], axis=dims[0][0]),
        jnp.concatenate([rh, rm, rh, rm, rl, rh], axis=dims[1][0]),
        (dims, ((), ())), preferred_element_type=jnp.float32,
    )


def factor_block(work, inv):
    rows = lax.broadcasted_iota(jnp.int32, (8, BLK), 0)
    lane = lax.broadcasted_iota(jnp.int32, (8, BLK), 1)
    tall = 64
    for q in range(BLK // tall):
        at = [tall * q + 8 * s for s in range(tall // 8)]
        xs = [work[a:a + 8, :] for a in at]
        ahead = None
        for s in range(len(at)):
            start = at[s]
            cols = ahead or [across(xs[s], start + t) for t in range(8)]
            later = range(s + 1, len(at))
            below = {n: [across(xs[n], start + t) for t in range(8)] for n in later}
            ahead = [across(xs[s + 1], at[s + 1] + t) for t in range(8)] if later else None
            here = jnp.logical_and(lane >= start, lane < start + 8)
            xs[s] = jnp.where(here, jnp.where(lane - start == rows, 1.0, 0.0), xs[s])
            for n in later:
                xs[n] = jnp.where(here, 0.0, xs[n])
            pivot = along(cols[0], 0)
            pivots = pivot
            for t in range(8):
                entry = {u: along(cols[t], u) for u in range(t + 1, 8)}
                recip = 1.0 / pivot
                row = along(xs[s], t)
                if t < 7:
                    pivot = along(cols[t + 1], t + 1) - (entry[t + 1] * recip) * entry[t + 1]
                    pivots = jnp.where(rows >= t + 1, pivot, pivots)
                    mult = cols[t] * recip
                    for u in range(t + 1, 8):
                        cols[u] = cols[u] - mult * entry[u]
                    xs[s] = xs[s] - jnp.where(rows > t, mult, 0.0) * row
                for n in later:
                    mult = below[n][t] * recip
                    if n == s + 1:
                        for u in range(8):
                            ahead[u] = ahead[u] - mult * along(below[n][t], u)
                    for u in range(t + 1, 8):
                        below[n][u] = below[n][u] - mult * entry[u]
                    xs[n] = xs[n] - mult * row
            inv[start:start + 8, :] = xs[s] * (1.0 / jnp.sqrt(pivots))
        low = tall * (q + 1)
        if low < BLK:
            done = inv[tall * q:low, :]
            row_at = lax.broadcasted_iota(jnp.int32, done.shape, 0) + tall * q
            col_at = lax.broadcasted_iota(jnp.int32, done.shape, 1)
            past = jnp.where(jnp.logical_and(col_at < low, col_at > row_at), 0.0, done)
            rest = work[low:BLK, :]
            col_at = lax.broadcasted_iota(jnp.int32, rest.shape, 1)
            rest = jnp.where(jnp.logical_and(col_at >= tall * q, col_at < low), 0.0, rest)
            work[low:BLK, :] = rest - dot_f32(done[:, low:BLK], past, ((0,), (0,)))
    lower = (
        lax.broadcasted_iota(jnp.int32, (BLK, BLK), 0)
        >= lax.broadcasted_iota(jnp.int32, (BLK, BLK), 1)
    )
    inv[...] = jnp.where(lower, inv[...], 0.0)


def factor_kernel(head_a, head_b, own_ref, r_ref, m_ref, mat, head_ref, work, inv):
    c = lax.axis_index("cols")
    for spot in range(12):
        k, at_x, at_y = spot // 6, spot // 3 % 2, spot % 3
        head_ref[spot, 0:LEAD] = head_a[k, at_x, at_y]
        head_ref[spot, LEAD:BLK] = head_b[k, at_y, at_x]
    near = jnp.minimum(c, 3)
    for k in range(4):
        for j in range(k, 4):
            mat[k, :, j * BLK:(j + 1) * BLK] = head_ref[HEAD.index((k, j))]
        low, high = jnp.minimum(near, k), jnp.maximum(near, k)
        found = head_ref[low * 4 - low * (low - 1) // 2 + high - low]
        found = jnp.where(k <= near, found, found.T)
        mat[k, :, 512:640] = jnp.where(c >= 4, own_ref[k], found)
        mat[k, :, 640:768] = jnp.broadcast_to(head_ref[len(HEAD), k:k + 1, :], (BLK, BLK)).T
    for k in range(4):
        work[...] = mat[k, :, k * BLK:(k + 1) * BLK]
        factor_block(work, inv.at[k])
        low = (k + 1) * BLK
        inverse = inv[k]
        if k == 3:
            mat[k, :, low:768] = dot_f32(inverse, mat[k, :, low:768])
            r_ref[k * BLK:(k + 1) * BLK, :] = mat[k, :, 512:640]
            continue
        near_cols = dot_f32(inverse, mat[k, :, low:low + BLK])
        mat[k, :, low:low + BLK] = near_cols
        mat[k + 1, :, low:low + BLK] = mat[k + 1, :, low:low + BLK] - dot_f32(
            near_cols, near_cols, ((0,), (0,))
        )
        far = low + BLK
        mat[k, :, far:768] = dot_f32(inverse, mat[k, :, far:768])
        r_ref[k * BLK:(k + 1) * BLK, :] = mat[k, :, 512:640]
        mat[k + 1, :, far:768] = mat[k + 1, :, far:768] - dot_f32(
            near_cols, mat[k, :, far:768], ((0,), (0,))
        )
        for i in range(k + 2, 4):
            mat[i, :, i * BLK:768] = mat[i, :, i * BLK:768] - dot_f32(
                mat[k, :, i * BLK:(i + 1) * BLK], mat[k, :, i * BLK:768], ((0,), (0,))
            )
    rest = [mat[k, :, 640:768] for k in range(4)]
    for k in (3, 2, 1, 0):
        solved = dot_f32(inv[k], rest[k], ((0,), (0,)))
        for i in range(k):
            rest[i] = rest[i] - dot_f32(mat[i, :, k * BLK:(k + 1) * BLK], solved)
        m_ref[k:k + 1, :] = solved.T[0:1, :]


def factor_and_solve(head_a, head_b, own):
    f32 = jnp.float32
    vmem = pl.BlockSpec(memory_space=pltpu.VMEM)
    return pl.pallas_call(
        factor_kernel,
        out_shape=(
            jax.ShapeDtypeStruct((512, BLK), f32),
            jax.ShapeDtypeStruct((4, BLK), f32),
        ),
        in_specs=[vmem, vmem, vmem],
        out_specs=(vmem, vmem),
        scratch_shapes=[
            pltpu.VMEM((4, BLK, 768), f32),
            pltpu.VMEM((12, BLK, BLK), f32),
            pltpu.VMEM((BLK, BLK), f32),
            pltpu.VMEM((4, BLK, BLK), f32),
        ],
        compiler_params=pltpu.CompilerParams(vmem_limit_bytes=48 << 20),
        name="factor",
    )(head_a, head_b, own)


def shards(n_rows, sens_base, design_field, gradient, tile_index, type_codes):
    head_a, head_b, own = gram_everywhere(
        n_rows, sens_base, design_field, gradient,
        tile_index.reshape(1, BLK), type_codes.reshape(1, BLK),
    )
    r_panels, multipliers = factor_and_solve(head_a, head_b, own)
    return r_panels, multipliers.reshape(-1)


def solution(mesh):
    placed = (P("rows", "cols"), P("rows", None), P("rows", None), P("cols"), P("cols"))
    return jax.shard_map(
        functools.partial(shards, mesh.shape["rows"]),
        mesh=mesh, in_specs=placed, out_specs=(P(None, "cols"), P()), check_vma=False,
    )
```

```python
import functools

import jax
import jax.numpy as jnp
from jax import lax
from jax.experimental import pallas as pl
from jax.experimental.pallas import tpu as pltpu
from jax.sharding import PartitionSpec as P

TILE = 128
BLK = 128
NX = 4
NY = 4
MESH = pl.DeviceIdType.MESH
HEAD = [(a, b) for a in range(4) for b in range(a, 4)]
COUNT_X = (3, 3, 4, 4)
FIRST_X = (0, 3, 6, 10)
COUNT_Y = (4, 4, 4, 2)
FIRST_Y = (0, 4, 8, 12)
HALF = 14
ROWS = BLK // 2
LEAD = 48
PARTS = 2


def slot_of(core, x, y):
    if x < 2:
        spot = (core * 2 + x) * 3 + y
        if spot < len(HEAD):
            return HEAD[spot]
        return "proj" if spot == len(HEAD) else None
    return (y, x * 2 + core)


def gram_kernel(
    n_rows,
    base_ref, field_hbm, grad_hbm, tile_hbm, type_hbm,
    out_a, out_b, own_ref,
    raw, jac, field_ref, grad_ref, tile_ref, type_ref, codes_mine, codes, north, south,
    parts, from_core, half, from_x, from_y, sum_a, sum_b, from_x2, from_y2,
    block, from_zl, from_zh, line,
    load_sems, a2a_send, a2a_recv, code_send, code_recv, halo_send, halo_recv, core_sems,
    xa_send, xa_recv, yb_send, yb_recv, ya_send, ya_recv, xb_send, xb_recv,
    zl_send, zl_recv, zh_send, zh_recv, zg_send, zg_recv,
    gy_send, gy_recv, gx_send, gx_recv, hx_send, hx_recv, hy_send, hy_recv,
    cg_send, cg_recv,
):
    r = lax.axis_index("rows")
    c = lax.axis_index("cols")
    z, y = r // NY, r % NY
    zh, zl = z // 4, z % 4
    hops = n_rows // NY // 4
    x, core = c // 2, c % 2
    up, down = (r + n_rows - 1) % n_rows, (r + 1) % n_rows
    cells = raw.shape[1]

    def dev_c(col):
        return (r, col)

    def dev_x(xx):
        return (r, xx * 2 + core)

    def dev_y(yy):
        return (z * NY + yy, c)

    def dev_z(hi, lo):
        return ((hi * 4 + lo) * NY + y, c)

    def remote(src, dst, send, recv, device):
        return pltpu.make_async_remote_copy(
            src_ref=src, dst_ref=dst, send_sem=send, recv_sem=recv,
            device_id=device, device_id_type=MESH,
        )

    barrier = pltpu.get_barrier_semaphore()

    def greet(device):
        pl.semaphore_signal(barrier, inc=1, device_id=device, device_id_type=MESH)

    for d in range(1, hops):
        greet(dev_z((zh + d) % hops, zl))
    for d in range(1, 8):
        greet(dev_c((c + d) % 8))
    for d in range(1, NY):
        greet(dev_y((y + d) % NY))
    for d in range(1, 4):
        greet(dev_z(zh, (zl + d) % 4))
    greet((up, c))
    greet((down, c))
    loads = []
    for i, (src, dst) in enumerate((
        (field_hbm, field_ref), (tile_hbm, tile_ref), (type_hbm, type_ref), (grad_hbm, grad_ref),
    )):
        loads.append(pltpu.make_async_copy(src, dst, load_sems.at[i]))
        loads[-1].start()
    codes_mine[...] = jnp.zeros_like(codes_mine)
    loads[1].wait()
    loads[2].wait()
    codes_mine[0:1, :] = tile_ref[...]
    codes_mine[1:2, :] = type_ref[...]
    loads[0].wait()
    pl.semaphore_wait(barrier, 7 + (NY - 1) + 3 + (hops - 1) + 2)

    sent = []
    for d in range(1, 8):
        to = (c + d) % 8
        cp = remote(codes_mine, codes.at[c], code_send.at[d], code_recv.at[d], dev_c(to))
        cp.start()
        sent.append(cp)
    cp = remote(field_ref, north, halo_send.at[0], halo_recv.at[0], (down, c))
    cp.start()
    sent.append(cp)
    cp = remote(field_ref, south, halo_send.at[1], halo_recv.at[1], (up, c))
    cp.start()
    sent.append(cp)
    part = cells // PARTS

    def a2a_copy(h, d, spot, peer):
        return remote(
            base_ref.at[pl.ds(peer * cells + h * part, part), :],
            raw.at[spot, pl.ds(h * part, part)],
            a2a_send.at[h * 8 + d], a2a_recv.at[h * 8 + d], dev_c(peer),
        )

    for h in range(PARTS):
        for d in (4, 3, 5, 2, 6, 1, 7):
            cp = a2a_copy(h, d, c, (c + d) % 8)
            cp.start()
            sent.append(cp)
    mine = pltpu.make_async_copy(
        base_ref.at[pl.ds(c * cells, cells), :], raw.at[c], a2a_recv.at[0]
    )
    mine.start()
    codes[c] = codes_mine[...]

    remote(field_ref, north, halo_send.at[0], halo_recv.at[0], (up, c)).wait_recv()
    remote(field_ref, south, halo_send.at[1], halo_recv.at[1], (down, c)).wait_recv()
    here = field_ref[pl.ds(c, 1), :]
    above = field_ref[pl.ds((c + 7) % 8, 1), :]
    below = field_ref[pl.ds((c + 1) % 8, 1), :]
    above = jnp.where(c == 0, jnp.where(r == 0, 0.0, north[7:8, :]), above)
    below = jnp.where(c == 7, jnp.where(r == n_rows - 1, 0.0, south[0:1, :]), below)
    wide = (8, cells)
    here = jnp.broadcast_to(here, wide)
    above = jnp.broadcast_to(above, wide)
    below = jnp.broadcast_to(below, wide)
    lane = lax.broadcasted_iota(jnp.int32, wide, 1)
    west = jnp.where(lane == 0, 0.0, pltpu.roll(here, 1, 1))
    east = jnp.where(lane == cells - 1, 0.0, pltpu.roll(here, cells - 1, 1))
    laplace = 4.0 * here - (above + below + west + east)
    slope_x = 0.5 * (east - west)
    slope_y = 0.5 * (below - above)
    srow = lax.broadcasted_iota(jnp.int32, wide, 0)
    terms = []
    for fieldval in (laplace, slope_x, slope_y):
        rest = fieldval / TILE
        for _ in range(3):
            term = rest.astype(jnp.bfloat16).astype(jnp.float32)
            terms.append(term)
            rest = rest - term
    low = jnp.zeros(wide, jnp.float32)
    for k in range(8):
        low = jnp.where(srow == k, terms[(k % 3) * 3 + k // 3], low)
    high = jnp.where(srow == 0, terms[2 * 3 + 2], 0.0)
    both = jnp.concatenate([low, high], axis=0)
    tiles = cells // TILE
    spread = jnp.concatenate([both] * tiles, axis=0)
    krow = lax.broadcasted_iota(jnp.int32, spread.shape, 0)
    kcol = lax.broadcasted_iota(jnp.int32, spread.shape, 1)
    spread = jnp.where(krow // 16 == kcol // TILE, spread, 0.0)
    spread_t = spread.T.astype(jnp.bfloat16)

    first_tile = (r * 8 // TILE) * tiles
    rows16 = lax.broadcasted_iota(jnp.int32, (16 * tiles, BLK), 0)
    term_id = rows16 % 16
    kind_of = jnp.where(term_id < 9, term_id % 3, 3)
    tile_of = first_tile + rows16 // 16
    for d in range(1, 8):
        src = (c + 8 - d) % 8
        remote(codes_mine, codes.at[src], code_send.at[d], code_recv.at[d], dev_c(src)).wait_recv()

    where = {}
    for k in range(2):
        for xx in range(NX):
            for yy in range(COUNT_X[xx]):
                low = FIRST_Y[yy] + (xx if yy < 3 else xx - 2)
                where[slot_of(k, xx, yy)] = (k, FIRST_X[xx] + yy, HALF + low)

    def put(key, value, add=False):
        k, upper, lower = where[key]
        parts[k, upper] = value[0:ROWS] + (parts[k, upper] if add else 0.0)
        parts[k, lower] = value[ROWS:BLK] + (parts[k, lower] if add else 0.0)

    contract = (((0,), (0,)), ((), ()))
    for h in range(PARTS):
        for cs in range(8):
            if h == 0:
                @pl.when(c == cs)
                def _():
                    mine.wait()

            @pl.when(c != cs)
            def _():
                a2a_copy(h, (c + 8 - cs) % 8, cs, cs).wait_recv()

            chosen = jnp.logical_and(
                kind_of == codes[cs, 1:2, :], tile_of == codes[cs, 0:1, :]
            ).astype(jnp.float32).astype(jnp.bfloat16)
            span = slice(h * part, (h + 1) * part)
            added = jnp.dot(spread_t[span], chosen, preferred_element_type=jnp.float32)
            jac[span, cs * BLK:(cs + 1) * BLK] = (
                raw[cs, span].astype(jnp.float32) + added
            ).astype(jnp.bfloat16)

        for pa in range(2):
            left = jac[span, pa * 256:(pa + 1) * 256]
            for pb in range(pa, 4):
                prod = lax.dot_general(
                    left, jac[span, pb * 256:(pb + 1) * 256], contract,
                    preferred_element_type=jnp.float32,
                )
                for i in range(2):
                    for j in range(2):
                        key = (pa * 2 + i, pb * 2 + j)
                        if key in where:
                            put(key, prod[i * BLK:(i + 1) * BLK, j * BLK:(j + 1) * BLK], h > 0)
    loads[3].wait()
    proj = jnp.dot(grad_ref[...], jac[:, 0:512], preferred_element_type=jnp.float32)
    proj = jnp.sum(
        jnp.where(lax.broadcasted_iota(jnp.int32, proj.shape, 0) == c, proj, 0.0),
        axis=0, keepdims=True,
    )
    put("proj", jnp.zeros((BLK, BLK), jnp.float32))
    put(None, jnp.zeros((BLK, BLK), jnp.float32))
    k, upper, _ = where["proj"]
    for i in range(4):
        parts[k, upper, i:i + 1, :] = proj[:, i * BLK:(i + 1) * BLK]

    cp = remote(
        parts.at[1 - core], from_core, core_sems.at[0], core_sems.at[1], dev_c(x * 2 + 1 - core)
    )
    cp.start()
    sent.append(cp)
    cp.wait_recv()

    def xa_copy(xx, d, peer):
        span = COUNT_X[xx]
        return remote(
            half.at[pl.ds(FIRST_X[xx], span)], from_x.at[d, pl.ds(0, span)],
            xa_send.at[d], xa_recv.at[d], dev_x(peer),
        )

    def yb_copy(yy, d, peer):
        span = COUNT_Y[yy]
        return remote(
            half.at[pl.ds(HALF + FIRST_Y[yy], span)], from_y.at[d, pl.ds(0, span)],
            yb_send.at[d], yb_recv.at[d], dev_y(peer),
        )

    half[0:HALF] = parts[core, 0:HALF] + from_core[0:HALF]
    for q in range(4):
        @pl.when(x != q)
        def _():
            xa_copy(q, (q + NX - x) % NX, q).start()

    half[HALF:2 * HALF] = parts[core, HALF:2 * HALF] + from_core[HALF:2 * HALF]
    for q in range(4):
        @pl.when(y != q)
        def _():
            yb_copy(q, (q + NY - y) % NY, q).start()

    for q in range(4):
        @pl.when(x == q)
        def _():
            span = COUNT_X[q]
            total = half[FIRST_X[q]:FIRST_X[q] + span]
            for d in (1, 3, 2):
                xa_copy(q, d, (q + NX - d) % NX).wait_recv()
                total = total + from_x[d, 0:span]
            sum_a[0:span] = total

    skip = jnp.where(y == 3, 2, 0)
    holds = jnp.logical_or(x >= 2, y < 3)

    def ya_copy(d, yy, peer):
        return remote(sum_a.at[yy], from_y2.at[d], ya_send.at[d], ya_recv.at[d], dev_y(peer))

    def xb_copy(d, spot, peer):
        return remote(sum_b.at[spot], from_x2.at[d], xb_send.at[d], xb_recv.at[d], dev_x(peer))

    for d in range(1, 4):
        yy = (y + d) % NY

        @pl.when(jnp.logical_or(x >= 2, yy < 3))
        def _():
            ya_copy(d, yy, yy).start()

    for q in range(4):
        @pl.when(y == q)
        def _():
            span = COUNT_Y[q]
            total = half[HALF + FIRST_Y[q]:HALF + FIRST_Y[q] + span]
            for d in (1, 3, 2):
                yb_copy(q, d, (q + NY - d) % NY).wait_recv()
                total = total + from_y[d, 0:span]
            sum_b[0:span] = total

    for d in range(1, 4):
        xx = (x + d) % NX

        @pl.when(jnp.logical_or(xx >= 2, y < 3))
        def _():
            xb_copy(d, xx - skip, xx).start()

    def zl_copy(d, spot, peer):
        return remote(
            block.at[pl.ds(spot * 32, 32)], from_zl.at[d],
            zl_send.at[d], zl_recv.at[d], dev_z(zh, peer),
        )

    def zh_copy(d, spot, peer):
        return remote(
            from_zh.at[spot], from_zh.at[spot], zh_send.at[d], zh_recv.at[d], dev_z(peer, zl)
        )

    def zg_copy(d, spot, peer):
        return remote(
            line.at[pl.ds(spot * 32, 32)], line.at[pl.ds(spot * 32, 32)],
            zg_send.at[d], zg_recv.at[d], dev_z(zh, peer),
        )

    def gy_own(d, spot, peer):
        return remote(line, own_ref.at[spot], gy_send.at[d], gy_recv.at[d], dev_y(peer))

    def gy_head(d, spot, peer):
        return remote(
            line.at[pl.ds(0, LEAD)], out_a.at[core, x, spot],
            gy_send.at[d], gy_recv.at[d], dev_y(peer),
        )

    def gx_head(d, spot, peer):
        return remote(
            line.at[pl.ds(LEAD, BLK - LEAD)], out_b.at[core, y, spot],
            gx_send.at[d], gx_recv.at[d], dev_x(peer),
        )

    @pl.when(holds)
    def _():
        upper = sum_a[y]
        lower = sum_b[x - skip]
        for d in (1, 3, 2):
            ya_copy(d, 0, (y + NY - d) % NY).wait_recv()
            upper = upper + from_y2[d]
        for d in (1, 3, 2):
            xb_copy(d, 0, (x + NX - d) % NX).wait_recv()
            lower = lower + from_x2[d]
        block[0:ROWS] = upper
        block[ROWS:BLK] = lower
        for d in range(1, 4):
            lo = (zl + d) % 4
            zl_copy(d, lo, lo).start()
        total = block[pl.ds(pl.multiple_of(zl * 32, 32), 32)]
        for d in range(1, 4):
            zl_copy(d, 0, (zl + 4 - d) % 4).wait_recv()
            total = total + from_zl[d]
        from_zh[zh] = total
        for d in range(1, hops):
            zh_copy(d, zh, (zh + d) % hops).start()
        for d in range(1, hops):
            src = (zh + hops - d) % hops
            zh_copy(d, src, src).wait_recv()
        total = from_zh[0]
        for i in range(1, hops):
            total = total + from_zh[i]
        line[pl.ds(pl.multiple_of(zl * 32, 32), 32)] = total
        for d in range(1, 4):
            zg_copy(d, zl, (zl + d) % 4).start()
        for d in range(1, 4):
            src = (zl + 4 - d) % 4
            zg_copy(d, src, src).wait_recv()

        @pl.when(x >= 2)
        def _():
            for d in range(1, 4):
                gy_own(d, y, (y + d) % NY).start()
            own_ref[y] = line[...]

        @pl.when(x < 2)
        def _():
            for d in range(1, 4):
                gy_head(d, y, (y + d) % NY).start()
                gx_head(d, x, (x + d) % NX).start()
            out_a[core, x, y] = line[0:LEAD]
            out_b[core, y, x] = line[LEAD:BLK]

    def hx_copy(d, xx, peer):
        return remote(
            out_a.at[core, xx], out_a.at[core, xx], hx_send.at[d], hx_recv.at[d], dev_x(peer)
        )

    def hy_copy(d, yy, peer):
        return remote(
            out_b.at[core, yy], out_b.at[core, yy], hy_send.at[d], hy_recv.at[d], dev_y(peer)
        )

    @pl.when(x < 2)
    def _():
        for d in range(1, 4):
            src = (y + NY - d) % NY

            @pl.when(src < 3)
            def _():
                gy_head(d, src, src).wait_recv()

        for d in range(1, 4):
            hx_copy(d, x, (x + d) % NX).start()
        own_ref[...] = jnp.zeros_like(own_ref)

    @pl.when(y < 3)
    def _():
        for d in range(1, 4):
            src = (x + NX - d) % NX

            @pl.when(src < 2)
            def _():
                gx_head(d, src, src).wait_recv()

        for d in range(1, 4):
            hy_copy(d, y, (y + d) % NY).start()

    def swap_a(half_core):
        return remote(
            out_a.at[half_core], out_a.at[half_core], cg_send.at[0], cg_recv.at[0],
            dev_c(x * 2 + 1 - core),
        )

    def swap_b(half_core):
        return remote(
            out_b.at[half_core], out_b.at[half_core], cg_send.at[1], cg_recv.at[1],
            dev_c(x * 2 + 1 - core),
        )

    for d in range(1, 4):
        src = (y + NY - d) % NY

        @pl.when(src < 3)
        def _():
            hy_copy(d, src, src).wait_recv()

    swap_b(core).start()
    for d in range(1, 4):
        src = (x + NX - d) % NX

        @pl.when(src < 2)
        def _():
            hx_copy(d, src, src).wait_recv()

    swap_a(core).start()

    @pl.when(x >= 2)
    def _():
        for d in range(1, 4):
            src = (y + NY - d) % NY
            gy_own(d, src, src).wait_recv()

    swap_b(1 - core).wait_recv()
    swap_a(1 - core).wait_recv()

    for cp in sent:
        cp.wait_send()
    for q in range(4):
        @pl.when(x != q)
        def _():
            xa_copy(q, (q + NX - x) % NX, q).wait_send()

        @pl.when(y != q)
        def _():
            yb_copy(q, (q + NY - y) % NY, q).wait_send()

    for d in range(1, 4):
        yy = (y + d) % NY
        xx = (x + d) % NX

        @pl.when(jnp.logical_or(x >= 2, yy < 3))
        def _():
            ya_copy(d, yy, yy).wait_send()

        @pl.when(jnp.logical_or(xx >= 2, y < 3))
        def _():
            xb_copy(d, xx - skip, xx).wait_send()

    @pl.when(holds)
    def _():
        for d in range(1, 4):
            lo = (zl + d) % 4
            zl_copy(d, lo, lo).wait_send()
            zg_copy(d, zl, lo).wait_send()
        for d in range(1, hops):
            zh_copy(d, zh, (zh + d) % hops).wait_send()

        @pl.when(x >= 2)
        def _():
            for d in range(1, 4):
                gy_own(d, y, (y + d) % NY).wait_send()

        @pl.when(x < 2)
        def _():
            for d in range(1, 4):
                gy_head(d, y, (y + d) % NY).wait_send()
                gx_head(d, x, (x + d) % NX).wait_send()

    @pl.when(x < 2)
    def _():
        for d in range(1, 4):
            hx_copy(d, x, (x + d) % NX).wait_send()

    @pl.when(y < 3)
    def _():
        for d in range(1, 4):
            hy_copy(d, y, (y + d) % NY).wait_send()

    swap_b(core).wait_send()
    swap_a(core).wait_send()


def gram_everywhere(n_rows, base, field, grad, tile, kind):
    cells = field.shape[1]
    hops = n_rows // NY // 4
    f32 = jnp.float32
    vmem = pl.BlockSpec(memory_space=pltpu.VMEM)
    hbm = pl.BlockSpec(memory_space=pltpu.HBM)
    pairs = [pltpu.SemaphoreType.DMA((4,))] * 2
    halves = lambda *lead: pltpu.VMEM(lead + (ROWS, BLK), f32)
    strip = lambda dtype: pltpu.VMEM((8, cells), dtype)
    return pl.pallas_call(
        functools.partial(gram_kernel, n_rows),
        out_shape=(
            jax.ShapeDtypeStruct((2, 2, 3, LEAD, BLK), f32),
            jax.ShapeDtypeStruct((2, 3, 2, BLK - LEAD, BLK), f32),
            jax.ShapeDtypeStruct((4, BLK, BLK), f32),
        ),
        in_specs=[hbm] * 5,
        out_specs=(vmem, vmem, vmem),
        scratch_shapes=[
            pltpu.VMEM((8, cells, BLK), jnp.bfloat16),
            pltpu.VMEM((cells, 8 * BLK), jnp.bfloat16),
            strip(f32), strip(jnp.bfloat16),
            pltpu.VMEM((1, BLK), jnp.int32), pltpu.VMEM((1, BLK), jnp.int32),
            pltpu.VMEM((8, BLK), jnp.int32), pltpu.VMEM((8, 8, BLK), jnp.int32),
            strip(f32), strip(f32),
            halves(2, 2 * HALF), halves(2 * HALF), halves(2 * HALF),
            halves(4, 4), halves(4, 4), halves(4), halves(4), halves(4), halves(4),
            pltpu.VMEM((BLK, BLK), f32), pltpu.VMEM((4, 32, BLK), f32),
            pltpu.VMEM((hops, 32, BLK), f32), pltpu.VMEM((BLK, BLK), f32),
            pltpu.SemaphoreType.DMA((4,)),
            *[pltpu.SemaphoreType.DMA((8 * PARTS,))] * 2, *[pltpu.SemaphoreType.DMA((8,))] * 2,
            pltpu.SemaphoreType.DMA((2,)), pltpu.SemaphoreType.DMA((2,)),
            pltpu.SemaphoreType.DMA((2,)),
            *pairs * 4, *pairs, *pairs, *pairs, *pairs * 4,
            pltpu.SemaphoreType.DMA((2,)), pltpu.SemaphoreType.DMA((2,)),
        ],
        compiler_params=pltpu.CompilerParams(
            collective_id=0, has_side_effects=True, vmem_limit_bytes=48 << 20
        ),
        name="gram",
    )(*[pltpu.with_memory_space_constraint(v, pltpu.HBM) for v in (base, field, grad, tile, kind)])


def across(vec, col):
    return jnp.broadcast_to(vec[:, col:col + 1], (8, BLK))


def along(vec, row):
    return jnp.broadcast_to(vec[row:row + 1, :], (8, BLK))


def split_3(x):
    high = x.astype(jnp.bfloat16)
    rest = x - high.astype(jnp.float32)
    mid = rest.astype(jnp.bfloat16)
    return high, mid, (rest - mid.astype(jnp.float32)).astype(jnp.bfloat16)


def dot_f32(left, right, dims=((1,), (0,))):
    lh, lm, ll = split_3(left)
    rh, rm, rl = split_3(right)
    return lax.dot_general(
        jnp.concatenate([lh, lh, lm, lm, lh, ll], axis=dims[0][0]),
        jnp.concatenate([rh, rm, rh, rm, rl, rh], axis=dims[1][0]),
        (dims, ((), ())), preferred_element_type=jnp.float32,
    )


def factor_block(work, inv):
    rows = lax.broadcasted_iota(jnp.int32, (8, BLK), 0)
    lane = lax.broadcasted_iota(jnp.int32, (8, BLK), 1)
    tall = 64
    for q in range(BLK // tall):
        at = [tall * q + 8 * s for s in range(tall // 8)]
        xs = [work[a:a + 8, :] for a in at]
        ahead = None
        for s in range(len(at)):
            start = at[s]
            cols = ahead or [across(xs[s], start + t) for t in range(8)]
            later = range(s + 1, len(at))
            below = {n: [across(xs[n], start + t) for t in range(8)] for n in later}
            ahead = [across(xs[s + 1], at[s + 1] + t) for t in range(8)] if later else None
            here = jnp.logical_and(lane >= start, lane < start + 8)
            xs[s] = jnp.where(here, jnp.where(lane - start == rows, 1.0, 0.0), xs[s])
            for n in later:
                xs[n] = jnp.where(here, 0.0, xs[n])
            pivot = along(cols[0], 0)
            pivots = pivot
            for t in range(8):
                entry = {u: along(cols[t], u) for u in range(t + 1, 8)}
                recip = 1.0 / pivot
                row = along(xs[s], t)
                if t < 7:
                    pivot = along(cols[t + 1], t + 1) - (entry[t + 1] * recip) * entry[t + 1]
                    pivots = jnp.where(rows >= t + 1, pivot, pivots)
                    mult = cols[t] * recip
                    for u in range(t + 1, 8):
                        cols[u] = cols[u] - mult * entry[u]
                    xs[s] = xs[s] - jnp.where(rows > t, mult, 0.0) * row
                for n in later:
                    mult = below[n][t] * recip
                    if n == s + 1:
                        for u in range(8):
                            ahead[u] = ahead[u] - mult * along(below[n][t], u)
                    for u in range(t + 1, 8):
                        below[n][u] = below[n][u] - mult * entry[u]
                    xs[n] = xs[n] - mult * row
            inv[start:start + 8, :] = xs[s] * (1.0 / jnp.sqrt(pivots))
        low = tall * (q + 1)
        if low < BLK:
            done = inv[tall * q:low, :]
            row_at = lax.broadcasted_iota(jnp.int32, done.shape, 0) + tall * q
            col_at = lax.broadcasted_iota(jnp.int32, done.shape, 1)
            past = jnp.where(jnp.logical_and(col_at < low, col_at > row_at), 0.0, done)
            rest = work[low:BLK, :]
            col_at = lax.broadcasted_iota(jnp.int32, rest.shape, 1)
            rest = jnp.where(jnp.logical_and(col_at >= tall * q, col_at < low), 0.0, rest)
            work[low:BLK, :] = rest - dot_f32(done[:, low:BLK], past, ((0,), (0,)))
    lower = (
        lax.broadcasted_iota(jnp.int32, (BLK, BLK), 0)
        >= lax.broadcasted_iota(jnp.int32, (BLK, BLK), 1)
    )
    inv[...] = jnp.where(lower, inv[...], 0.0)


def factor_kernel(head_a, head_b, own_ref, r_ref, m_ref, mat, back, head_ref, work, inv):
    c = lax.axis_index("cols")
    for spot in range(12):
        k, at_x, at_y = spot // 6, spot // 3 % 2, spot % 3
        head_ref[spot, 0:LEAD] = head_a[k, at_x, at_y]
        head_ref[spot, LEAD:BLK] = head_b[k, at_y, at_x]
    near = jnp.minimum(c, 3)
    for k in range(4):
        for j in range(k, 4):
            mat[k, :, j * BLK:(j + 1) * BLK] = head_ref[HEAD.index((k, j))]
        low, high = jnp.minimum(near, k), jnp.maximum(near, k)
        found = head_ref[low * 4 - low * (low - 1) // 2 + high - low]
        found = jnp.where(k <= near, found, found.T)
        mat[k, :, 512:640] = jnp.where(c >= 4, own_ref[k], found)
        mat[k, :, 640:768] = jnp.broadcast_to(head_ref[len(HEAD), k:k + 1, :], (BLK, BLK)).T
    for k in range(4):
        work[...] = mat[k, :, k * BLK:(k + 1) * BLK]
        factor_block(work, inv.at[k])
        low = (k + 1) * BLK
        inverse = inv[k]
        if k == 3:
            mat[k, :, low:768] = dot_f32(inverse, mat[k, :, low:768])
            r_ref[k * BLK:(k + 1) * BLK, :] = mat[k, :, 512:640]
            continue
        near_cols = dot_f32(inverse, mat[k, :, low:low + BLK])
        mat[k, :, low:low + BLK] = near_cols
        mat[k + 1, :, low:low + BLK] = mat[k + 1, :, low:low + BLK] - dot_f32(
            near_cols, near_cols, ((0,), (0,))
        )
        far = low + BLK
        mat[k, :, far:768] = dot_f32(inverse, mat[k, :, far:768])
        r_ref[k * BLK:(k + 1) * BLK, :] = mat[k, :, 512:640]
        mat[k + 1, :, far:768] = mat[k + 1, :, far:768] - dot_f32(
            near_cols, mat[k, :, far:768], ((0,), (0,))
        )
        for i in range(k + 2, 4):
            mat[i, :, i * BLK:768] = mat[i, :, i * BLK:768] - dot_f32(
                mat[k, :, i * BLK:(i + 1) * BLK], mat[k, :, i * BLK:768], ((0,), (0,))
            )
        back[k, :, low:512] = dot_f32(inverse, mat[k, :, low:512], ((0,), (0,)))
        back[k, :, 640:768] = dot_f32(inverse, mat[k, :, 640:768], ((0,), (0,)))
    rest = [back[k, :, 640:768] for k in range(3)]
    rest.append(dot_f32(inv[3], mat[3, :, 640:768], ((0,), (0,))))
    for k in (3, 2, 1, 0):
        for i in range(k):
            rest[i] = rest[i] - dot_f32(back[i, :, k * BLK:(k + 1) * BLK], rest[k])
        m_ref[k:k + 1, :] = rest[k].T[0:1, :]


def factor_and_solve(head_a, head_b, own):
    f32 = jnp.float32
    vmem = pl.BlockSpec(memory_space=pltpu.VMEM)
    return pl.pallas_call(
        factor_kernel,
        out_shape=(
            jax.ShapeDtypeStruct((512, BLK), f32),
            jax.ShapeDtypeStruct((4, BLK), f32),
        ),
        in_specs=[vmem, vmem, vmem],
        out_specs=(vmem, vmem),
        scratch_shapes=[
            pltpu.VMEM((4, BLK, 768), f32),
            pltpu.VMEM((3, BLK, 768), f32),
            pltpu.VMEM((12, BLK, BLK), f32),
            pltpu.VMEM((BLK, BLK), f32),
            pltpu.VMEM((4, BLK, BLK), f32),
        ],
        compiler_params=pltpu.CompilerParams(vmem_limit_bytes=48 << 20),
        name="factor",
    )(head_a, head_b, own)


def shards(n_rows, sens_base, design_field, gradient, tile_index, type_codes):
    head_a, head_b, own = gram_everywhere(
        n_rows, sens_base, design_field, gradient,
        tile_index.reshape(1, BLK), type_codes.reshape(1, BLK),
    )
    r_panels, multipliers = factor_and_solve(head_a, head_b, own)
    return r_panels, multipliers.reshape(-1)


def solution(mesh):
    placed = (P("rows", "cols"), P("rows", None), P("rows", None), P("cols"), P("cols"))
    return jax.shard_map(
        functools.partial(shards, mesh.shape["rows"]),
        mesh=mesh, in_specs=placed, out_specs=(P(None, "cols"), P()), check_vma=False,
    )
```
